32 devices in a mesh: dp: 8 (over y, x, core), tensor: 4 (over z).
Axes of the slice: x: 2, y: 2, z: 4, core: 2. Of those that a mesh axis runs over, the one named last changes fastest.
Arguments:
- inputs: bfloat16 [32, 1024, 1024], P(None, 'dp', 'tensor'), may hold values from -6 to 6
- cotangent: bfloat16 [32, 1024, 1024], P(None, 'dp', 'tensor'), may hold values from -6 to 6
- lengths: int32 [32], replicated, may hold values from 513 to 1024, as said below
- dealing: int32 [32], replicated, may hold values from 0 to 31, each once
- buckets: int32 [2047], replicated, may hold values from 1 to 511, as said below
- rel_embed: bfloat16 [512, 1024], P('dp'), may hold values from -6 to 6
- query_weight: bfloat16 [1024, 1024], P('dp', 'tensor'), may hold values from -0.25 to 0.25
- key_weight: bfloat16 [1024, 1024], P('dp', 'tensor'), may hold values from -0.25 to 0.25
- value_weight: bfloat16 [1024, 1024], P('dp', 'tensor'), may hold values from -0.1875 to 0.1875
- proj_shifts: bfloat16 [3, 1024], P(None, 'tensor'), may hold values from -3 to 3
- merge_weight: bfloat16 [1024, 1024], P('dp', 'tensor'), may hold values from -1.5 to 1.5
- inner_weight: bfloat16 [1024, 4096], P('dp', 'tensor'), may hold values from -0.1875 to 0.1875
- hidden_shift: bfloat16 [4096], P('tensor'), may hold values from -3 to 3
- outer_weight: bfloat16 [1024, 4096], P('dp', 'tensor'), may hold values from -0.09375 to 0.09375
- layer_vectors: bfloat16 [6, 1024], replicated, may hold values from -2 to 2, as said below
Outputs:
- output: bfloat16 [32, 1024, 1024], P(None, 'dp', 'tensor')
- input_grad: bfloat16 [32, 1024, 1024], P(None, 'dp', 'tensor')
- rel_grad: float32 [512, 1024], replicated
- query_grad: float32 [1024, 1024], P('dp', 'tensor')
- key_grad: float32 [1024, 1024], P('dp', 'tensor')
- value_grad: float32 [1024, 1024], P('dp', 'tensor')
- shifts_grad: float32 [3, 1024], replicated
- merge_grad: float32 [1024, 1024], P('dp', 'tensor')
- inner_grad: float32 [1024, 4096], P('dp', 'tensor')
- hidden_grad: float32 [4096], replicated
- outer_grad: float32 [1024, 4096], P('dp', 'tensor')
- vectors_grad: float32 [6, 1024], replicated
The draws below stay inside these ranges and needn't reach their ends.
Inputs may be any that keep to these rules, and one draw needn't show every extreme that they name: lengths[k] is the length of the sequence in slot k; in each aligned block of 4 slots one has length 1024. Slot k holds the given sequence dealing[k]; each sequence once. buckets[r + 1023] is the bucket of distance r; it equals 256 at r = 0, never falls as r rises, rises by one per step while |r| <= 128, beyond that by one at each even |r| and by zero or one at each odd |r| until it is capped, and the buckets of r and -r sum to 512. `layer_vectors`: rows 1 and 4 (from 0) are gains near one, the others biases.
All inputs are finite; a program needn't handle non-finite values.
Results may differ from the reference program's by a relative error of at most 0.02.
Values may be sent and summed in bfloat16 or wider, within the bound.
A program may use at most 512 MiB of HBM per device.

```python
import math
import jax
import jax.numpy as jnp
from jax import lax

D = 1024
HEADS = 16
HEAD = 64
FF = 4096
SPAN = 256
LEN = 1024
SEQS = 32


def draw_lengths(key, part):
    short = jax.random.randint(jax.random.fold_in(key, 11), (SEQS,), 0, LEN // 2)
    full_at = jax.random.randint(jax.random.fold_in(key, 12), (), 0, 4)
    slots = jnp.arange(SEQS, dtype=jnp.int32)
    return jnp.where(slots % 4 == full_at, LEN, LEN - short).astype(jnp.int32)


def draw_buckets(key, part):
    reach = jnp.arange(1, LEN, dtype=jnp.int32)
    coin = jax.random.randint(jax.random.fold_in(key, 21), (LEN - 1,), 0, 2)
    stepping = jnp.where((reach <= SPAN // 2) | (reach % 2 == 0), 1, coin).astype(jnp.int32)
    distant = jnp.minimum(jnp.cumsum(stepping), SPAN - 1).astype(jnp.int32)
    below = (SPAN - distant[::-1]).astype(jnp.int32)
    above = (SPAN + distant).astype(jnp.int32)
    middle = jnp.full((1,), SPAN, jnp.int32)
    return jnp.concatenate([below, middle, above]).astype(jnp.int32)


def draw_layer_vectors(key, part):
    noise = jax.random.normal(jax.random.fold_in(key, 31), (6, D), jnp.float32)
    noise = jnp.clip(noise, -3.5, 3.5)
    rows = jnp.arange(6)[:, None]
    gain_rows = (rows == 1) | (rows == 4)
    return jnp.where(gain_rows, 1.0 + 0.1 * noise, 0.5 * noise).astype(jnp.bfloat16)


def levels(key, extent, cuts, least, largest):
    factor_of = 1.0
    for dim, parts in cuts:
        heights = jax.random.uniform(jax.random.fold_in(jax.random.fold_in(key, 6), dim), (parts,), jnp.float32, least / len(cuts), largest / len(cuts))
        factor_of = factor_of * jnp.repeat(jnp.exp(heights), extent[dim] // parts).reshape((-1,) + (1,) * (len(extent) - 1 - dim))
    return factor_of


def normal_values(rng, extent, scale, most, cuts=(), held_as=jnp.bfloat16):
    level = levels(rng, extent, cuts, -0.22, 0.18) if cuts else 1.0
    values = jax.random.normal(rng, extent, jnp.float32) * scale * level
    return jnp.minimum(jnp.maximum(values, -most), most).astype(held_as)


def setup_inputs(seed: int = 0) -> dict:
    streams_of = jax.random.split(jax.random.key(seed), 16)
    inputs = normal_values(streams_of[0], (SEQS, LEN, D), 1.0, 6.0, ((1, 8), (2, 4)))
    cotangent = normal_values(streams_of[1], (SEQS, LEN, D), 1.0, 6.0, ((1, 8), (2, 4)))
    lengths = draw_lengths(jax.random.fold_in(streams_of[15], 71), 0)
    dealing = jax.random.permutation(streams_of[3], SEQS).astype(jnp.int32)
    buckets = draw_buckets(jax.random.fold_in(streams_of[15], 71), 0)
    rel_embed = normal_values(streams_of[5], (2 * SPAN, D), 1.0, 6.0, ((0, 8),))
    query_weight = normal_values(streams_of[6], (D, D), (D // 2) ** -0.5, 0.25, ((0, 8), (1, 4)))
    key_weight = normal_values(streams_of[7], (D, D), (D // 2) ** -0.5, 0.25, ((0, 8), (1, 4)))
    value_weight = normal_values(streams_of[8], (D, D), D ** -0.5, 0.1875, ((0, 8), (1, 4)))
    proj_shifts = normal_values(streams_of[9], (3, D), 0.5, 3.0, ((1, 4),))
    merge_weight = normal_values(streams_of[10], (D, D), (D // 64) ** -0.5, 1.5, ((0, 8), (1, 4)))
    inner_weight = normal_values(streams_of[11], (D, FF), D ** -0.5, 0.1875, ((0, 8), (1, 4)))
    hidden_shift = normal_values(streams_of[12], (FF,), 0.5, 3.0, ((0, 4),))
    outer_weight = normal_values(streams_of[13], (D, FF), FF ** -0.5, 0.09375, ((0, 8), (1, 4)))
    layer_vectors = draw_layer_vectors(jax.random.fold_in(streams_of[15], 71), 0)
    return {"inputs": inputs, "cotangent": cotangent, "lengths": lengths, "dealing": dealing, "buckets": buckets, "rel_embed": rel_embed, "query_weight": query_weight, "key_weight": key_weight, "value_weight": value_weight, "proj_shifts": proj_shifts, "merge_weight": merge_weight, "inner_weight": inner_weight, "hidden_shift": hidden_shift, "outer_weight": outer_weight, "layer_vectors": layer_vectors}


EPSILON = 1e-07
NEGATIVE = -1e+30

@jax.custom_vjp
def low(v):
    return lax.optimization_barrier(v.astype(jnp.bfloat16)).astype(jnp.float32)

@jax.custom_vjp
def low_back(v):
    return v

def low_keep(v):
    return (low(v), None)

def low_pass(kept, grad):
    return (grad,)

def back_keep(v):
    return (v, None)

def back_low(kept, grad):
    return (low(grad),)
low.defvjp(low_keep, low_pass)
low_back.defvjp(back_keep, back_low)

def product(left, right):
    return jnp.matmul(left, right, precision=lax.Precision.HIGHEST)

def layer_norm(values, gain, shift):
    center = values - lax.optimization_barrier(jnp.mean(values, axis=-1, keepdims=True))
    spread = lax.optimization_barrier(jnp.mean(center * center, axis=-1, keepdims=True))
    return center * lax.rsqrt(spread + EPSILON) * gain + shift

def skew_rows(table):
    count = table.shape[0]
    width = table.shape[1]
    padded = jnp.pad(table, ((0, 0), (0, 1)))
    flat = padded.reshape(count * (width + 1))
    cut = lax.slice_in_dim(flat, count - 1, count - 1 + count * width, axis=0)
    return cut.reshape(count, width)[:, :count]

def forward(block, lengths_here, reversed_buckets, params):
    query_weight, key_weight, value_weight, shifts, merge_weight, inner_weight, hidden_shift, outer_weight, rel, vectors = params
    count = block.shape[0]
    scale = 1.0 / math.sqrt(3.0 * HEAD)
    query_matrix = low(low_back(product(block, query_weight)) + shifts[0])
    keys = low(low_back(product(block, key_weight)) + shifts[1])
    values = low(low_back(product(block, value_weight)) + shifts[2])
    query_pos = low(product(rel, query_weight) + shifts[0])
    key_position_rows = low(product(rel, key_weight) + shifts[1])
    query_far = query_pos[reversed_buckets]
    key_far = key_position_rows[reversed_buckets]

    def heads_first(tensor):
        return tensor.reshape(count, LEN, HEADS, HEAD).transpose(0, 2, 1, 3).reshape(count * HEADS, LEN, HEAD)

    def pos_heads(tensor):
        split_pos = tensor.reshape(2 * LEN - 1, HEADS, HEAD).transpose(1, 0, 2)
        return jnp.broadcast_to(split_pos[None], (count, HEADS, 2 * LEN - 1, HEAD)).reshape(count * HEADS, 2 * LEN - 1, HEAD)
    item_lengths = jnp.repeat(lengths_here, HEADS)

    def attend(item):
        head_q, head_k, head_v, head_qpos, head_kpos, length = item
        content = low_back(product(head_q, head_k.T))
        into_position = low_back(product(head_q, head_kpos.T))
        from_pos = low_back(product(head_k, head_qpos.T))
        score = (content + skew_rows(into_position) + skew_rows(from_pos).T) * scale
        column = jnp.arange(LEN, dtype=jnp.int32)
        score = jnp.where((column < length)[None, :], score, NEGATIVE)
        probs = jax.nn.softmax(score, axis=-1)
        return low(low_back(product(low(probs), head_v)))
    context = lax.map(jax.checkpoint(attend), (heads_first(query_matrix), heads_first(keys), heads_first(values), pos_heads(query_far), pos_heads(key_far), item_lengths))
    context = context.reshape(count, HEADS, LEN, HEAD).transpose(0, 2, 1, 3).reshape(count, LEN, D)
    attn = low_back(product(context, merge_weight.T)) + vectors[0]
    first_out = layer_norm(attn + block, vectors[1], vectors[2])
    pre_act = low_back(product(low(first_out), inner_weight)) + hidden_shift
    act = low(jax.nn.gelu(pre_act, approximate=False))
    ffn = low_back(product(act, outer_weight.T)) + vectors[3]
    return layer_norm(ffn + first_out, vectors[4], vectors[5])

def reference(inputs, cotangent, lengths, dealing, buckets, rel_embed, query_weight, key_weight, value_weight, proj_shifts, merge_weight, inner_weight, hidden_shift, outer_weight, layer_vectors):
    count = inputs.shape[0]
    slots = jnp.arange(count, dtype=jnp.int32)
    inverse = jnp.zeros((count,), jnp.int32).at[dealing].set(slots)
    given_lengths = lengths[inverse]
    reversed_buckets = buckets[::-1].astype(jnp.int32)
    params = tuple((p.astype(jnp.float32) for p in (query_weight, key_weight, value_weight, proj_shifts, merge_weight, inner_weight, hidden_shift, outer_weight, rel_embed, layer_vectors)))
    batch = math.gcd(count, max(1, 4096 // LEN))
    rounds = count // batch
    feed = (inputs.reshape(rounds, batch, LEN, D), cotangent.reshape(rounds, batch, LEN, D), given_lengths.reshape(rounds, batch))

    def step(totals, item):
        block, cot_block, len_block = item

        def run(block_value, params_value):
            return forward(block_value, len_block, reversed_buckets, params_value)
        result, pullback = jax.vjp(run, block.astype(jnp.float32), params)
        dblock, dparams = pullback(cot_block.astype(jnp.float32))
        totals = jax.tree.map(lambda left, right: left + right, totals, dparams)
        return (totals, (result.astype(jnp.bfloat16), dblock.astype(jnp.bfloat16)))
    zeros = jax.tree.map(jnp.zeros_like, params)
    totals, (outs, grads) = lax.scan(step, zeros, feed)
    return (outs.reshape(count, LEN, D), grads.reshape(count, LEN, D), totals[8], totals[0], totals[1], totals[2], totals[3], totals[4], totals[5], totals[6], totals[7], totals[9])
```

```python
import functools
import math

import jax
import jax.numpy as jnp
from jax import lax
from jax.experimental import pallas as pl
from jax.experimental.pallas import tpu as pltpu
from jax.sharding import PartitionSpec as P

EPSILON = 1e-07
HEAD = 64
B = 128
SR = 16
UN = 8
NT = (((1,), (1,)), ((), ()))


def dotnt(a, b):
    return lax.dot_general(a, b, NT, preferred_element_type=jnp.float32)


def dotnn(a, b):
    return lax.dot_general(a, b, (((1,), (0,)), ((), ())), preferred_element_type=jnp.float32)


def skew(g_ref, a, n, L):
    parts=[]
    nb=L//B
    for a8 in range(a,a+n,8):
        rot=[pltpu.roll(g_ref[a8:a8+8,t*128:t*128+128], 1+a8, 1, stride=1, stride_axis=0) for t in range(nb+1)]
        msk=lax.broadcasted_iota(jnp.int32,(8,128),1) < (1+a8+lax.broadcasted_iota(jnp.int32,(8,128),0))
        parts.append(jnp.concatenate([jnp.where(msk,rot[t],rot[t+1]) for t in range(nb)],axis=1))
    return jnp.concatenate(parts,axis=0)

def fwd_kernel(len_ref, q_ref, k_ref, v_ref, kf_ref, qf_ref, ctx_ref, p_ref, l_ref, t_ref, kx_ref, vx_ref, g0, g1, s0, s1, *, L, scale):
    W = L + B
    nb = L // B
    gs=(g0,g1); ss=(s0,s1)
    lane = lax.broadcasted_iota(jnp.int32, (1, 128), 1)
    length = len_ref[0]
    row = lax.broadcasted_iota(jnp.int32, (L, 128), 0)
    c2 = scale * math.log2(math.e)
    eye = (lax.broadcasted_iota(jnp.int32,(B,B),0)==lax.broadcasted_iota(jnp.int32,(B,B),1)).astype(jnp.bfloat16)
    zero = jnp.zeros((), jnp.bfloat16)
    mine = [lane < 64, lane >= 64]
    first_other = [lane==64, lane==0]
    for h in range(2):
        bias = jnp.where((row >= length) & first_other[h], -1e30, 0.0).astype(jnp.bfloat16)
        kx_ref[h] = jnp.where(mine[h], k_ref[...], bias)
        vx_ref[h] = jnp.where(mine[h], v_ref[...], jnp.ones((), jnp.bfloat16))
    def tblock(b, _):
        r0 = pl.multiple_of(b*B, B)
        base = pl.multiple_of(L - B - b*B, B)
        for h in range(2):
            kb = jnp.where(mine[h], k_ref[pl.ds(r0,B),:], zero)
            gs[h][...] = dotnt(kb, qf_ref[pl.ds(base, W), :])
        for h in range(2):
            for a in range(0, B, SR):
                t_ref[h, pl.ds(r0+a,SR), :] = skew(gs[h], a, SR, L).astype(jnp.bfloat16)
        return 0
    lax.fori_loop(0, nb, tblock, 0, unroll=2)
    def scores(b, h):
        r0 = pl.multiple_of(b*B, B)
        base = pl.multiple_of(L - B - b*B, B)
        qb = q_ref[pl.ds(r0,B),:]
        qm = jnp.where(mine[h], qb, zero)
        qx = jnp.where(mine[h], qb, first_other[h].astype(jnp.bfloat16))
        gs[h][...] = dotnt(qm, kf_ref[pl.ds(base, W), :])
        lhs = jnp.concatenate([qx, eye], axis=1)
        rhs = jnp.concatenate([kx_ref[h], t_ref[h, :, pl.ds(r0,B)]], axis=1)
        ss[h][...] = dotnt(lhs, rhs)
    def soft(b, h):
        r0 = pl.multiple_of(b*B, B)
        tops=[]
        for a in range(0, B, 8):
            s = ss[h][a:a+8] + skew(gs[h], a, 8, L)
            ss[h][a:a+8] = s
            tops.append(functools.reduce(jnp.maximum,[s[:,t*128:t*128+128] for t in range(nb)]))
        m = jnp.max(jnp.concatenate(tops,axis=0), axis=1, keepdims=True) * c2
        for a in range(0, B, SR):
            p_ref[h, pl.ds(r0+a,SR), :] = jnp.exp2(ss[h][a:a+SR]*c2 - m[a:a+SR]).astype(jnp.bfloat16)
    def out(b, h):
        r0 = pl.multiple_of(b*B, B)
        return dotnn(p_ref[h, pl.ds(r0,B), :], vx_ref[h])
    def finish(b, o0, o1):
        r0 = pl.multiple_of(b*B, B)
        num = jnp.where(mine[0], o0, o1)
        den = jnp.where(mine[0], pltpu.roll(o0,64,1), pltpu.roll(o1,64,1))
        inv = 1.0/den
        ctx_ref[pl.ds(r0,B),:] = (num*inv).astype(jnp.bfloat16)
        l_ref[pl.ds(r0,B),:] = inv
    scores(0,0)
    def sblock(b, o0):
        scores(b,1)
        soft(b,0)
        o0 = out(b,0)
        scores(jnp.minimum(b+1,nb-1),0)
        soft(b,1)
        o1 = out(b,1)
        finish(b,o0,o1)
        return 0
    lax.fori_loop(0, nb, sblock, 0, unroll=8)

def attn_fwd(length, q, k, v, kf, qf, *, scale):
    L, C = q.shape
    col = lambda r: pl.BlockSpec((r,128), lambda h, *_: (0,h))
    return pl.pallas_call(
        functools.partial(fwd_kernel, L=L, scale=scale),
        grid_spec=pltpu.PrefetchScalarGridSpec(num_scalar_prefetch=1, grid=(C//128,),
            in_specs=[col(L),col(L),col(L),col(2*L),col(2*L)],
            out_specs=[col(L), pl.BlockSpec((2,L,L), lambda h,*_: (h,0,0)), col(L)],
            scratch_shapes=[pltpu.VMEM((2,L,L),jnp.bfloat16), pltpu.VMEM((2,L,128),jnp.bfloat16), pltpu.VMEM((2,L,128),jnp.bfloat16)]
              +[pltpu.VMEM((B,L+B),jnp.float32)]*2+[pltpu.VMEM((B,L),jnp.float32)]*2),
        out_shape=[jax.ShapeDtypeStruct((L,C),jnp.bfloat16), jax.ShapeDtypeStruct((C//64,L,L),jnp.bfloat16), jax.ShapeDtypeStruct((L,C),jnp.float32)],
        compiler_params=pltpu.CompilerParams(vmem_limit_bytes=50<<20),
    )(length, q, k, v, kf, qf)


def unskew(x, a8):
    nb = x.shape[1]//B
    sub = lax.broadcasted_iota(jnp.int32,(8,128),0)
    lane = lax.broadcasted_iota(jnp.int32,(8,128),1)
    keep = lane >= (127-a8) - sub
    idx=(lane-(127-a8)+sub)&127
    rot=[jnp.take_along_axis(x[:,t*128:t*128+128], idx, axis=1) for t in range(nb)]
    zero = jnp.zeros((8,128), x.dtype)
    return jnp.concatenate([jnp.where(keep, rot[t] if t<nb else zero, rot[t-1] if t>0 else zero) for t in range(nb+1)], axis=1)

def bwd_kernel(p_ref, q_ref, k_ref, v_ref, do_ref, ctx_ref, li_ref, kf_ref, qf_ref,
               dq_ref, dk_ref, dv_ref, dkf_ref, dqf_ref, sums_ref,
               dox_ref, dot_ref, qt_ref, kt_ref, vx_ref, ds_ref, d0, d1, akf, aqf, *, L, scale):
    W = L + B
    nb = L // B
    dd=(d0,d1)
    lane = lax.broadcasted_iota(jnp.int32, (1, 128), 1)
    mine = [lane < 64, lane >= 64]
    base_lane = [64, 0]
    dos = (do_ref[...].astype(jnp.float32) * li_ref[...]).astype(jnp.bfloat16)
    prod = dos.astype(jnp.float32) * ctx_ref[...].astype(jnp.float32)
    for h in range(2):
        delta = -jnp.sum(jnp.where(mine[h], prod, 0.0), axis=1, keepdims=True)
        hi = delta.astype(jnp.bfloat16).astype(jnp.float32)
        lo = delta - hi
        extra = jnp.where(lane == base_lane[h], hi, jnp.where(lane == base_lane[h]+1, lo, 0.0)).astype(jnp.bfloat16)
        dox_ref[h] = jnp.where(mine[h], dos, extra)
        vx_ref[h] = jnp.where(mine[h], v_ref[...], jnp.ones((), jnp.bfloat16))
    dot_ref[...] = dos.T
    qt_ref[...] = q_ref[...].T
    kt_ref[...] = k_ref[...].T
    akf[...] = jnp.zeros_like(akf)
    aqf[...] = jnp.zeros_like(aqf)
    def iblock(b, sq):
        r0 = pl.multiple_of(b*B, B)
        base = pl.multiple_of(L - B - b*B, B)
        outs=[]
        for h in range(2):
            dp = dotnt(dox_ref[h, pl.ds(r0,B), :], vx_ref[h])
            for a in range(0, B, SR):
                ds = p_ref[h, pl.ds(r0+a,SR), :].astype(jnp.float32) * dp[a:a+SR]
                ds_ref[h, pl.ds(r0+a,SR), :] = ds.astype(jnp.bfloat16)
                dd[h][a:a+SR, :] = jnp.concatenate([unskew(ds[s:s+8], a+s) for s in range(0,SR,8)],axis=0).astype(jnp.bfloat16)
            outs.append(dotnn(ds_ref[h, pl.ds(r0,B), :], k_ref[...]) + dotnn(dd[h][...], kf_ref[pl.ds(base, W), :]))
            akf[h*64:h*64+64, pl.ds(base, W)] += dotnn(qt_ref[h*64:h*64+64, pl.ds(r0,B)], dd[h][...])
        dq = jnp.where(mine[0], outs[0], outs[1]) * scale
        dq_ref[pl.ds(r0,B),:] = dq.astype(jnp.bfloat16)
        return sq + jnp.sum(dq.reshape(B//8,8,128), axis=0)
    sq = lax.fori_loop(0, nb, iblock, jnp.zeros((8,128),jnp.float32), unroll=UN)
    def jblock(b, sk):
        r0 = pl.multiple_of(b*B, B)
        base = pl.multiple_of(L - B - b*B, B)
        outs=[]
        for h in range(2):
            dst = ds_ref[h, :, pl.ds(r0,B)].T
            for a in range(0, B, SR):
                x = dst[a:a+SR].astype(jnp.float32)
                dd[h][a:a+SR, :] = jnp.concatenate([unskew(x[s:s+8], a+s) for s in range(0,SR,8)],axis=0).astype(jnp.bfloat16)
            outs.append(dotnn(dst, q_ref[...]) + dotnn(dd[h][...], qf_ref[pl.ds(base, W), :]))
            aqf[h*64:h*64+64, pl.ds(base, W)] += dotnn(kt_ref[h*64:h*64+64, pl.ds(r0,B)], dd[h][...])
        dk = jnp.where(mine[0], outs[0], outs[1]) * scale
        dk_ref[pl.ds(r0,B),:] = dk.astype(jnp.bfloat16)
        return sk + jnp.sum(dk.reshape(B//8,8,128), axis=0)
    sk = lax.fori_loop(0, nb, jblock, jnp.zeros((8,128),jnp.float32), unroll=UN)
    dvt = jnp.concatenate([dotnn(dot_ref[h*64:h*64+64,:], p_ref[h]) for h in range(2)], axis=0)
    dv = dvt.T
    dv_ref[...] = dv.astype(jnp.bfloat16)
    sv = jnp.sum(dv.reshape(L//8,8,128), axis=0)
    sums_ref[0:8] = sq
    sums_ref[8:16] = sk
    sums_ref[16:24] = sv
    dkf_ref[...] = (akf[...]*scale).astype(jnp.bfloat16)
    dqf_ref[...] = (aqf[...]*scale).astype(jnp.bfloat16)

def attn_bwd(p, q, k, v, do, ctx, linv, kf, qf, *, scale):
    L, C = q.shape
    col = lambda r: pl.BlockSpec((r,128), lambda h: (0,h))
    rowb = pl.BlockSpec((128,2*L), lambda h: (h,0))
    bf=jnp.bfloat16
    return pl.pallas_call(
        functools.partial(bwd_kernel, L=L, scale=scale),
        grid=(C//128,),
        in_specs=[pl.BlockSpec((2,L,L), lambda h:(h,0,0))]+[col(L)]*6+[col(2*L)]*2,
        out_specs=[col(L)]*3+[rowb]*2+[pl.BlockSpec((24,128), lambda h:(0,h))],
        scratch_shapes=[pltpu.VMEM((2,L,128),bf), pltpu.VMEM((128,L),bf), pltpu.VMEM((128,L),bf), pltpu.VMEM((128,L),bf), pltpu.VMEM((2,L,128),bf),
            pltpu.VMEM((2,L,L),bf), pltpu.VMEM((B,L+B),bf), pltpu.VMEM((B,L+B),bf), pltpu.VMEM((128,2*L),jnp.float32), pltpu.VMEM((128,2*L),jnp.float32)],
        out_shape=[jax.ShapeDtypeStruct((L,C),bf)]*3+[jax.ShapeDtypeStruct((C,2*L),bf)]*2+[jax.ShapeDtypeStruct((24,C),jnp.float32)],
        compiler_params=pltpu.CompilerParams(vmem_limit_bytes=56<<20),
    )(p, q, k, v, do, ctx, linv, kf, qf)


def normalize(z):
    center = z - jnp.mean(z, axis=-1, keepdims=True)
    r = lax.rsqrt(jnp.mean(center * center, axis=-1, keepdims=True) + EPSILON)
    return center * r, r


def norm_back(g, n, r):
    return r * (g - jnp.mean(g, axis=-1, keepdims=True) - n * jnp.mean(g * n, axis=-1, keepdims=True))


def mm(spec, a, b):
    return jnp.einsum(spec, a, b, preferred_element_type=jnp.float32)


def shards(
    inputs,
    cotangent,
    lengths,
    dealing,
    buckets,
    rel_embed,
    query_weight,
    key_weight,
    value_weight,
    proj_shifts,
    merge_weight,
    inner_weight,
    hidden_shift,
    outer_weight,
    layer_vectors,
):
    tn = lax.axis_size("tensor")
    gn = lax.axis_size("dp")
    me = lax.axis_index("dp") * tn + lax.axis_index("tensor")
    count, lg, dt = inputs.shape
    L, D = lg * gn, dt * tn
    assert count == tn * gn
    bf = jnp.bfloat16
    f32 = jnp.float32
    scale = 1.0 / math.sqrt(3.0 * HEAD)
    seq_axes = ("dp", "tensor")
    w_axes = ("tensor", "dp")

    def deal(a):
        a = lax.all_to_all(a, seq_axes, split_axis=0, concat_axis=0, tiled=True)
        return a.reshape(gn, tn, lg, dt).transpose(0, 2, 1, 3).reshape(L, D)

    def undeal(a):
        a = a.reshape(gn, lg, tn, dt).transpose(0, 2, 1, 3).reshape(count, lg, dt)
        return lax.all_to_all(a, seq_axes, split_axis=0, concat_axis=0, tiled=True)

    def gather(w):
        rows, cols = w.shape
        return lax.all_gather(w, w_axes, axis=0, tiled=False).reshape(tn, gn * rows, cols)

    def scatter(g):
        t, rows, cols = g.shape
        g = g.astype(bf).reshape(t, gn, rows // gn, cols)
        g = lax.psum_scatter(g, "dp", scatter_dimension=1, tiled=False)
        return lax.psum_scatter(g, "tensor", scatter_dimension=0, tiled=False)

    x = deal(inputs)
    rel_cols = lax.dynamic_slice_in_dim(rel_embed, lax.axis_index("tensor") * dt, dt, 1)
    first = gather(jnp.concatenate([query_weight, key_weight, value_weight], axis=1))
    rel4 = gather(rel_cols)
    wq, wk, wv = first[:, :, :dt], first[:, :, dt : 2 * dt], first[:, :, 2 * dt :]
    ff = inner_weight.shape[1]
    second = gather(jnp.concatenate([inner_weight, outer_weight, merge_weight], axis=1))
    wi, wo, wm = second[:, :, :ff], second[:, :, ff : 2 * ff], second[:, :, 2 * ff :]
    cot = deal(cotangent)
    biases = lax.all_gather(
        jnp.concatenate([proj_shifts.reshape(-1), hidden_shift]), "tensor", axis=0, tiled=False
    ).astype(f32)
    shifts = biases[:, : 3 * dt].reshape(tn, 3, dt)
    hidden_bias = biases[:, 3 * dt :]
    vectors = layer_vectors.astype(f32)
    length = jnp.sum(jnp.where(dealing == me, lengths, 0)).reshape(1)
    spans = rel4.shape[1]
    places = jnp.concatenate([buckets[::-1], jnp.full((1,), -1, jnp.int32)])
    onehot = (places[:, None] == jnp.arange(spans, dtype=jnp.int32)[None, :]).astype(bf)
    rel = rel4.transpose(1, 0, 2).reshape(spans, D)

    q = (mm("lk,tkc->ltc", x, wq) + shifts[:, 0]).astype(bf).reshape(L, D)
    k = (mm("lk,tkc->ltc", x, wk) + shifts[:, 1]).astype(bf).reshape(L, D)
    v = (mm("lk,tkc->ltc", x, wv) + shifts[:, 2]).astype(bf).reshape(L, D)
    qpos = (mm("lk,tkc->ltc", rel, wq) + shifts[:, 0]).astype(bf).reshape(spans, D)
    kpos = (mm("lk,tkc->ltc", rel, wk) + shifts[:, 1]).astype(bf).reshape(spans, D)
    qf = mm("ms,sd->md", onehot, qpos).astype(bf)
    kf = mm("ms,sd->md", onehot, kpos).astype(bf)
    ctx, probs, inv = attn_fwd(length, q, k, v, kf, qf, scale=scale)
    ctx4 = ctx.reshape(L, tn, dt)
    z1 = mm("ltc,toc->lo", ctx4, wm) + vectors[0] + x.astype(f32)
    n1, r1 = normalize(z1)
    h1 = n1 * vectors[1] + vectors[2]
    h1_low = h1.astype(bf)
    pre = mm("la,tah->lth", h1_low, wi) + hidden_bias
    phi = 0.5 + 0.5 * lax.erf(pre * math.sqrt(0.5))
    act = (pre * phi).astype(bf)
    slope = phi + pre * jnp.exp(-0.5 * pre * pre) * (1.0 / math.sqrt(2.0 * math.pi))
    slope = slope.astype(bf)
    z2 = mm("ltf,tof->lo", act, wo) + vectors[3] + h1
    n2, r2 = normalize(z2)
    y = n2 * vectors[4] + vectors[5]
    out = undeal(y.astype(bf))
    dy = cot.astype(f32)
    dz2 = norm_back(dy * vectors[4], n2, r2)
    dffn = dz2.astype(bf)
    outer_part = mm("lo,ltf->tof", dffn, act)
    dact = mm("lo,tof->ltf", dffn, wo)
    dpre = dact * slope.astype(f32)
    dpre_low = dpre.astype(bf)
    hidden_sum = jnp.sum(dpre, axis=0).reshape(-1)
    inner_part = mm("la,lth->tah", h1_low, dpre_low)
    dh1 = dz2 + mm("lth,tah->la", dpre_low, wi)
    dz1 = norm_back(dh1 * vectors[1], n1, r1)
    dattn = dz1.astype(bf)
    merge_part = mm("lo,ltc->toc", dattn, ctx4)
    dctx = mm("lo,toc->ltc", dattn, wm).astype(bf).reshape(L, D)
    outer_grad = scatter(outer_part)
    inner_grad = scatter(inner_part)
    merge_grad = scatter(merge_part)
    dq, dk, dv, dkf, dqf, sums = attn_bwd(probs, q, k, v, dctx, ctx, inv, kf, qf, scale=scale)
    dkpos = mm("dm,ms->sd", dkf, onehot)
    dqpos = mm("dm,ms->sd", dqf, onehot)
    sums = sums.reshape(3, 8, D).sum(axis=1)
    shift_sum = sums + jnp.stack(
        [jnp.sum(dqpos, axis=0), jnp.sum(dkpos, axis=0), jnp.zeros((D,), f32)]
    )
    dq4, dk4, dv4 = (a.reshape(L, tn, dt) for a in (dq, dk, dv))
    dqp4, dkp4 = (a.astype(bf).reshape(spans, tn, dt) for a in (dqpos, dkpos))
    dx = dz1 + mm("ltj,tej->le", dq4, wq) + mm("ltj,tej->le", dk4, wk) + mm("ltj,tej->le", dv4, wv)
    grad_in = undeal(dx.astype(bf))
    query_part = mm("le,ltj->tej", x, dq4) + mm("se,stj->tej", rel, dqp4)
    key_part = mm("le,ltj->tej", x, dk4) + mm("se,stj->tej", rel, dkp4)
    value_part = mm("le,ltj->tej", x, dv4)
    rel_part = mm("stj,tej->se", dqp4, wq) + mm("stj,tej->se", dkp4, wk)
    qkv = scatter(jnp.concatenate([query_part, key_part, value_part], axis=2)).astype(f32)
    rel_mine = lax.psum_scatter(
        rel_part.astype(bf).reshape(count, spans // count, D), seq_axes, scatter_dimension=0, tiled=False
    )
    rel_grad = lax.all_gather(rel_mine.astype(f32), seq_axes, axis=0, tiled=True)
    vector_sum = jnp.stack(
        [
            jnp.sum(dz1, axis=0),
            jnp.sum(dh1 * n1, axis=0),
            jnp.sum(dh1, axis=0),
            jnp.sum(dz2, axis=0),
            jnp.sum(dy * n2, axis=0),
            jnp.sum(dy, axis=0),
        ]
    )
    hidden_sum, vector_sum = lax.psum((hidden_sum, vector_sum), seq_axes)
    shift_sum = lax.psum(shift_sum, seq_axes)
    return (
        out,
        grad_in,
        rel_grad,
        qkv[:, :dt],
        qkv[:, dt : 2 * dt],
        qkv[:, 2 * dt :],
        shift_sum,
        merge_grad.astype(f32),
        inner_grad.astype(f32),
        hidden_sum,
        outer_grad.astype(f32),
        vector_sum,
    )


def solution(mesh):
    split = P("dp", "tensor")
    whole = P(None, "dp", "tensor")
    in_specs = (
        whole, whole, P(), P(), P(), P("dp", None), split, split, split, P(None, "tensor"),
        split, split, P("tensor"), split, P(),
    )
    out_specs = (whole, whole, P(), split, split, split, P(), split, split, P(), split, P())
    return jax.shard_map(shards, mesh=mesh, in_specs=in_specs, out_specs=out_specs, check_vma=False)
```

```python
import functools
import math

import jax
import jax.numpy as jnp
from jax import lax
from jax.experimental import pallas as pl
from jax.experimental.pallas import tpu as pltpu
from jax.sharding import PartitionSpec as P

EPSILON = 1e-07
HEAD = 64
B = 128
SR = 16
UN = 8
NT = (((1,), (1,)), ((), ()))


def dotnt(a, b):
    return lax.dot_general(a, b, NT, preferred_element_type=jnp.float32)


def dotnn(a, b):
    return lax.dot_general(a, b, (((1,), (0,)), ((), ())), preferred_element_type=jnp.float32)


def skew(g_ref, a, n, L):
    parts=[]
    nb=L//B
    for a8 in range(a,a+n,8):
        rot=[pltpu.roll(g_ref[a8:a8+8,t*128:t*128+128], 1+a8, 1, stride=1, stride_axis=0) for t in range(nb+1)]
        msk=lax.broadcasted_iota(jnp.int32,(8,128),1) < (1+a8+lax.broadcasted_iota(jnp.int32,(8,128),0))
        parts.append(jnp.concatenate([jnp.where(msk,rot[t],rot[t+1]) for t in range(nb)],axis=1))
    return jnp.concatenate(parts,axis=0)

def fwd_kernel(len_ref, q_ref, k_ref, v_ref, kf_ref, qf_ref, ctx_ref, p_ref, l_ref, t_ref, kx_ref, vx_ref, g0, g1, s0, s1, *, L, scale):
    W = L + B
    nb = L // B
    gs=(g0,g1); ss=(s0,s1)
    lane = lax.broadcasted_iota(jnp.int32, (1, 128), 1)
    length = len_ref[0]
    row = lax.broadcasted_iota(jnp.int32, (L, 128), 0)
    c2 = scale * math.log2(math.e)
    eye = (lax.broadcasted_iota(jnp.int32,(B,B),0)==lax.broadcasted_iota(jnp.int32,(B,B),1)).astype(jnp.bfloat16)
    zero = jnp.zeros((), jnp.bfloat16)
    mine = [lane < 64, lane >= 64]
    first_other = [lane==64, lane==0]
    for h in range(2):
        bias = jnp.where((row >= length) & first_other[h], -1e30, 0.0).astype(jnp.bfloat16)
        kx_ref[h] = jnp.where(mine[h], k_ref[...], bias)
        vx_ref[h] = jnp.where(mine[h], v_ref[...], jnp.ones((), jnp.bfloat16))
    def tblock(b, _):
        r0 = pl.multiple_of(b*B, B)
        base = pl.multiple_of(L - B - b*B, B)
        for h in range(2):
            kb = jnp.where(mine[h], k_ref[pl.ds(r0,B),:], zero)
            gs[h][...] = dotnt(kb, qf_ref[pl.ds(base, W), :])
        for h in range(2):
            for a in range(0, B, SR):
                t_ref[h, pl.ds(r0+a,SR), :] = skew(gs[h], a, SR, L).astype(jnp.bfloat16)
        return 0
    lax.fori_loop(0, nb, tblock, 0, unroll=2)
    def scores(b, h):
        r0 = pl.multiple_of(b*B, B)
        base = pl.multiple_of(L - B - b*B, B)
        qb = q_ref[pl.ds(r0,B),:]
        qm = jnp.where(mine[h], qb, zero)
        qx = jnp.where(mine[h], qb, first_other[h].astype(jnp.bfloat16))
        gs[h][...] = dotnt(qm, kf_ref[pl.ds(base, W), :])
        lhs = jnp.concatenate([qx, eye], axis=1)
        rhs = jnp.concatenate([kx_ref[h], t_ref[h, :, pl.ds(r0,B)]], axis=1)
        ss[h][...] = dotnt(lhs, rhs)
    def soft(b, h):
        r0 = pl.multiple_of(b*B, B)
        tops=[]
        for a in range(0, B, 8):
            s = ss[h][a:a+8] + skew(gs[h], a, 8, L)
            ss[h][a:a+8] = s
            tops.append(functools.reduce(jnp.maximum,[s[:,t*128:t*128+128] for t in range(nb)]))
        m = jnp.max(jnp.concatenate(tops,axis=0), axis=1, keepdims=True) * c2
        for a in range(0, B, SR):
            p_ref[h, pl.ds(r0+a,SR), :] = jnp.exp2(ss[h][a:a+SR]*c2 - m[a:a+SR]).astype(jnp.bfloat16)
    def out(b, h):
        r0 = pl.multiple_of(b*B, B)
        return dotnn(p_ref[h, pl.ds(r0,B), :], vx_ref[h])
    def finish(b, o0, o1):
        r0 = pl.multiple_of(b*B, B)
        num = jnp.where(mine[0], o0, o1)
        den = jnp.where(mine[0], pltpu.roll(o0,64,1), pltpu.roll(o1,64,1))
        inv = 1.0/den
        ctx_ref[pl.ds(r0,B),:] = (num*inv).astype(jnp.bfloat16)
        l_ref[pl.ds(r0,B),:] = inv
    scores(0,0)
    def sblock(b, o0):
        scores(b,1)
        soft(b,0)
        o0 = out(b,0)
        scores(jnp.minimum(b+1,nb-1),0)
        soft(b,1)
        o1 = out(b,1)
        finish(b,o0,o1)
        return 0
    lax.fori_loop(0, nb, sblock, 0, unroll=8)


def attn_fwd(length, qkv, far, *, scale):
    _, L, C = qkv.shape
    part = lambda j, r: pl.BlockSpec((None, r, 128), lambda h, *_: (j, 0, h))
    return pl.pallas_call(
        functools.partial(fwd_kernel, L=L, scale=scale),
        grid_spec=pltpu.PrefetchScalarGridSpec(
            num_scalar_prefetch=1,
            grid=(C // 128,),
            in_specs=[part(0, L), part(1, L), part(2, L), part(1, 2 * L), part(0, 2 * L)],
            out_specs=[
                pl.BlockSpec((L, 128), lambda h, *_: (0, h)),
                pl.BlockSpec((2, L, L), lambda h, *_: (h, 0, 0)),
                pl.BlockSpec((L, 128), lambda h, *_: (0, h)),
            ],
            scratch_shapes=[pltpu.VMEM((2, L, L), jnp.bfloat16)]
            + [pltpu.VMEM((2, L, 128), jnp.bfloat16)] * 2
            + [pltpu.VMEM((B, L + B), jnp.float32)] * 2
            + [pltpu.VMEM((B, L), jnp.float32)] * 2,
        ),
        out_shape=[
            jax.ShapeDtypeStruct((L, C), jnp.bfloat16),
            jax.ShapeDtypeStruct((C // HEAD, L, L), jnp.bfloat16),
            jax.ShapeDtypeStruct((L, C), jnp.float32),
        ],
        compiler_params=pltpu.CompilerParams(vmem_limit_bytes=50 << 20),
        cost_estimate=pl.CostEstimate(flops=80 * 10**9, bytes_accessed=60 * 10**6, transcendentals=0),
    )(length, qkv, qkv, qkv, far, far)


def unskew(x, a8):
    nb = x.shape[1]//B
    sub = lax.broadcasted_iota(jnp.int32,(8,128),0)
    lane = lax.broadcasted_iota(jnp.int32,(8,128),1)
    keep = lane >= (127-a8) - sub
    idx=(lane-(127-a8)+sub)&127
    rot=[jnp.take_along_axis(x[:,t*128:t*128+128], idx, axis=1) for t in range(nb)]
    zero = jnp.zeros((8,128), x.dtype)
    return jnp.concatenate([jnp.where(keep, rot[t] if t<nb else zero, rot[t-1] if t>0 else zero) for t in range(nb+1)], axis=1)

def bwd_kernel(p_ref, q_ref, k_ref, v_ref, do_ref, ctx_ref, li_ref, kf_ref, qf_ref,
               dq_ref, dk_ref, dv_ref, dkf_ref, dqf_ref, sums_ref,
               dox_ref, dot_ref, qt_ref, kt_ref, vx_ref, ds_ref, d0, d1, akf, aqf, *, L, scale):
    W = L + B
    nb = L // B
    dd=(d0,d1)
    lane = lax.broadcasted_iota(jnp.int32, (1, 128), 1)
    mine = [lane < 64, lane >= 64]
    base_lane = [64, 0]
    dos = (do_ref[...].astype(jnp.float32) * li_ref[...]).astype(jnp.bfloat16)
    prod = dos.astype(jnp.float32) * ctx_ref[...].astype(jnp.float32)
    for h in range(2):
        delta = -jnp.sum(jnp.where(mine[h], prod, 0.0), axis=1, keepdims=True)
        hi = delta.astype(jnp.bfloat16).astype(jnp.float32)
        lo = delta - hi
        extra = jnp.where(lane == base_lane[h], hi, jnp.where(lane == base_lane[h]+1, lo, 0.0)).astype(jnp.bfloat16)
        dox_ref[h] = jnp.where(mine[h], dos, extra)
        vx_ref[h] = jnp.where(mine[h], v_ref[...], jnp.ones((), jnp.bfloat16))
    dot_ref[...] = dos.T
    qt_ref[...] = q_ref[...].T
    kt_ref[...] = k_ref[...].T
    akf[...] = jnp.zeros_like(akf)
    aqf[...] = jnp.zeros_like(aqf)
    def iblock(b, sq):
        r0 = pl.multiple_of(b*B, B)
        base = pl.multiple_of(L - B - b*B, B)
        outs=[]
        for h in range(2):
            dp = dotnt(dox_ref[h, pl.ds(r0,B), :], vx_ref[h])
            for a in range(0, B, SR):
                ds = p_ref[h, pl.ds(r0+a,SR), :].astype(jnp.float32) * dp[a:a+SR]
                ds_ref[h, pl.ds(r0+a,SR), :] = ds.astype(jnp.bfloat16)
                dd[h][a:a+SR, :] = jnp.concatenate([unskew(ds[s:s+8], a+s) for s in range(0,SR,8)],axis=0).astype(jnp.bfloat16)
            outs.append(dotnn(ds_ref[h, pl.ds(r0,B), :], k_ref[...]) + dotnn(dd[h][...], kf_ref[pl.ds(base, W), :]))
            akf[h*64:h*64+64, pl.ds(base, W)] += dotnn(qt_ref[h*64:h*64+64, pl.ds(r0,B)], dd[h][...])
        dq = jnp.where(mine[0], outs[0], outs[1]) * scale
        dq_ref[pl.ds(r0,B),:] = dq.astype(jnp.bfloat16)
        return sq + jnp.sum(dq.reshape(B//8,8,128), axis=0)
    sq = lax.fori_loop(0, nb, iblock, jnp.zeros((8,128),jnp.float32), unroll=UN)
    def jblock(b, sk):
        r0 = pl.multiple_of(b*B, B)
        base = pl.multiple_of(L - B - b*B, B)
        outs=[]
        for h in range(2):
            dst = ds_ref[h, :, pl.ds(r0,B)].T
            for a in range(0, B, SR):
                x = dst[a:a+SR].astype(jnp.float32)
                dd[h][a:a+SR, :] = jnp.concatenate([unskew(x[s:s+8], a+s) for s in range(0,SR,8)],axis=0).astype(jnp.bfloat16)
            outs.append(dotnn(dst, q_ref[...]) + dotnn(dd[h][...], qf_ref[pl.ds(base, W), :]))
            aqf[h*64:h*64+64, pl.ds(base, W)] += dotnn(kt_ref[h*64:h*64+64, pl.ds(r0,B)], dd[h][...])
        dk = jnp.where(mine[0], outs[0], outs[1]) * scale
        dk_ref[pl.ds(r0,B),:] = dk.astype(jnp.bfloat16)
        return sk + jnp.sum(dk.reshape(B//8,8,128), axis=0)
    sk = lax.fori_loop(0, nb, jblock, jnp.zeros((8,128),jnp.float32), unroll=UN)
    dvt = jnp.concatenate([dotnn(dot_ref[h*64:h*64+64,:], p_ref[h]) for h in range(2)], axis=0)
    dv = dvt.T
    dv_ref[...] = dv.astype(jnp.bfloat16)
    sv = jnp.sum(dv.reshape(L//8,8,128), axis=0)
    sums_ref[0:8] = sq
    sums_ref[8:16] = sk
    sums_ref[16:24] = sv
    dkf_ref[...] = (akf[...]*scale).astype(jnp.bfloat16)
    dqf_ref[...] = (aqf[...]*scale).astype(jnp.bfloat16)


def attn_bwd(p, qkv, do, ctx, linv, far, *, scale):
    _, L, C = qkv.shape
    bf = jnp.bfloat16
    part = lambda j, r: pl.BlockSpec((None, r, 128), lambda h: (j, 0, h))
    col = lambda r: pl.BlockSpec((r, 128), lambda h: (0, h))
    rowb = pl.BlockSpec((128, 2 * L), lambda h: (h, 0))
    return pl.pallas_call(
        functools.partial(bwd_kernel, L=L, scale=scale),
        grid=(C // 128,),
        in_specs=[pl.BlockSpec((2, L, L), lambda h: (h, 0, 0)), part(0, L), part(1, L), part(2, L)]
        + [col(L)] * 3
        + [part(1, 2 * L), part(0, 2 * L)],
        out_specs=[col(L)] * 3 + [rowb] * 2 + [col(24)],
        scratch_shapes=[pltpu.VMEM((2, L, 128), bf)]
        + [pltpu.VMEM((128, L), bf)] * 3
        + [pltpu.VMEM((2, L, 128), bf), pltpu.VMEM((2, L, L), bf)]
        + [pltpu.VMEM((B, L + B), bf)] * 2
        + [pltpu.VMEM((128, 2 * L), jnp.float32)] * 2,
        out_shape=[jax.ShapeDtypeStruct((L, C), bf)] * 3
        + [jax.ShapeDtypeStruct((C, 2 * L), bf)] * 2
        + [jax.ShapeDtypeStruct((24, C), jnp.float32)],
        compiler_params=pltpu.CompilerParams(vmem_limit_bytes=56 << 20),
        cost_estimate=pl.CostEstimate(flops=120 * 10**9, bytes_accessed=80 * 10**6, transcendentals=0),
    )(p, qkv, qkv, qkv, do, ctx, linv, far, far)


def spec(block, index, once=False):
    if once:
        return pl.BlockSpec(block, index, pipeline_mode=pl.Buffered(1))
    return pl.BlockSpec(block, index)


def norm_rows(z):
    center = z - jnp.mean(z, axis=-1, keepdims=True)
    r = lax.rsqrt(jnp.mean(center * center, axis=-1, keepdims=True) + EPSILON)
    return center * r, r


def norm_back(g, n, r):
    return r * (g - jnp.mean(g, axis=-1, keepdims=True) - n * jnp.mean(g * n, axis=-1, keepdims=True))


def fold8(v):
    return jnp.sum(v.reshape(v.shape[0] // 8, 8, v.shape[1]), axis=0)


def project_kernel(xd_ref, rel4_ref, w_ref, sh_ref, pl_ref, qkv_ref, far_ref, x_ref, rel_ref, hot_ref):
    t, j = pl.program_id(0), pl.program_id(1)
    gn, tn, lg, dt = xd_ref.shape
    spans = rel_ref.shape[0]
    rg = spans // gn

    @pl.when((t == 0) & (j == 0))
    def _():
        for g in range(gn):
            for s in range(tn):
                x_ref[g * lg : (g + 1) * lg, s * dt : (s + 1) * dt] = xd_ref[g, s]
                rel_ref[g * rg : (g + 1) * rg, s * dt : (s + 1) * dt] = rel4_ref[g, s]
        rows = hot_ref.shape[0]
        lanes = lax.broadcasted_iota(jnp.int32, (rows, spans), 1)
        hot_ref[...] = (pl_ref[...] == lanes).astype(jnp.float32).astype(jnp.bfloat16)

    w = w_ref[:, 0].reshape(x_ref.shape[1], dt)
    shift = sh_ref[0, pl.ds(j, 1), :]
    qkv_ref[0] = (dotnn(x_ref[...], w) + shift).astype(jnp.bfloat16)

    @pl.when(j < 2)
    def _():
        place = (dotnn(rel_ref[...], w) + shift).astype(jnp.bfloat16)
        far_ref[0] = dotnn(hot_ref[...], place).astype(jnp.bfloat16)


def project(xd, first, shifts, places, per):
    gn, tn, lg, dt = xd.shape
    L, D = gn * lg, tn * dt
    rg = (first.shape[2] - 3 * per - 8)
    spans = rg * gn
    bf = jnp.bfloat16
    return pl.pallas_call(
        project_kernel,
        grid=(tn, 3),
        in_specs=[
            spec((gn, tn, lg, dt), lambda t, j: (0, 0, 0, 0), True),
            spec((gn, tn, rg, dt), lambda t, j: (0, 0, 3 * per // rg, 0), True),
            spec((gn, 1, per, dt), lambda t, j: (0, t, j, 0)),
            spec((1, 3, dt), lambda t, j: (t, 0, 0)),
            spec((2 * L, 1), lambda t, j: (0, 0), True),
        ],
        out_specs=[
            spec((1, L, dt), lambda t, j: (j, 0, t)),
            spec((1, 2 * L, dt), lambda t, j: (jnp.minimum(j, 1), 0, t)),
            spec((L, D), lambda t, j: (0, 0)),
            spec((spans, D), lambda t, j: (0, 0)),
            spec((2 * L, spans), lambda t, j: (0, 0)),
        ],
        out_shape=[
            jax.ShapeDtypeStruct((3, L, D), bf),
            jax.ShapeDtypeStruct((2, 2 * L, D), bf),
            jax.ShapeDtypeStruct((L, D), bf),
            jax.ShapeDtypeStruct((spans, D), bf),
            jax.ShapeDtypeStruct((2 * L, spans), bf),
        ],
        compiler_params=pltpu.CompilerParams(vmem_limit_bytes=50 << 20),
        cost_estimate=pl.CostEstimate(flops=14 * 10**9, bytes_accessed=30 * 10**6, transcendentals=0),
    )(xd, first, first, shifts, places)


RB = 256


def middle_kernel(ctx_ref, x_ref, wm_ref, wi_ref, wo_ref, hb_ref, vec_ref, cot_ref,
                  hl_ref, n1_ref, r1_ref, act_ref, slope_ref, y_ref, df_ref, sums_ref, acc_ref, h1_ref):
    t = pl.program_id(0)
    L, D = x_ref.shape
    gn, tn, lg, dt = cot_ref.shape
    f32, bf = jnp.float32, jnp.bfloat16

    @pl.when(t == 0)
    def _():
        for r in range(0, L, RB):
            z1 = vec_ref[0:1] + x_ref[r : r + RB].astype(f32)
            for s in range(tn):
                z1 = z1 + dotnt(ctx_ref[r : r + RB, s * dt : (s + 1) * dt], wm_ref[s].reshape(D, dt))
            n1, r1 = norm_rows(z1)
            h1 = n1 * vec_ref[1:2] + vec_ref[2:3]
            h1_ref[r : r + RB] = h1
            hl_ref[r : r + RB] = h1.astype(bf)
            n1_ref[r : r + RB] = n1.astype(bf)
            r1_ref[r : r + RB] = jnp.broadcast_to(r1, (RB, 128))

    wi = wi_ref[0].reshape(D, wi_ref.shape[3])
    wo = wo_ref[0].reshape(D, wo_ref.shape[3])
    for r in range(0, L, RB):
        pre = dotnn(hl_ref[r : r + RB], wi) + hb_ref[0]
        phi = 0.5 + 0.5 * lax.erf(pre * math.sqrt(0.5))
        act = (pre * phi).astype(bf)
        act_ref[r : r + RB] = act
        bell = jnp.exp(-0.5 * pre * pre) * (1.0 / math.sqrt(2.0 * math.pi))
        slope_ref[r : r + RB] = (phi + pre * bell).astype(bf)
        part = dotnt(act, wo)

        @pl.when(t == 0)
        def _():
            acc_ref[r : r + RB] = part

        @pl.when(t > 0)
        def _():
            acc_ref[r : r + RB] += part

    @pl.when(t == pl.num_programs(0) - 1)
    def _():
        s0 = jnp.zeros((8, D), f32)
        s1 = jnp.zeros((8, D), f32)
        s2 = jnp.zeros((8, D), f32)
        for g in range(gn):
            rows = slice(g * lg, (g + 1) * lg)
            z2 = acc_ref[rows] + vec_ref[3:4] + h1_ref[rows]
            n2, r2 = norm_rows(z2)
            y = (n2 * vec_ref[4:5] + vec_ref[5:6]).astype(bf)
            for s in range(tn):
                y_ref[g, s] = y[:, s * dt : (s + 1) * dt]
            dy = jnp.concatenate([cot_ref[g, s] for s in range(tn)], axis=1).astype(f32)
            dz2 = norm_back(dy * vec_ref[4:5], n2, r2)
            df_ref[rows] = dz2.astype(bf)
            s0, s1, s2 = s0 + fold8(dz2), s1 + fold8(dy * n2), s2 + fold8(dy)
        sums_ref[0:8], sums_ref[8:16], sums_ref[16:24] = s0, s1, s2


def middle(ctx, x, second, hidden_bias, vectors, cot, per):
    gn, tn, lg, dt = cot.shape
    L, D = x.shape
    ff = hidden_bias.shape[2]
    bf, f32 = jnp.bfloat16, jnp.float32
    full = lambda shape: spec(shape, lambda t: (0,) * len(shape), True)
    return pl.pallas_call(
        middle_kernel,
        grid=(tn,),
        in_specs=[
            full((L, D)),
            full((L, D)),
            spec((tn, gn, per, dt), lambda t: (0, 0, 0, 2 * ff // dt), True),
            spec((1, gn, per, ff), lambda t: (t, 0, 0, 0)),
            spec((1, gn, per, ff), lambda t: (t, 0, 0, 1)),
            spec((1, 1, ff), lambda t: (t, 0, 0)),
            full((6, D)),
            full((gn, tn, lg, dt)),
        ],
        out_specs=[
            full((L, D)), full((L, D)), full((L, 128)),
            spec((L, ff), lambda t: (0, t)), spec((L, ff), lambda t: (0, t)),
            full((gn, tn, lg, dt)), full((L, D)), full((24, D)),
        ],
        out_shape=[
            jax.ShapeDtypeStruct((L, D), bf),
            jax.ShapeDtypeStruct((L, D), bf),
            jax.ShapeDtypeStruct((L, 128), f32),
            jax.ShapeDtypeStruct((L, tn * ff), bf),
            jax.ShapeDtypeStruct((L, tn * ff), bf),
            jax.ShapeDtypeStruct((gn, tn, lg, dt), bf),
            jax.ShapeDtypeStruct((L, D), bf),
            jax.ShapeDtypeStruct((24, D), f32),
        ],
        scratch_shapes=[pltpu.VMEM((L, D), f32), pltpu.VMEM((L, D), f32)],
        compiler_params=pltpu.CompilerParams(vmem_limit_bytes=58 << 20),
        cost_estimate=pl.CostEstimate(flops=30 * 10**9, bytes_accessed=60 * 10**6, transcendentals=0),
    )(ctx, x, second, second, second, hidden_bias, vectors, cot)


def ffn_back_kernel(df_ref, hl_ref, n1_ref, r1_ref, act_ref, slope_ref, wi_ref, wo_ref, vec_ref,
                    pay_ref, hid_ref, da_ref, sums_ref, dft_ref, hlt_ref, acc_ref, dp_ref):
    t = pl.program_id(0)
    L, D = df_ref.shape
    ff = act_ref.shape[1]
    gn, _, per, _ = pay_ref.shape
    f32, bf = jnp.float32, jnp.bfloat16

    @pl.when(t == 0)
    def _():
        for r in range(0, L, RB):
            dft_ref[:, r : r + RB] = df_ref[r : r + RB].T
            hlt_ref[:, r : r + RB] = hl_ref[r : r + RB].T
            acc_ref[r : r + RB] = df_ref[r : r + RB].astype(f32)

    wi = wi_ref[0].reshape(D, ff)
    wo = wo_ref[0].reshape(D, ff)
    hid = jnp.zeros((8, ff), f32)
    for r in range(0, L, RB):
        dpre = dotnn(df_ref[r : r + RB], wo) * slope_ref[r : r + RB].astype(f32)
        hid = hid + fold8(dpre)
        low = dpre.astype(bf)
        dp_ref[r : r + RB] = low
        acc_ref[r : r + RB] += dotnt(low, wi)
    hid_ref[0] = hid
    for r in range(0, D, RB):
        og = dotnn(dft_ref[r : r + RB], act_ref[...]).astype(bf)
        ig = dotnn(hlt_ref[r : r + RB], dp_ref[...]).astype(bf)
        for c in range(0, RB, per):
            pay_ref[(r + c) // per, 0, :, 0:ff] = ig[c : c + per]
            pay_ref[(r + c) // per, 0, :, ff : 2 * ff] = og[c : c + per]

    @pl.when(t == pl.num_programs(0) - 1)
    def _():
        s0 = jnp.zeros((8, D), f32)
        s1 = jnp.zeros((8, D), f32)
        s2 = jnp.zeros((8, D), f32)
        for r in range(0, L, 128):
            rows = slice(r, r + 128)
            dh1 = acc_ref[rows]
            n1 = n1_ref[rows].astype(f32)
            dz1 = norm_back(dh1 * vec_ref[1:2], n1, r1_ref[rows, 0:1])
            da_ref[rows] = dz1.astype(bf)
            s0, s1, s2 = s0 + fold8(dz1), s1 + fold8(dh1 * n1), s2 + fold8(dh1)
        sums_ref[0:8], sums_ref[8:16], sums_ref[16:24] = s0, s1, s2


def ffn_back(dffn, h1_low, n1, r1, act, slope, second, vectors):
    tn, gn, per, wide = second.shape
    L, D = dffn.shape
    ff = act.shape[1] // tn
    bf, f32 = jnp.bfloat16, jnp.float32
    full = lambda shape: spec(shape, lambda t: (0,) * len(shape), True)
    return pl.pallas_call(
        ffn_back_kernel,
        grid=(tn,),
        in_specs=[
            full((L, D)), full((L, D)), full((L, D)), full((L, 128)),
            spec((L, ff), lambda t: (0, t)), spec((L, ff), lambda t: (0, t)),
            spec((1, gn, per, ff), lambda t: (t, 0, 0, 0)),
            spec((1, gn, per, ff), lambda t: (t, 0, 0, 1)),
            full((6, D)),
        ],
        out_specs=[
            spec((gn, 1, per, 2 * ff), lambda t: (0, t, 0, 0)),
            spec((1, 8, ff), lambda t: (t, 0, 0)),
            full((L, D)), full((24, D)),
        ],
        out_shape=[
            jax.ShapeDtypeStruct((gn, tn, per, wide), bf),
            jax.ShapeDtypeStruct((tn, 8, ff), f32),
            jax.ShapeDtypeStruct((L, D), bf),
            jax.ShapeDtypeStruct((24, D), f32),
        ],
        scratch_shapes=[pltpu.VMEM((D, L), bf), pltpu.VMEM((D, L), bf), pltpu.VMEM((L, D), f32), pltpu.VMEM((L, ff), bf)],
        compiler_params=pltpu.CompilerParams(vmem_limit_bytes=58 << 20),
        cost_estimate=pl.CostEstimate(flops=40 * 10**9, bytes_accessed=80 * 10**6, transcendentals=0),
    )(dffn, h1_low, n1, r1, act, slope, second, second, vectors)


def merge_back_kernel(da_ref, ctx_ref, wm_ref, pay_in, pay_ref, dctx_ref, dat_ref):
    t = pl.program_id(0)
    L, D = da_ref.shape
    gn, _, per, dt = pay_ref.shape

    @pl.when(t == 0)
    def _():
        for r in range(0, L, RB):
            dat_ref[:, r : r + RB] = da_ref[r : r + RB].T

    dctx_ref[...] = dotnn(da_ref[...], wm_ref[0].reshape(D, dt)).astype(jnp.bfloat16)
    pay_ref[:, 0] = dotnn(dat_ref[...], ctx_ref[...]).astype(jnp.bfloat16).reshape(gn, per, dt)


def merge_back(dattn, ctx, second, payload):
    tn, gn, per, wide = second.shape
    L, D = dattn.shape
    dt = D // tn
    last = wide // dt - 1
    bf = jnp.bfloat16
    return pl.pallas_call(
        merge_back_kernel,
        grid=(tn,),
        in_specs=[
            spec((L, D), lambda t: (0, 0), True),
            spec((L, dt), lambda t: (0, t)),
            spec((1, gn, per, dt), lambda t: (t, 0, 0, last)),
            pl.BlockSpec(memory_space=pl.ANY),
        ],
        out_specs=[
            spec((gn, 1, per, dt), lambda t: (0, t, 0, last)),
            spec((L, dt), lambda t: (0, t)),
        ],
        out_shape=[
            jax.ShapeDtypeStruct((gn, tn, per, wide), bf),
            jax.ShapeDtypeStruct((L, D), bf),
        ],
        scratch_shapes=[pltpu.VMEM((D, L), bf)],
        input_output_aliases={3: 0},
        compiler_params=pltpu.CompilerParams(vmem_limit_bytes=50 << 20),
        cost_estimate=pl.CostEstimate(flops=4 * 10**9, bytes_accessed=10 * 10**6, transcendentals=0),
    )(dattn, ctx, second, payload)


def tail_kernel(x_ref, rel_ref, hot_ref, da_ref, dq_ref, dk_ref, dv_ref, dqf_ref, dkf_ref, sm_ref, w_ref, small_ref,
                pay_ref, dx_ref, xt_ref, acc_ref, ra_ref, *, first_shift):
    t = pl.program_id(0)
    L, D = x_ref.shape
    spans = rel_ref.shape[0]
    gn, tn, lg, dt = dx_ref.shape
    per = D // gn
    rg = spans // gn
    sr = small_ref.shape[2]
    f32, bf = jnp.float32, jnp.bfloat16

    @pl.when(t == 0)
    def _():
        for r in range(0, L, RB):
            xt_ref[:, r : r + RB] = x_ref[r : r + RB].T
            acc_ref[r : r + RB] = da_ref[r : r + RB].astype(f32)
        for r in range(0, spans, RB):
            xt_ref[:, L + r : L + r + RB] = rel_ref[r : r + RB].T
        ra_ref[...] = jnp.zeros_like(ra_ref)

    w = [w_ref[:, 0, j * per : (j + 1) * per, :].reshape(D, dt) for j in range(3)]
    qp = dotnn(dqf_ref[...], hot_ref[...]).T
    kp = dotnn(dkf_ref[...], hot_ref[...]).T
    pos = [qp.astype(bf), kp.astype(bf)]
    tops = [dq_ref, dk_ref, dv_ref]
    rows = 3 * per + rg
    pay_ref[:, t, rows : rows + sr, :] = small_ref[0].astype(bf)
    for j in range(3):
        total = jnp.sum(sm_ref[8 * j : 8 * j + 8], axis=0, keepdims=True)
        if j < 2:
            total = total + jnp.sum((qp, kp)[j], axis=0, keepdims=True)
            both = jnp.concatenate([tops[j][...], pos[j]], axis=0)
            grad = dotnn(xt_ref[...], both)
            ra_ref[...] += dotnt(pos[j], w[j])
        else:
            grad = dotnn(xt_ref[:, 0:L], tops[j][...])
        pay_ref[:, t, j * per : (j + 1) * per, :] = grad.astype(bf).reshape(gn, per, dt)
        at = first_shift + j
        pay_ref[at // sr, t, rows + at % sr : rows + at % sr + 1, :] = total.astype(bf)
    for r in range(0, L, RB):
        acc_ref[r : r + RB] += sum(dotnt(tops[j][r : r + RB], w[j]) for j in range(3))

    @pl.when(t == pl.num_programs(0) - 1)
    def _():
        for g in range(gn):
            for s in range(tn):
                cols = slice(s * dt, (s + 1) * dt)
                pay_ref[g, s, 3 * per : rows, :] = ra_ref[g * rg : (g + 1) * rg, cols].astype(bf)
                dx_ref[g, s] = acc_ref[g * lg : (g + 1) * lg, cols].astype(bf)


def tail(x, rel, hot, dattn, dq, dk, dv, dqf, dkf, sums, first, small, first_shift):
    gn, tn, wide, dt = first.shape
    L, D = x.shape
    spans = rel.shape[0]
    rows = 3 * D // gn + spans // gn + small.shape[2]
    bf, f32 = jnp.bfloat16, jnp.float32
    full = lambda shape: spec(shape, lambda t: (0,) * len(shape), True)
    col = lambda: spec((L, dt), lambda t: (0, t))
    return pl.pallas_call(
        functools.partial(tail_kernel, first_shift=first_shift),
        grid=(tn,),
        in_specs=[
            full((L, D)), full((spans, D)), full((2 * L, spans)), full((L, D)),
            col(), col(), col(),
            spec((dt, 2 * L), lambda t: (t, 0)), spec((dt, 2 * L), lambda t: (t, 0)),
            spec((24, dt), lambda t: (0, t)),
            spec((gn, 1, wide, dt), lambda t: (0, t, 0, 0)),
            spec((1,) + small.shape[1:], lambda t: (t, 0, 0, 0)),
        ],
        out_specs=[full((gn, tn, rows, dt)), full((gn, tn, L // gn, dt))],
        out_shape=[
            jax.ShapeDtypeStruct((gn, tn, rows, dt), bf),
            jax.ShapeDtypeStruct((gn, tn, L // gn, dt), bf),
        ],
        scratch_shapes=[pltpu.VMEM((D, L + spans), bf), pltpu.VMEM((L, D), f32), pltpu.VMEM((spans, D), f32)],
        compiler_params=pltpu.CompilerParams(vmem_limit_bytes=56 << 20),
        cost_estimate=pl.CostEstimate(flops=20 * 10**9, bytes_accessed=40 * 10**6, transcendentals=0),
    )(x, rel, hot, dattn, dq, dk, dv, dqf, dkf, sums, first, small)


MESH = pl.DeviceIdType.MESH


def bit_of(place, i):
    return (place // (1 << i)) % 2


def flipped(place, flips):
    for i in flips:
        place = place + (1 << i) * (1 - 2 * bit_of(place, i))
    return place


def subsets(bits):
    out = [()]
    for i in bits:
        out += [s + (i,) for s in out]
    return out


def orders(bits):
    return bits[1:] + bits[:1], bits[:0:-1] + bits[:1]


def greet(tn, gn):
    t, g = lax.axis_index("tensor"), lax.axis_index("dp")
    barrier = pltpu.get_barrier_semaphore()
    bits = list(range(gn.bit_length() - 1))
    for d in range(1, tn):
        pl.semaphore_signal(barrier, inc=1, device_id={"tensor": lax.rem(t + d, tn)}, device_id_type=MESH)
    for i in bits:
        pl.semaphore_signal(barrier, inc=1, device_id={"dp": flipped(g, (i,))}, device_id_type=MESH)
    pl.semaphore_wait(barrier, tn - 1 + len(bits))


def spread(src_ref, out_ref, sems, tn, gn):
    local, send, recv = sems
    t, g = lax.axis_index("tensor"), lax.axis_index("dp")
    bits = list(range(gn.bit_length() - 1))
    own = pltpu.make_async_copy(src_ref, out_ref.at[g, t], local)
    own.start()
    first = []
    for d in range(1, tn):
        c = pltpu.make_async_remote_copy(
            src_ref, out_ref.at[g, t], send.at[d - 1], recv.at[d - 1],
            device_id={"tensor": lax.rem(t + d, tn)}, device_id_type=MESH,
        )
        c.start()
        first.append(c)
    own.wait()
    for c in first:
        c.wait()
    at = tn - 1
    half = tn // 2
    halves = [(0, half), (half, half)]
    plans = orders(bits)
    for step in range(len(bits)):
        copies = []
        for (lo, size), plan in zip(halves, plans):
            for s in subsets(plan[:step]):
                part = out_ref.at[flipped(g, s), pl.ds(lo, size)]
                c = pltpu.make_async_remote_copy(
                    part, part, send.at[at], recv.at[at],
                    device_id={"dp": flipped(g, (plan[step],))}, device_id_type=MESH,
                )
                c.start()
                copies.append(c)
                at += 1
        for c in copies:
            c.wait()


def spread_count(tn, gn):
    return tn - 1 + 2 * (gn - 1)


def gather_kernel(src_ref, out_ref, local, send, recv, *, tn, gn):
    greet(tn, gn)
    spread(src_ref, out_ref, (local, send, recv), tn, gn)


def gather_all(w, tn, gn, number):
    n = spread_count(tn, gn)
    size = w.size * 2
    return pl.pallas_call(
        functools.partial(gather_kernel, tn=tn, gn=gn),
        in_specs=[pl.BlockSpec(memory_space=pl.ANY)],
        out_specs=pl.BlockSpec(memory_space=pl.ANY),
        out_shape=jax.ShapeDtypeStruct((gn, tn) + w.shape, w.dtype),
        scratch_shapes=[pltpu.SemaphoreType.DMA(()), pltpu.SemaphoreType.DMA((n,)), pltpu.SemaphoreType.DMA((n,))],
        compiler_params=pltpu.CompilerParams(collective_id=number, has_side_effects=True),
        cost_estimate=pl.CostEstimate(flops=0, bytes_accessed=size * tn * gn * 8, transcendentals=0),
    )(w)


def reduce_kernel(pay_ref, q_ref, k_ref, v_ref, rel_ref, small_ref, all_ref, acc_ref, rx_ref, rz_ref, rest_ref,
                  local, asend, arecv, bsend, brecv, *, tn, gn, keep):
    t, g = lax.axis_index("tensor"), lax.axis_index("dp")
    bits = list(range(gn.bit_length() - 1))
    f32, bf = jnp.float32, jnp.bfloat16
    greet(tn, gn)
    rest_bits = bits[1:]
    masks = subsets(rest_bits)
    index = {s: n for n, s in enumerate(masks)}
    sends, locals_ = [], []
    for n, s in enumerate(masks):
        c = pltpu.make_async_remote_copy(
            pay_ref.at[flipped(g, (0,) + s)], rx_ref.at[n], bsend.at[n], brecv.at[n],
            device_id={"dp": flipped(g, (0,))}, device_id_type=MESH,
        )
        c.start()
        sends.append(c)
    for n, s in enumerate(masks):
        c = pltpu.make_async_copy(pay_ref.at[flipped(g, s)], acc_ref.at[n], local.at[n])
        c.start()
        locals_.append(c)

    def add(dst, lo, size, src_ref, slot):
        for i in range(size):
            acc_ref[dst, lo + i] = (acc_ref[dst, lo + i].astype(f32) + src_ref[slot, i].astype(f32)).astype(bf)

    half = tn // 2
    for n in range(len(masks)):
        locals_[n].wait()
        sends[n].wait()
        for i in range(tn):
            acc_ref[n, i] = (acc_ref[n, i].astype(f32) + rx_ref[n, i].astype(f32)).astype(bf)
    at = len(masks)
    plans = [rest_bits, rest_bits[::-1]]
    base = 0
    for step in range(len(rest_bits)):
        flight = []
        for lo, plan in zip((0, half), plans):
            bit = plan[step]
            left = [s for s in masks if not any(i in plan[: step + 1] for i in s)]
            for s in left:
                src = tuple(i for i in rest_bits if i in s or i == bit)
                c = pltpu.make_async_remote_copy(
                    acc_ref.at[index[src], pl.ds(lo, half)], rz_ref.at[base], bsend.at[at], brecv.at[at],
                    device_id={"dp": flipped(g, (bit,))}, device_id_type=MESH,
                )
                c.start()
                flight.append((c, index[s], lo, base))
                at += 1
                base += 1
        for c, n, lo, slot in flight:
            c.wait()
            add(n, lo, half, rz_ref, slot)
    flight = []
    for d in range(1, tn):
        to = lax.rem(t + d, tn)
        c = pltpu.make_async_remote_copy(
            acc_ref.at[0, to], rx_ref.at[len(masks), d - 1], bsend.at[at], brecv.at[at],
            device_id={"tensor": to}, device_id_type=MESH,
        )
        c.start()
        flight.append(c)
        at += 1
    total = acc_ref[0, t].astype(f32)
    for d, c in enumerate(flight):
        c.wait()
        total = total + rx_ref[len(masks), d].astype(f32)
    per = keep // 3
    for j, out in enumerate((q_ref, k_ref, v_ref)):
        out[...] = total[j * per : (j + 1) * per]
    rest_ref[...] = total[keep:].astype(bf)
    spread(rest_ref, all_ref, (local.at[len(masks)], asend, arecv), tn, gn)
    dt = q_ref.shape[1]
    rg = rel_ref.shape[0] // gn
    for s in range(tn):
        cols = slice(s * dt, (s + 1) * dt)
        for i in range(gn):
            rel_ref[i * rg : (i + 1) * rg, cols] = all_ref[i, s, :rg].astype(f32)
        small_ref[:, cols] = all_ref[0, s, rg:].astype(f32)


def reduce_all(pay, keep, spans, number):
    gn, tn, rows, dt = pay.shape
    bf, f32 = jnp.bfloat16, jnp.float32
    n = spread_count(tn, gn)
    m = gn // 2
    pieces = 2 * (m - 1)
    count = m + pieces + tn - 1
    dma = lambda k: pltpu.SemaphoreType.DMA((k,))
    return pl.pallas_call(
        functools.partial(reduce_kernel, tn=tn, gn=gn, keep=keep),
        in_specs=[pl.BlockSpec(memory_space=pl.ANY)],
        out_specs=[pl.BlockSpec(memory_space=pltpu.VMEM)] * 5,
        out_shape=[jax.ShapeDtypeStruct((keep // 3, dt), f32)] * 3
        + [
            jax.ShapeDtypeStruct((spans, tn * dt), f32),
            jax.ShapeDtypeStruct((rows - keep - spans // gn, tn * dt), f32),
        ],
        scratch_shapes=[
            pltpu.VMEM((gn, tn, rows - keep, dt), bf),
            pltpu.VMEM((m, tn, rows, dt), bf),
            pltpu.VMEM((m + 1, tn, rows, dt), bf),
            pltpu.VMEM((pieces, tn // 2, rows, dt), bf),
            pltpu.VMEM((rows - keep, dt), bf),
            dma(m + 1), dma(n), dma(n), dma(count), dma(count),
        ],
        compiler_params=pltpu.CompilerParams(collective_id=number, has_side_effects=True, vmem_limit_bytes=40 << 20),
        cost_estimate=pl.CostEstimate(flops=0, bytes_accessed=200 * 10**6, transcendentals=0),
    )(pay)


def shards(
    inputs,
    cotangent,
    lengths,
    dealing,
    buckets,
    rel_embed,
    query_weight,
    key_weight,
    value_weight,
    proj_shifts,
    merge_weight,
    inner_weight,
    hidden_shift,
    outer_weight,
    layer_vectors,
):
    tn = lax.axis_size("tensor")
    gn = lax.axis_size("dp")
    me = lax.axis_index("dp") * tn + lax.axis_index("tensor")
    count, lg, dt = inputs.shape
    L, D = lg * gn, dt * tn
    per = query_weight.shape[0]
    rg = rel_embed.shape[0]
    spans = rg * gn
    assert count == tn * gn
    bf = jnp.bfloat16
    f32 = jnp.float32
    scale = 1.0 / math.sqrt(3.0 * HEAD)
    seq_axes = ("dp", "tensor")
    w_axes = ("tensor", "dp")

    def swap(a):
        return lax.all_to_all(a, seq_axes, split_axis=0, concat_axis=0, tiled=True)

    def gather(w):
        return lax.all_gather(w, w_axes, axis=0, tiled=False).reshape((tn, gn) + w.shape)

    rel_cols = lax.dynamic_slice_in_dim(rel_embed, lax.axis_index("tensor") * dt, dt, 1)
    first = gather_all(
        jnp.concatenate(
            [
                query_weight,
                key_weight,
                value_weight,
                rel_cols,
                proj_shifts,
                hidden_shift.reshape(-1, dt),
                jnp.zeros((1, dt), bf),
            ],
            axis=0,
        ),
        tn,
        gn,
        0,
    )
    xd = swap(inputs).reshape(gn, tn, lg, dt)
    second = gather(jnp.concatenate([inner_weight, outer_weight, merge_weight], axis=1))
    cot = swap(cotangent).reshape(gn, tn, lg, dt)
    biases = first[0, :, 3 * per + rg :].astype(f32)
    shifts = biases[:, :3]
    hidden_bias = biases[:, 3:7].reshape(tn, 1, -1)
    vectors = layer_vectors.astype(f32)
    length = jnp.sum(jnp.where(dealing == me, lengths, 0)).reshape(1)
    places = jnp.concatenate([buckets[::-1], jnp.full((1,), -1, jnp.int32)])[:, None]

    qkv, far, x, rel, hot = project(xd, first, shifts, places, per)
    ctx, probs, inv = attn_fwd(length, qkv, far, scale=scale)
    h1_low, n1, r1, act, slope, y, dffn, sums2 = middle(
        ctx, x, second, hidden_bias, vectors, cot, per
    )
    out = swap(y.reshape(count, lg, dt))
    payload, hidden, dattn, sums1 = ffn_back(dffn, h1_low, n1, r1, act, slope, second, vectors)
    payload, dctx = merge_back(dattn, ctx, second, payload)
    wide_grads = lax.psum_scatter(payload, "dp", scatter_dimension=0, tiled=False)
    dq, dk, dv, dkf, dqf, sums = attn_bwd(probs, qkv, dctx, ctx, inv, far, scale=scale)
    dq, out, wide_grads = lax.optimization_barrier((dq, out, wide_grads))
    wide_grads = lax.psum_scatter(wide_grads, "tensor", scatter_dimension=0, tiled=False)
    ff = hidden.shape[2]
    small = jnp.concatenate(
        [
            jnp.sum(sums1.reshape(3, 8, D), axis=1),
            jnp.sum(sums2.reshape(3, 8, D), axis=1),
            jnp.sum(hidden, axis=1).reshape(-1, D),
        ],
        axis=0,
    )
    first_shift = small.shape[0]
    sr = 16
    small = jnp.pad(small, ((0, sr - first_shift), (0, 0)))
    small = small.reshape(sr, tn, dt).transpose(1, 0, 2)[:, None]
    small = jnp.pad(small, ((0, 0), (0, gn - 1), (0, 0), (0, 0)))
    pay, dx = tail(x, rel, hot, dattn, dq, dk, dv, dqf, dkf, sums, first, small, first_shift)
    grad_in = swap(dx.reshape(count, lg, dt))
    wide_grads = wide_grads.astype(f32)
    query_grad, key_grad, value_grad, rel_grad, rest = reduce_all(pay, 3 * per, spans, 1)
    return (
        out,
        grad_in,
        rel_grad,
        query_grad,
        key_grad,
        value_grad,
        rest[first_shift : first_shift + 3],
        wide_grads[:, 2 * ff :],
        wide_grads[:, :ff],
        rest[6:first_shift].reshape(-1),
        wide_grads[:, ff : 2 * ff],
        rest[:6],
    )


def solution(mesh):
    split = P("dp", "tensor")
    whole = P(None, "dp", "tensor")
    in_specs = (
        whole, whole, P(), P(), P(), P("dp", None), split, split, split, P(None, "tensor"),
        split, split, P("tensor"), split, P(),
    )
    out_specs = (whole, whole, P(), split, split, split, P(), split, split, P(), split, P())
    return jax.shard_map(shards, mesh=mesh, in_specs=in_specs, out_specs=out_specs, check_vma=False)
```

```python
import functools
import math

import jax
import jax.numpy as jnp
from jax import lax
from jax.experimental import pallas as pl
from jax.experimental.pallas import tpu as pltpu
from jax.sharding import PartitionSpec as P

EPSILON = 1e-07
HEAD = 64
B = 128
SR = 16
UN = 8
NT = (((1,), (1,)), ((), ()))


def dotnt(a, b):
    return lax.dot_general(a, b, NT, preferred_element_type=jnp.float32)


def dotnn(a, b):
    return lax.dot_general(a, b, (((1,), (0,)), ((), ())), preferred_element_type=jnp.float32)


def skew(g_ref, a, n, L):
    parts=[]
    nb=L//B
    for a8 in range(a,a+n,8):
        rot=[pltpu.roll(g_ref[a8:a8+8,t*128:t*128+128], 1+a8, 1, stride=1, stride_axis=0) for t in range(nb+1)]
        msk=lax.broadcasted_iota(jnp.int32,(8,128),1) < (1+a8+lax.broadcasted_iota(jnp.int32,(8,128),0))
        parts.append(jnp.concatenate([jnp.where(msk,rot[t],rot[t+1]) for t in range(nb)],axis=1))
    return jnp.concatenate(parts,axis=0)

def fwd_kernel(len_ref, q_ref, k_ref, v_ref, kf_ref, qf_ref, ctx_ref, p_ref, l_ref, t_ref, kx_ref, vx_ref, g0, g1, s0, s1, *, L, scale):
    W = L + B
    nb = L // B
    gs=(g0,g1); ss=(s0,s1)
    lane = lax.broadcasted_iota(jnp.int32, (1, 128), 1)
    length = len_ref[0]
    row = lax.broadcasted_iota(jnp.int32, (L, 128), 0)
    c2 = scale * math.log2(math.e)
    eye = (lax.broadcasted_iota(jnp.int32,(B,B),0)==lax.broadcasted_iota(jnp.int32,(B,B),1)).astype(jnp.bfloat16)
    zero = jnp.zeros((), jnp.bfloat16)
    mine = [lane < 64, lane >= 64]
    first_other = [lane==64, lane==0]
    for h in range(2):
        bias = jnp.where((row >= length) & first_other[h], -1e30, 0.0).astype(jnp.bfloat16)
        kx_ref[h] = jnp.where(mine[h], k_ref[...], bias)
        vx_ref[h] = jnp.where(mine[h], v_ref[...], jnp.ones((), jnp.bfloat16))
    def tblock(b, _):
        r0 = pl.multiple_of(b*B, B)
        base = pl.multiple_of(L - B - b*B, B)
        for h in range(2):
            kb = jnp.where(mine[h], k_ref[pl.ds(r0,B),:], zero)
            gs[h][...] = dotnt(kb, qf_ref[pl.ds(base, W), :])
        for h in range(2):
            for a in range(0, B, SR):
                t_ref[h, pl.ds(r0+a,SR), :] = skew(gs[h], a, SR, L).astype(jnp.bfloat16)
        return 0
    lax.fori_loop(0, nb, tblock, 0, unroll=2)
    def scores(b, h):
        r0 = pl.multiple_of(b*B, B)
        base = pl.multiple_of(L - B - b*B, B)
        qb = q_ref[pl.ds(r0,B),:]
        qm = jnp.where(mine[h], qb, zero)
        qx = jnp.where(mine[h], qb, first_other[h].astype(jnp.bfloat16))
        gs[h][...] = dotnt(qm, kf_ref[pl.ds(base, W), :])
        lhs = jnp.concatenate([qx, eye], axis=1)
        rhs = jnp.concatenate([kx_ref[h], t_ref[h, :, pl.ds(r0,B)]], axis=1)
        ss[h][...] = dotnt(lhs, rhs)
    def soft(b, h):
        r0 = pl.multiple_of(b*B, B)
        tops=[]
        for a in range(0, B, 8):
            s = ss[h][a:a+8] + skew(gs[h], a, 8, L)
            ss[h][a:a+8] = s
            tops.append(functools.reduce(jnp.maximum,[s[:,t*128:t*128+128] for t in range(nb)]))
        m = jnp.max(jnp.concatenate(tops,axis=0), axis=1, keepdims=True) * c2
        for a in range(0, B, SR):
            p_ref[h, pl.ds(r0+a,SR), :] = jnp.exp2(ss[h][a:a+SR]*c2 - m[a:a+SR]).astype(jnp.bfloat16)
    def out(b, h):
        r0 = pl.multiple_of(b*B, B)
        return dotnn(p_ref[h, pl.ds(r0,B), :], vx_ref[h])
    def finish(b, o0, o1):
        r0 = pl.multiple_of(b*B, B)
        num = jnp.where(mine[0], o0, o1)
        den = jnp.where(mine[0], pltpu.roll(o0,64,1), pltpu.roll(o1,64,1))
        inv = 1.0/den
        ctx_ref[pl.ds(r0,B),:] = (num*inv).astype(jnp.bfloat16)
        l_ref[pl.ds(r0,B),:] = inv
    scores(0,0)
    def sblock(b, o0):
        scores(b,1)
        soft(b,0)
        o0 = out(b,0)
        scores(jnp.minimum(b+1,nb-1),0)
        soft(b,1)
        o1 = out(b,1)
        finish(b,o0,o1)
        return 0
    lax.fori_loop(0, nb, sblock, 0, unroll=8)


def attn_fwd(length, qkv, far, *, scale):
    _, L, C = qkv.shape
    part = lambda j, r: pl.BlockSpec((None, r, 128), lambda h, *_: (j, 0, h))
    return pl.pallas_call(
        functools.partial(fwd_kernel, L=L, scale=scale),
        grid_spec=pltpu.PrefetchScalarGridSpec(
            num_scalar_prefetch=1,
            grid=(C // 128,),
            in_specs=[part(0, L), part(1, L), part(2, L), part(1, 2 * L), part(0, 2 * L)],
            out_specs=[
                pl.BlockSpec((L, 128), lambda h, *_: (0, h)),
                pl.BlockSpec((2, L, L), lambda h, *_: (h, 0, 0)),
                pl.BlockSpec((L, 128), lambda h, *_: (0, h)),
            ],
            scratch_shapes=[pltpu.VMEM((2, L, L), jnp.bfloat16)]
            + [pltpu.VMEM((2, L, 128), jnp.bfloat16)] * 2
            + [pltpu.VMEM((B, L + B), jnp.float32)] * 2
            + [pltpu.VMEM((B, L), jnp.float32)] * 2,
        ),
        out_shape=[
            jax.ShapeDtypeStruct((L, C), jnp.bfloat16),
            jax.ShapeDtypeStruct((C // HEAD, L, L), jnp.bfloat16),
            jax.ShapeDtypeStruct((L, C), jnp.float32),
        ],
        compiler_params=pltpu.CompilerParams(vmem_limit_bytes=50 << 20),
        cost_estimate=pl.CostEstimate(flops=80 * 10**9, bytes_accessed=60 * 10**6, transcendentals=0),
    )(length, qkv, qkv, qkv, far, far)


def unskew(x, a8):
    nb = x.shape[1]//B
    sub = lax.broadcasted_iota(jnp.int32,(8,128),0)
    lane = lax.broadcasted_iota(jnp.int32,(8,128),1)
    keep = lane >= (127-a8) - sub
    idx=(lane-(127-a8)+sub)&127
    rot=[jnp.take_along_axis(x[:,t*128:t*128+128], idx, axis=1) for t in range(nb)]
    zero = jnp.zeros((8,128), x.dtype)
    return jnp.concatenate([jnp.where(keep, rot[t] if t<nb else zero, rot[t-1] if t>0 else zero) for t in range(nb+1)], axis=1)

def bwd_kernel(p_ref, q_ref, k_ref, v_ref, do_ref, ctx_ref, li_ref, kf_ref, qf_ref,
               dq_ref, dk_ref, dv_ref, dkf_ref, dqf_ref, sums_ref,
               dox_ref, dot_ref, qt_ref, kt_ref, vx_ref, ds_ref, d0, d1, akf, aqf, *, L, scale):
    W = L + B
    nb = L // B
    dd=(d0,d1)
    lane = lax.broadcasted_iota(jnp.int32, (1, 128), 1)
    mine = [lane < 64, lane >= 64]
    base_lane = [64, 0]
    dos = (do_ref[...].astype(jnp.float32) * li_ref[...]).astype(jnp.bfloat16)
    prod = dos.astype(jnp.float32) * ctx_ref[...].astype(jnp.float32)
    for h in range(2):
        delta = -jnp.sum(jnp.where(mine[h], prod, 0.0), axis=1, keepdims=True)
        hi = delta.astype(jnp.bfloat16).astype(jnp.float32)
        lo = delta - hi
        extra = jnp.where(lane == base_lane[h], hi, jnp.where(lane == base_lane[h]+1, lo, 0.0)).astype(jnp.bfloat16)
        dox_ref[h] = jnp.where(mine[h], dos, extra)
        vx_ref[h] = jnp.where(mine[h], v_ref[...], jnp.ones((), jnp.bfloat16))
    dot_ref[...] = dos.T
    qt_ref[...] = q_ref[...].T
    kt_ref[...] = k_ref[...].T
    akf[...] = jnp.zeros_like(akf)
    aqf[...] = jnp.zeros_like(aqf)
    def iblock(b, sq):
        r0 = pl.multiple_of(b*B, B)
        base = pl.multiple_of(L - B - b*B, B)
        outs=[]
        for h in range(2):
            dp = dotnt(dox_ref[h, pl.ds(r0,B), :], vx_ref[h])
            for a in range(0, B, SR):
                ds = p_ref[h, pl.ds(r0+a,SR), :].astype(jnp.float32) * dp[a:a+SR]
                ds_ref[h, pl.ds(r0+a,SR), :] = ds.astype(jnp.bfloat16)
                dd[h][a:a+SR, :] = jnp.concatenate([unskew(ds[s:s+8], a+s) for s in range(0,SR,8)],axis=0).astype(jnp.bfloat16)
            outs.append(dotnn(ds_ref[h, pl.ds(r0,B), :], k_ref[...]) + dotnn(dd[h][...], kf_ref[pl.ds(base, W), :]))
            akf[h*64:h*64+64, pl.ds(base, W)] += dotnn(qt_ref[h*64:h*64+64, pl.ds(r0,B)], dd[h][...])
        dq = jnp.where(mine[0], outs[0], outs[1]) * scale
        dq_ref[pl.ds(r0,B),:] = dq.astype(jnp.bfloat16)
        return sq + jnp.sum(dq.reshape(B//8,8,128), axis=0)
    sq = lax.fori_loop(0, nb, iblock, jnp.zeros((8,128),jnp.float32), unroll=UN)
    def jblock(b, sk):
        r0 = pl.multiple_of(b*B, B)
        base = pl.multiple_of(L - B - b*B, B)
        outs=[]
        for h in range(2):
            dst = ds_ref[h, :, pl.ds(r0,B)].T
            for a in range(0, B, SR):
                x = dst[a:a+SR].astype(jnp.float32)
                dd[h][a:a+SR, :] = jnp.concatenate([unskew(x[s:s+8], a+s) for s in range(0,SR,8)],axis=0).astype(jnp.bfloat16)
            outs.append(dotnn(dst, q_ref[...]) + dotnn(dd[h][...], qf_ref[pl.ds(base, W), :]))
            aqf[h*64:h*64+64, pl.ds(base, W)] += dotnn(kt_ref[h*64:h*64+64, pl.ds(r0,B)], dd[h][...])
        dk = jnp.where(mine[0], outs[0], outs[1]) * scale
        dk_ref[pl.ds(r0,B),:] = dk.astype(jnp.bfloat16)
        return sk + jnp.sum(dk.reshape(B//8,8,128), axis=0)
    sk = lax.fori_loop(0, nb, jblock, jnp.zeros((8,128),jnp.float32), unroll=UN)
    dvt = jnp.concatenate([dotnn(dot_ref[h*64:h*64+64,:], p_ref[h]) for h in range(2)], axis=0)
    dv = dvt.T
    dv_ref[...] = dv.astype(jnp.bfloat16)
    sv = jnp.sum(dv.reshape(L//8,8,128), axis=0)
    sums_ref[0:8] = sq
    sums_ref[8:16] = sk
    sums_ref[16:24] = sv
    dkf_ref[...] = (akf[...]*scale).astype(jnp.bfloat16)
    dqf_ref[...] = (aqf[...]*scale).astype(jnp.bfloat16)


def attn_bwd(p, qkv, do, ctx, linv, far, *, scale):
    _, L, C = qkv.shape
    bf = jnp.bfloat16
    part = lambda j, r: pl.BlockSpec((None, r, 128), lambda h: (j, 0, h))
    col = lambda r: pl.BlockSpec((r, 128), lambda h: (0, h))
    rowb = pl.BlockSpec((128, 2 * L), lambda h: (h, 0))
    return pl.pallas_call(
        functools.partial(bwd_kernel, L=L, scale=scale),
        grid=(C // 128,),
        in_specs=[pl.BlockSpec((2, L, L), lambda h: (h, 0, 0)), part(0, L), part(1, L), part(2, L)]
        + [col(L)] * 3
        + [part(1, 2 * L), part(0, 2 * L)],
        out_specs=[col(L)] * 3 + [rowb] * 2 + [col(24)],
        scratch_shapes=[pltpu.VMEM((2, L, 128), bf)]
        + [pltpu.VMEM((128, L), bf)] * 3
        + [pltpu.VMEM((2, L, 128), bf), pltpu.VMEM((2, L, L), bf)]
        + [pltpu.VMEM((B, L + B), bf)] * 2
        + [pltpu.VMEM((128, 2 * L), jnp.float32)] * 2,
        out_shape=[jax.ShapeDtypeStruct((L, C), bf)] * 3
        + [jax.ShapeDtypeStruct((C, 2 * L), bf)] * 2
        + [jax.ShapeDtypeStruct((24, C), jnp.float32)],
        compiler_params=pltpu.CompilerParams(vmem_limit_bytes=56 << 20),
        cost_estimate=pl.CostEstimate(flops=120 * 10**9, bytes_accessed=80 * 10**6, transcendentals=0),
    )(p, qkv, qkv, qkv, do, ctx, linv, far, far)


def spec(block, index, once=False):
    if once:
        return pl.BlockSpec(block, index, pipeline_mode=pl.Buffered(1))
    return pl.BlockSpec(block, index)


def norm_rows(z):
    center = z - jnp.mean(z, axis=-1, keepdims=True)
    r = lax.rsqrt(jnp.mean(center * center, axis=-1, keepdims=True) + EPSILON)
    return center * r, r


def norm_back(g, n, r):
    return r * (g - jnp.mean(g, axis=-1, keepdims=True) - n * jnp.mean(g * n, axis=-1, keepdims=True))


def fold8(v):
    return jnp.sum(v.reshape(v.shape[0] // 8, 8, v.shape[1]), axis=0)


def project_kernel(xd_ref, rel4_ref, w_ref, sh_ref, pl_ref, qkv_ref, far_ref, x_ref, rel_ref, hot_ref):
    t, j = pl.program_id(0), pl.program_id(1)
    gn, tn, lg, dt = xd_ref.shape
    spans = rel_ref.shape[0]
    rg = spans // gn

    @pl.when((t == 0) & (j == 0))
    def _():
        for g in range(gn):
            for s in range(tn):
                x_ref[g * lg : (g + 1) * lg, s * dt : (s + 1) * dt] = xd_ref[g, s]
                rel_ref[g * rg : (g + 1) * rg, s * dt : (s + 1) * dt] = rel4_ref[g, s]
        rows = hot_ref.shape[0]
        lanes = lax.broadcasted_iota(jnp.int32, (rows, spans), 1)
        hot_ref[...] = (pl_ref[...] == lanes).astype(jnp.float32).astype(jnp.bfloat16)

    w = w_ref[:, 0].reshape(x_ref.shape[1], dt)
    shift = sh_ref[0, pl.ds(j, 1), :]
    qkv_ref[0] = (dotnn(x_ref[...], w) + shift).astype(jnp.bfloat16)

    @pl.when(j < 2)
    def _():
        place = (dotnn(rel_ref[...], w) + shift).astype(jnp.bfloat16)
        far_ref[0] = dotnn(hot_ref[...], place).astype(jnp.bfloat16)


def project(xd, first, shifts, places, per):
    gn, tn, lg, dt = xd.shape
    L, D = gn * lg, tn * dt
    rg = (first.shape[2] - 3 * per - 8)
    spans = rg * gn
    bf = jnp.bfloat16
    return pl.pallas_call(
        project_kernel,
        grid=(tn, 3),
        in_specs=[
            spec((gn, tn, lg, dt), lambda t, j: (0, 0, 0, 0), True),
            spec((gn, tn, rg, dt), lambda t, j: (0, 0, 3 * per // rg, 0), True),
            spec((gn, 1, per, dt), lambda t, j: (0, t, j, 0)),
            spec((1, 3, dt), lambda t, j: (t, 0, 0)),
            spec((2 * L, 1), lambda t, j: (0, 0), True),
        ],
        out_specs=[
            spec((1, L, dt), lambda t, j: (j, 0, t)),
            spec((1, 2 * L, dt), lambda t, j: (jnp.minimum(j, 1), 0, t)),
            spec((L, D), lambda t, j: (0, 0)),
            spec((spans, D), lambda t, j: (0, 0)),
            spec((2 * L, spans), lambda t, j: (0, 0)),
        ],
        out_shape=[
            jax.ShapeDtypeStruct((3, L, D), bf),
            jax.ShapeDtypeStruct((2, 2 * L, D), bf),
            jax.ShapeDtypeStruct((L, D), bf),
            jax.ShapeDtypeStruct((spans, D), bf),
            jax.ShapeDtypeStruct((2 * L, spans), bf),
        ],
        compiler_params=pltpu.CompilerParams(vmem_limit_bytes=50 << 20),
        cost_estimate=pl.CostEstimate(flops=14 * 10**9, bytes_accessed=30 * 10**6, transcendentals=0),
    )(xd, first, first, shifts, places)


RB = 256


def middle_kernel(ctx_ref, x_ref, wm_ref, wi_ref, wo_ref, hb_ref, vec_ref, cot_ref,
                  hl_ref, n1_ref, r1_ref, act_ref, slope_ref, y_ref, df_ref, sums_ref, acc_ref, h1_ref):
    t = pl.program_id(0)
    L, D = x_ref.shape
    gn, tn, lg, dt = cot_ref.shape
    f32, bf = jnp.float32, jnp.bfloat16

    @pl.when(t == 0)
    def _():
        for r in range(0, L, RB):
            z1 = vec_ref[0:1] + x_ref[r : r + RB].astype(f32)
            for s in range(tn):
                z1 = z1 + dotnt(ctx_ref[r : r + RB, s * dt : (s + 1) * dt], wm_ref[s].reshape(D, dt))
            n1, r1 = norm_rows(z1)
            h1 = n1 * vec_ref[1:2] + vec_ref[2:3]
            h1_ref[r : r + RB] = h1
            hl_ref[r : r + RB] = h1.astype(bf)
            n1_ref[r : r + RB] = n1.astype(bf)
            r1_ref[r : r + RB] = jnp.broadcast_to(r1, (RB, 128))

    wi = wi_ref[0].reshape(D, wi_ref.shape[3])
    wo = wo_ref[0].reshape(D, wo_ref.shape[3])
    for r in range(0, L, RB):
        pre = dotnn(hl_ref[r : r + RB], wi) + hb_ref[0]
        phi = 0.5 + 0.5 * lax.erf(pre * math.sqrt(0.5))
        act = (pre * phi).astype(bf)
        act_ref[r : r + RB] = act
        bell = jnp.exp(-0.5 * pre * pre) * (1.0 / math.sqrt(2.0 * math.pi))
        slope_ref[r : r + RB] = (phi + pre * bell).astype(bf)
        part = dotnt(act, wo)

        @pl.when(t == 0)
        def _():
            acc_ref[r : r + RB] = part

        @pl.when(t > 0)
        def _():
            acc_ref[r : r + RB] += part

    @pl.when(t == pl.num_programs(0) - 1)
    def _():
        s0 = jnp.zeros((8, D), f32)
        s1 = jnp.zeros((8, D), f32)
        s2 = jnp.zeros((8, D), f32)
        for g in range(gn):
            rows = slice(g * lg, (g + 1) * lg)
            z2 = acc_ref[rows] + vec_ref[3:4] + h1_ref[rows]
            n2, r2 = norm_rows(z2)
            y = (n2 * vec_ref[4:5] + vec_ref[5:6]).astype(bf)
            for s in range(tn):
                y_ref[g, s] = y[:, s * dt : (s + 1) * dt]
            dy = jnp.concatenate([cot_ref[g, s] for s in range(tn)], axis=1).astype(f32)
            dz2 = norm_back(dy * vec_ref[4:5], n2, r2)
            df_ref[rows] = dz2.astype(bf)
            s0, s1, s2 = s0 + fold8(dz2), s1 + fold8(dy * n2), s2 + fold8(dy)
        sums_ref[0:8], sums_ref[8:16], sums_ref[16:24] = s0, s1, s2


def middle(ctx, x, second, hidden_bias, vectors, cot, per):
    gn, tn, lg, dt = cot.shape
    L, D = x.shape
    ff = hidden_bias.shape[2]
    bf, f32 = jnp.bfloat16, jnp.float32
    full = lambda shape: spec(shape, lambda t: (0,) * len(shape), True)
    return pl.pallas_call(
        middle_kernel,
        grid=(tn,),
        in_specs=[
            full((L, D)),
            full((L, D)),
            spec((tn, gn, per, dt), lambda t: (0, 0, 0, 2 * ff // dt), True),
            spec((1, gn, per, ff), lambda t: (t, 0, 0, 0)),
            spec((1, gn, per, ff), lambda t: (t, 0, 0, 1)),
            spec((1, 1, ff), lambda t: (t, 0, 0)),
            full((6, D)),
            full((gn, tn, lg, dt)),
        ],
        out_specs=[
            full((L, D)), full((L, D)), full((L, 128)),
            spec((L, ff), lambda t: (0, t)), spec((L, ff), lambda t: (0, t)),
            full((gn, tn, lg, dt)), full((L, D)), full((24, D)),
        ],
        out_shape=[
            jax.ShapeDtypeStruct((L, D), bf),
            jax.ShapeDtypeStruct((L, D), bf),
            jax.ShapeDtypeStruct((L, 128), f32),
            jax.ShapeDtypeStruct((L, tn * ff), bf),
            jax.ShapeDtypeStruct((L, tn * ff), bf),
            jax.ShapeDtypeStruct((gn, tn, lg, dt), bf),
            jax.ShapeDtypeStruct((L, D), bf),
            jax.ShapeDtypeStruct((24, D), f32),
        ],
        scratch_shapes=[pltpu.VMEM((L, D), f32), pltpu.VMEM((L, D), f32)],
        compiler_params=pltpu.CompilerParams(vmem_limit_bytes=58 << 20),
        cost_estimate=pl.CostEstimate(flops=30 * 10**9, bytes_accessed=60 * 10**6, transcendentals=0),
    )(ctx, x, second, second, second, hidden_bias, vectors, cot)


def ffn_back_kernel(df_ref, hl_ref, n1_ref, r1_ref, act_ref, slope_ref, wi_ref, wo_ref, vec_ref,
                    pay_ref, hid_ref, da_ref, sums_ref, dft_ref, hlt_ref, acc_ref, dp_ref):
    t = pl.program_id(0)
    L, D = df_ref.shape
    ff = act_ref.shape[1]
    gn, _, per, _ = pay_ref.shape
    f32, bf = jnp.float32, jnp.bfloat16

    @pl.when(t == 0)
    def _():
        for r in range(0, L, RB):
            dft_ref[:, r : r + RB] = df_ref[r : r + RB].T
            hlt_ref[:, r : r + RB] = hl_ref[r : r + RB].T
            acc_ref[r : r + RB] = df_ref[r : r + RB].astype(f32)

    wi = wi_ref[0].reshape(D, ff)
    wo = wo_ref[0].reshape(D, ff)
    hid = jnp.zeros((8, ff), f32)
    for r in range(0, L, RB):
        dpre = dotnn(df_ref[r : r + RB], wo) * slope_ref[r : r + RB].astype(f32)
        hid = hid + fold8(dpre)
        low = dpre.astype(bf)
        dp_ref[r : r + RB] = low
        acc_ref[r : r + RB] += dotnt(low, wi)
    hid_ref[0] = hid
    for r in range(0, D, RB):
        og = dotnn(dft_ref[r : r + RB], act_ref[...]).astype(bf)
        ig = dotnn(hlt_ref[r : r + RB], dp_ref[...]).astype(bf)
        for c in range(0, RB, per):
            pay_ref[(r + c) // per, 0, :, 0:ff] = ig[c : c + per]
            pay_ref[(r + c) // per, 0, :, ff : 2 * ff] = og[c : c + per]

    @pl.when(t == pl.num_programs(0) - 1)
    def _():
        s0 = jnp.zeros((8, D), f32)
        s1 = jnp.zeros((8, D), f32)
        s2 = jnp.zeros((8, D), f32)
        for r in range(0, L, 128):
            rows = slice(r, r + 128)
            dh1 = acc_ref[rows]
            n1 = n1_ref[rows].astype(f32)
            dz1 = norm_back(dh1 * vec_ref[1:2], n1, r1_ref[rows, 0:1])
            da_ref[rows] = dz1.astype(bf)
            s0, s1, s2 = s0 + fold8(dz1), s1 + fold8(dh1 * n1), s2 + fold8(dh1)
        sums_ref[0:8], sums_ref[8:16], sums_ref[16:24] = s0, s1, s2


def ffn_back(dffn, h1_low, n1, r1, act, slope, second, vectors):
    tn, gn, per, wide = second.shape
    L, D = dffn.shape
    ff = act.shape[1] // tn
    bf, f32 = jnp.bfloat16, jnp.float32
    full = lambda shape: spec(shape, lambda t: (0,) * len(shape), True)
    return pl.pallas_call(
        ffn_back_kernel,
        grid=(tn,),
        in_specs=[
            full((L, D)), full((L, D)), full((L, D)), full((L, 128)),
            spec((L, ff), lambda t: (0, t)), spec((L, ff), lambda t: (0, t)),
            spec((1, gn, per, ff), lambda t: (t, 0, 0, 0)),
            spec((1, gn, per, ff), lambda t: (t, 0, 0, 1)),
            full((6, D)),
        ],
        out_specs=[
            spec((gn, 1, per, 2 * ff), lambda t: (0, t, 0, 0)),
            spec((1, 8, ff), lambda t: (t, 0, 0)),
            full((L, D)), full((24, D)),
        ],
        out_shape=[
            jax.ShapeDtypeStruct((gn, tn, per, wide), bf),
            jax.ShapeDtypeStruct((tn, 8, ff), f32),
            jax.ShapeDtypeStruct((L, D), bf),
            jax.ShapeDtypeStruct((24, D), f32),
        ],
        scratch_shapes=[pltpu.VMEM((D, L), bf), pltpu.VMEM((D, L), bf), pltpu.VMEM((L, D), f32), pltpu.VMEM((L, ff), bf)],
        compiler_params=pltpu.CompilerParams(vmem_limit_bytes=58 << 20),
        cost_estimate=pl.CostEstimate(flops=40 * 10**9, bytes_accessed=80 * 10**6, transcendentals=0),
    )(dffn, h1_low, n1, r1, act, slope, second, second, vectors)


def merge_back_kernel(da_ref, ctx_ref, wm_ref, pay_in, pay_ref, dctx_ref, dat_ref):
    t = pl.program_id(0)
    L, D = da_ref.shape
    gn, _, per, dt = pay_ref.shape

    @pl.when(t == 0)
    def _():
        for r in range(0, L, RB):
            dat_ref[:, r : r + RB] = da_ref[r : r + RB].T

    dctx_ref[...] = dotnn(da_ref[...], wm_ref[0].reshape(D, dt)).astype(jnp.bfloat16)
    pay_ref[:, 0] = dotnn(dat_ref[...], ctx_ref[...]).astype(jnp.bfloat16).reshape(gn, per, dt)


def merge_back(dattn, ctx, second, payload):
    tn, gn, per, wide = second.shape
    L, D = dattn.shape
    dt = D // tn
    last = wide // dt - 1
    bf = jnp.bfloat16
    return pl.pallas_call(
        merge_back_kernel,
        grid=(tn,),
        in_specs=[
            spec((L, D), lambda t: (0, 0), True),
            spec((L, dt), lambda t: (0, t)),
            spec((1, gn, per, dt), lambda t: (t, 0, 0, last)),
            pl.BlockSpec(memory_space=pl.ANY),
        ],
        out_specs=[
            spec((gn, 1, per, dt), lambda t: (0, t, 0, last)),
            spec((L, dt), lambda t: (0, t)),
        ],
        out_shape=[
            jax.ShapeDtypeStruct((gn, tn, per, wide), bf),
            jax.ShapeDtypeStruct((L, D), bf),
        ],
        scratch_shapes=[pltpu.VMEM((D, L), bf)],
        input_output_aliases={3: 0},
        compiler_params=pltpu.CompilerParams(vmem_limit_bytes=50 << 20),
        cost_estimate=pl.CostEstimate(flops=4 * 10**9, bytes_accessed=10 * 10**6, transcendentals=0),
    )(dattn, ctx, second, payload)


def input_back_kernel(da_ref, dq_ref, dk_ref, dv_ref, w_ref, dx_ref, acc_ref):
    t = pl.program_id(0)
    L, D = da_ref.shape
    gn, tn, lg, dt = dx_ref.shape
    per = D // gn

    @pl.when(t == 0)
    def _():
        acc_ref[...] = da_ref[...].astype(jnp.float32)

    w = [w_ref[:, 0, j * per : (j + 1) * per, :].reshape(D, dt) for j in range(3)]
    tops = [dq_ref, dk_ref, dv_ref]
    for r in range(0, L, RB):
        acc_ref[r : r + RB] += sum(dotnt(tops[j][r : r + RB], w[j]) for j in range(3))

    @pl.when(t == pl.num_programs(0) - 1)
    def _():
        for g in range(gn):
            for s in range(tn):
                cols = slice(s * dt, (s + 1) * dt)
                dx_ref[g, s] = acc_ref[g * lg : (g + 1) * lg, cols].astype(jnp.bfloat16)


def input_back(dattn, dq, dk, dv, first):
    gn, tn, wide, dt = first.shape
    L, D = dattn.shape
    col = lambda: spec((L, dt), lambda t: (0, t))
    return pl.pallas_call(
        input_back_kernel,
        grid=(tn,),
        in_specs=[
            spec((L, D), lambda t: (0, 0), True),
            col(), col(), col(),
            spec((gn, 1, wide, dt), lambda t: (0, t, 0, 0)),
        ],
        out_specs=spec((gn, tn, L // gn, dt), lambda t: (0, 0, 0, 0), True),
        out_shape=jax.ShapeDtypeStruct((gn, tn, L // gn, dt), jnp.bfloat16),
        scratch_shapes=[pltpu.VMEM((L, D), jnp.float32)],
        compiler_params=pltpu.CompilerParams(vmem_limit_bytes=50 << 20),
        cost_estimate=pl.CostEstimate(flops=7 * 10**9, bytes_accessed=20 * 10**6, transcendentals=0),
    )(dattn, dq, dk, dv, first)


def tail_kernel(x_ref, rel_ref, hot_ref, dq_ref, dk_ref, dv_ref, dqf_ref, dkf_ref, sm_ref, w_ref, small_ref,
                pay_ref, xt_ref, ra_ref, *, first_shift):
    t = pl.program_id(0)
    L, D = x_ref.shape
    spans = rel_ref.shape[0]
    gn, tn, _, dt = pay_ref.shape
    per = D // gn
    rg = spans // gn
    sr = small_ref.shape[2]
    f32, bf = jnp.float32, jnp.bfloat16

    @pl.when(t == 0)
    def _():
        for r in range(0, L, RB):
            xt_ref[:, r : r + RB] = x_ref[r : r + RB].T
        for r in range(0, spans, RB):
            xt_ref[:, L + r : L + r + RB] = rel_ref[r : r + RB].T
        ra_ref[...] = jnp.zeros_like(ra_ref)

    w = [w_ref[:, 0, j * per : (j + 1) * per, :].reshape(D, dt) for j in range(3)]
    qp = dotnn(dqf_ref[...], hot_ref[...]).T
    kp = dotnn(dkf_ref[...], hot_ref[...]).T
    pos = [qp.astype(bf), kp.astype(bf)]
    tops = [dq_ref, dk_ref, dv_ref]
    rows = 3 * per + rg
    pay_ref[:, t, rows : rows + sr, :] = small_ref[0].astype(bf)
    for j in range(3):
        total = jnp.sum(sm_ref[8 * j : 8 * j + 8], axis=0, keepdims=True)
        if j < 2:
            total = total + jnp.sum((qp, kp)[j], axis=0, keepdims=True)
            both = jnp.concatenate([tops[j][...], pos[j]], axis=0)
            grad = dotnn(xt_ref[...], both)
            ra_ref[...] += dotnt(pos[j], w[j])
        else:
            grad = dotnn(xt_ref[:, 0:L], tops[j][...])
        pay_ref[:, t, j * per : (j + 1) * per, :] = grad.astype(bf).reshape(gn, per, dt)
        at = first_shift + j
        pay_ref[at // sr, t, rows + at % sr : rows + at % sr + 1, :] = total.astype(bf)
    @pl.when(t == pl.num_programs(0) - 1)
    def _():
        for g in range(gn):
            for s in range(tn):
                cols = slice(s * dt, (s + 1) * dt)
                pay_ref[g, s, 3 * per : rows, :] = ra_ref[g * rg : (g + 1) * rg, cols].astype(bf)


def tail(x, rel, hot, dq, dk, dv, dqf, dkf, sums, first, small, first_shift):
    gn, tn, wide, dt = first.shape
    L, D = x.shape
    spans = rel.shape[0]
    rows = 3 * D // gn + spans // gn + small.shape[2]
    bf, f32 = jnp.bfloat16, jnp.float32
    full = lambda shape: spec(shape, lambda t: (0,) * len(shape), True)
    col = lambda: spec((L, dt), lambda t: (0, t))
    return pl.pallas_call(
        functools.partial(tail_kernel, first_shift=first_shift),
        grid=(tn,),
        in_specs=[
            full((L, D)), full((spans, D)), full((2 * L, spans)),
            col(), col(), col(),
            spec((dt, 2 * L), lambda t: (t, 0)), spec((dt, 2 * L), lambda t: (t, 0)),
            spec((24, dt), lambda t: (0, t)),
            spec((gn, 1, wide, dt), lambda t: (0, t, 0, 0)),
            spec((1,) + small.shape[1:], lambda t: (t, 0, 0, 0)),
        ],
        out_specs=full((gn, tn, rows, dt)),
        out_shape=jax.ShapeDtypeStruct((gn, tn, rows, dt), bf),
        scratch_shapes=[pltpu.VMEM((D, L + spans), bf), pltpu.VMEM((spans, D), f32)],
        compiler_params=pltpu.CompilerParams(vmem_limit_bytes=56 << 20),
        cost_estimate=pl.CostEstimate(flops=13 * 10**9, bytes_accessed=40 * 10**6, transcendentals=0),
    )(x, rel, hot, dq, dk, dv, dqf, dkf, sums, first, small)


MESH = pl.DeviceIdType.MESH


def bit_of(place, i):
    return (place // (1 << i)) % 2


def flipped(place, flips):
    for i in flips:
        place = place + (1 << i) * (1 - 2 * bit_of(place, i))
    return place


def subsets(bits):
    out = [()]
    for i in bits:
        out += [s + (i,) for s in out]
    return out


def orders(bits):
    return bits[1:] + bits[:1], bits[:0:-1] + bits[:1]


def greet(tn, gn):
    t, g = lax.axis_index("tensor"), lax.axis_index("dp")
    barrier = pltpu.get_barrier_semaphore()
    bits = list(range(gn.bit_length() - 1))
    for d in range(1, tn):
        pl.semaphore_signal(barrier, inc=1, device_id={"tensor": lax.rem(t + d, tn)}, device_id_type=MESH)
    for i in bits:
        pl.semaphore_signal(barrier, inc=1, device_id={"dp": flipped(g, (i,))}, device_id_type=MESH)
    pl.semaphore_wait(barrier, tn - 1 + len(bits))


def spread(src_ref, out_ref, sems, tn, gn):
    local, send, recv = sems
    t, g = lax.axis_index("tensor"), lax.axis_index("dp")
    bits = list(range(gn.bit_length() - 1))
    own = pltpu.make_async_copy(src_ref, out_ref.at[g, t], local)
    own.start()
    first = []
    for d in range(1, tn):
        c = pltpu.make_async_remote_copy(
            src_ref, out_ref.at[g, t], send.at[d - 1], recv.at[d - 1],
            device_id={"tensor": lax.rem(t + d, tn)}, device_id_type=MESH,
        )
        c.start()
        first.append(c)
    own.wait()
    for c in first:
        c.wait()
    at = tn - 1
    half = tn // 2
    halves = [(0, half), (half, half)]
    plans = orders(bits)
    for step in range(len(bits)):
        copies = []
        for (lo, size), plan in zip(halves, plans):
            for s in subsets(plan[:step]):
                part = out_ref.at[flipped(g, s), pl.ds(lo, size)]
                c = pltpu.make_async_remote_copy(
                    part, part, send.at[at], recv.at[at],
                    device_id={"dp": flipped(g, (plan[step],))}, device_id_type=MESH,
                )
                c.start()
                copies.append(c)
                at += 1
        for c in copies:
            c.wait()


def spread_count(tn, gn):
    return tn - 1 + 2 * (gn - 1)


def gather_kernel(src_ref, out_ref, local, send, recv, *, tn, gn):
    greet(tn, gn)
    spread(src_ref, out_ref, (local, send, recv), tn, gn)


def gather_all(w, tn, gn, number):
    n = spread_count(tn, gn)
    size = w.size * 2
    return pl.pallas_call(
        functools.partial(gather_kernel, tn=tn, gn=gn),
        in_specs=[pl.BlockSpec(memory_space=pl.ANY)],
        out_specs=pl.BlockSpec(memory_space=pl.ANY),
        out_shape=jax.ShapeDtypeStruct((gn, tn) + w.shape, w.dtype),
        scratch_shapes=[pltpu.SemaphoreType.DMA(()), pltpu.SemaphoreType.DMA((n,)), pltpu.SemaphoreType.DMA((n,))],
        compiler_params=pltpu.CompilerParams(collective_id=number, has_side_effects=True),
        cost_estimate=pl.CostEstimate(flops=0, bytes_accessed=size * tn * gn * 8, transcendentals=0),
    )(w)


def reduce_kernel(pay_ref, q_ref, k_ref, v_ref, rel_ref, small_ref, all_ref, acc_ref, rx_ref, rz_ref, rest_ref,
                  local, asend, arecv, bsend, brecv, *, tn, gn, keep):
    t, g = lax.axis_index("tensor"), lax.axis_index("dp")
    bits = list(range(gn.bit_length() - 1))
    f32, bf = jnp.float32, jnp.bfloat16
    greet(tn, gn)
    rest_bits = bits[1:]
    masks = subsets(rest_bits)
    index = {s: n for n, s in enumerate(masks)}
    sends, locals_ = [], []
    for n, s in enumerate(masks):
        c = pltpu.make_async_remote_copy(
            pay_ref.at[flipped(g, (0,) + s)], rx_ref.at[n], bsend.at[n], brecv.at[n],
            device_id={"dp": flipped(g, (0,))}, device_id_type=MESH,
        )
        c.start()
        sends.append(c)
    for n, s in enumerate(masks):
        c = pltpu.make_async_copy(pay_ref.at[flipped(g, s)], acc_ref.at[n], local.at[n])
        c.start()
        locals_.append(c)

    def add(dst, lo, size, src_ref, slot):
        for i in range(size):
            acc_ref[dst, lo + i] = (acc_ref[dst, lo + i].astype(f32) + src_ref[slot, i].astype(f32)).astype(bf)

    half = tn // 2
    for n in range(len(masks)):
        locals_[n].wait()
        sends[n].wait()
        for i in range(tn):
            acc_ref[n, i] = (acc_ref[n, i].astype(f32) + rx_ref[n, i].astype(f32)).astype(bf)
    at = len(masks)
    plans = [rest_bits, rest_bits[::-1]]
    base = 0
    for step in range(len(rest_bits)):
        flight = []
        for lo, plan in zip((0, half), plans):
            bit = plan[step]
            left = [s for s in masks if not any(i in plan[: step + 1] for i in s)]
            for s in left:
                src = tuple(i for i in rest_bits if i in s or i == bit)
                c = pltpu.make_async_remote_copy(
                    acc_ref.at[index[src], pl.ds(lo, half)], rz_ref.at[base], bsend.at[at], brecv.at[at],
                    device_id={"dp": flipped(g, (bit,))}, device_id_type=MESH,
                )
                c.start()
                flight.append((c, index[s], lo, base))
                at += 1
                base += 1
        for c, n, lo, slot in flight:
            c.wait()
            add(n, lo, half, rz_ref, slot)
    flight = []
    for d in range(1, tn):
        to = lax.rem(t + d, tn)
        c = pltpu.make_async_remote_copy(
            acc_ref.at[0, to], rx_ref.at[len(masks), d - 1], bsend.at[at], brecv.at[at],
            device_id={"tensor": to}, device_id_type=MESH,
        )
        c.start()
        flight.append(c)
        at += 1
    total = acc_ref[0, t].astype(f32)
    for d, c in enumerate(flight):
        c.wait()
        total = total + rx_ref[len(masks), d].astype(f32)
    per = keep // 3
    for j, out in enumerate((q_ref, k_ref, v_ref)):
        out[...] = total[j * per : (j + 1) * per]
    rest_ref[...] = total[keep:].astype(bf)
    spread(rest_ref, all_ref, (local.at[len(masks)], asend, arecv), tn, gn)
    dt = q_ref.shape[1]
    rg = rel_ref.shape[0] // gn
    for s in range(tn):
        cols = slice(s * dt, (s + 1) * dt)
        for i in range(gn):
            rel_ref[i * rg : (i + 1) * rg, cols] = all_ref[i, s, :rg].astype(f32)
        small_ref[:, cols] = all_ref[0, s, rg:].astype(f32)


def reduce_all(pay, keep, spans, number):
    gn, tn, rows, dt = pay.shape
    bf, f32 = jnp.bfloat16, jnp.float32
    n = spread_count(tn, gn)
    m = gn // 2
    pieces = 2 * (m - 1)
    count = m + pieces + tn - 1
    dma = lambda k: pltpu.SemaphoreType.DMA((k,))
    return pl.pallas_call(
        functools.partial(reduce_kernel, tn=tn, gn=gn, keep=keep),
        in_specs=[pl.BlockSpec(memory_space=pl.ANY)],
        out_specs=[pl.BlockSpec(memory_space=pltpu.VMEM)] * 5,
        out_shape=[jax.ShapeDtypeStruct((keep // 3, dt), f32)] * 3
        + [
            jax.ShapeDtypeStruct((spans, tn * dt), f32),
            jax.ShapeDtypeStruct((rows - keep - spans // gn, tn * dt), f32),
        ],
        scratch_shapes=[
            pltpu.VMEM((gn, tn, rows - keep, dt), bf),
            pltpu.VMEM((m, tn, rows, dt), bf),
            pltpu.VMEM((m + 1, tn, rows, dt), bf),
            pltpu.VMEM((pieces, tn // 2, rows, dt), bf),
            pltpu.VMEM((rows - keep, dt), bf),
            dma(m + 1), dma(n), dma(n), dma(count), dma(count),
        ],
        compiler_params=pltpu.CompilerParams(collective_id=number, has_side_effects=True, vmem_limit_bytes=40 << 20),
        cost_estimate=pl.CostEstimate(flops=0, bytes_accessed=200 * 10**6, transcendentals=0),
    )(pay)


def shards(
    inputs,
    cotangent,
    lengths,
    dealing,
    buckets,
    rel_embed,
    query_weight,
    key_weight,
    value_weight,
    proj_shifts,
    merge_weight,
    inner_weight,
    hidden_shift,
    outer_weight,
    layer_vectors,
):
    tn = lax.axis_size("tensor")
    gn = lax.axis_size("dp")
    me = lax.axis_index("dp") * tn + lax.axis_index("tensor")
    count, lg, dt = inputs.shape
    L, D = lg * gn, dt * tn
    per = query_weight.shape[0]
    rg = rel_embed.shape[0]
    spans = rg * gn
    assert count == tn * gn
    bf = jnp.bfloat16
    f32 = jnp.float32
    scale = 1.0 / math.sqrt(3.0 * HEAD)
    seq_axes = ("dp", "tensor")
    w_axes = ("tensor", "dp")

    def swap(a):
        return lax.all_to_all(a, seq_axes, split_axis=0, concat_axis=0, tiled=True)

    def gather(w):
        return lax.all_gather(w, w_axes, axis=0, tiled=False).reshape((tn, gn) + w.shape)

    rel_cols = lax.dynamic_slice_in_dim(rel_embed, lax.axis_index("tensor") * dt, dt, 1)
    first = gather_all(
        jnp.concatenate(
            [
                query_weight,
                key_weight,
                value_weight,
                rel_cols,
                proj_shifts,
                hidden_shift.reshape(-1, dt),
                jnp.zeros((1, dt), bf),
            ],
            axis=0,
        ),
        tn,
        gn,
        0,
    )
    xd = swap(inputs).reshape(gn, tn, lg, dt)
    wide = jnp.concatenate([inner_weight, outer_weight, merge_weight], axis=1)
    first, xd, wide, cotangent = lax.optimization_barrier((first, xd, wide, cotangent))
    second = gather(wide)
    cot = swap(cotangent).reshape(gn, tn, lg, dt)
    biases = first[0, :, 3 * per + rg :].astype(f32)
    shifts = biases[:, :3]
    hidden_bias = biases[:, 3:7].reshape(tn, 1, -1)
    vectors = layer_vectors.astype(f32)
    length = jnp.sum(jnp.where(dealing == me, lengths, 0)).reshape(1)
    places = jnp.concatenate([buckets[::-1], jnp.full((1,), -1, jnp.int32)])[:, None]

    qkv, far, x, rel, hot = project(xd, first, shifts, places, per)
    ctx, probs, inv = attn_fwd(length, qkv, far, scale=scale)
    h1_low, n1, r1, act, slope, y, dffn, sums2 = middle(
        ctx, x, second, hidden_bias, vectors, cot, per
    )
    out = swap(y.reshape(count, lg, dt))
    payload, hidden, dattn, sums1 = ffn_back(dffn, h1_low, n1, r1, act, slope, second, vectors)
    payload, dctx = merge_back(dattn, ctx, second, payload)
    wide_grads = lax.psum_scatter(payload, "dp", scatter_dimension=0, tiled=False)
    dq, dk, dv, dkf, dqf, sums = attn_bwd(probs, qkv, dctx, ctx, inv, far, scale=scale)
    dq, out, wide_grads = lax.optimization_barrier((dq, out, wide_grads))
    wide_grads = lax.psum_scatter(wide_grads, "tensor", scatter_dimension=0, tiled=False)
    ff = hidden.shape[2]
    small = jnp.concatenate(
        [
            jnp.sum(sums1.reshape(3, 8, D), axis=1),
            jnp.sum(sums2.reshape(3, 8, D), axis=1),
            jnp.sum(hidden, axis=1).reshape(-1, D),
        ],
        axis=0,
    )
    first_shift = small.shape[0]
    sr = 16
    small = jnp.pad(small, ((0, sr - first_shift), (0, 0)))
    small = small.reshape(sr, tn, dt).transpose(1, 0, 2)[:, None]
    small = jnp.pad(small, ((0, 0), (0, gn - 1), (0, 0), (0, 0)))
    dx = input_back(dattn, dq, dk, dv, first)
    dx, dq = lax.optimization_barrier((dx, dq))
    pay = tail(x, rel, hot, dq, dk, dv, dqf, dkf, sums, first, small, first_shift)
    grad_in = swap(dx.reshape(count, lg, dt))
    wide_grads = wide_grads.astype(f32)
    query_grad, key_grad, value_grad, rel_grad, rest = reduce_all(pay, 3 * per, spans, 1)
    return (
        out,
        grad_in,
        rel_grad,
        query_grad,
        key_grad,
        value_grad,
        rest[first_shift : first_shift + 3],
        wide_grads[:, 2 * ff :],
        wide_grads[:, :ff],
        rest[6:first_shift].reshape(-1),
        wide_grads[:, ff : 2 * ff],
        rest[:6],
    )


def solution(mesh):
    split = P("dp", "tensor")
    whole = P(None, "dp", "tensor")
    in_specs = (
        whole, whole, P(), P(), P(), P("dp", None), split, split, split, P(None, "tensor"),
        split, split, P("tensor"), split, P(),
    )
    out_specs = (whole, whole, P(), split, split, split, P(), split, split, P(), split, P())
    return jax.shard_map(shards, mesh=mesh, in_specs=in_specs, out_specs=out_specs, check_vma=False)
```

```python
import functools
import math

import jax
import jax.numpy as jnp
from jax import lax
from jax.experimental import pallas as pl
from jax.experimental.pallas import tpu as pltpu
from jax.sharding import PartitionSpec as P

EPSILON = 1e-07
HEAD = 64
B = 128
SR = 16
UN = 8
NT = (((1,), (1,)), ((), ()))


def dotnt(a, b):
    return lax.dot_general(a, b, NT, preferred_element_type=jnp.float32)


def dotnn(a, b):
    return lax.dot_general(a, b, (((1,), (0,)), ((), ())), preferred_element_type=jnp.float32)


def skew(g_ref, a, n, L):
    parts=[]
    nb=L//B
    for a8 in range(a,a+n,8):
        rot=[pltpu.roll(g_ref[a8:a8+8,t*128:t*128+128], 1+a8, 1, stride=1, stride_axis=0) for t in range(nb+1)]
        msk=lax.broadcasted_iota(jnp.int32,(8,128),1) < (1+a8+lax.broadcasted_iota(jnp.int32,(8,128),0))
        parts.append(jnp.concatenate([jnp.where(msk,rot[t],rot[t+1]) for t in range(nb)],axis=1))
    return jnp.concatenate(parts,axis=0)

def fwd_kernel(len_ref, q_ref, k_ref, v_ref, kf_ref, qf_ref, ctx_ref, p_ref, l_ref, t_ref, kx_ref, vx_ref, g0, g1, s0, s1, *, L, scale):
    W = L + B
    nb = L // B
    gs=(g0,g1); ss=(s0,s1)
    lane = lax.broadcasted_iota(jnp.int32, (1, 128), 1)
    length = len_ref[0]
    row = lax.broadcasted_iota(jnp.int32, (L, 128), 0)
    c2 = scale * math.log2(math.e)
    eye = (lax.broadcasted_iota(jnp.int32,(B,B),0)==lax.broadcasted_iota(jnp.int32,(B,B),1)).astype(jnp.bfloat16)
    zero = jnp.zeros((), jnp.bfloat16)
    mine = [lane < 64, lane >= 64]
    first_other = [lane==64, lane==0]
    for h in range(2):
        bias = jnp.where((row >= length) & first_other[h], -1e30, 0.0).astype(jnp.bfloat16)
        kx_ref[h] = jnp.where(mine[h], k_ref[...], bias)
        vx_ref[h] = jnp.where(mine[h], v_ref[...], jnp.ones((), jnp.bfloat16))
    def tblock(b, _):
        r0 = pl.multiple_of(b*B, B)
        base = pl.multiple_of(L - B - b*B, B)
        for h in range(2):
            kb = jnp.where(mine[h], k_ref[pl.ds(r0,B),:], zero)
            gs[h][...] = dotnt(kb, qf_ref[pl.ds(base, W), :])
        for h in range(2):
            for a in range(0, B, SR):
                t_ref[h, pl.ds(r0+a,SR), :] = skew(gs[h], a, SR, L).astype(jnp.bfloat16)
        return 0
    lax.fori_loop(0, nb, tblock, 0, unroll=2)
    def scores(b, h):
        r0 = pl.multiple_of(b*B, B)
        base = pl.multiple_of(L - B - b*B, B)
        qb = q_ref[pl.ds(r0,B),:]
        qm = jnp.where(mine[h], qb, zero)
        qx = jnp.where(mine[h], qb, first_other[h].astype(jnp.bfloat16))
        gs[h][...] = dotnt(qm, kf_ref[pl.ds(base, W), :])
        lhs = jnp.concatenate([qx, eye], axis=1)
        rhs = jnp.concatenate([kx_ref[h], t_ref[h, :, pl.ds(r0,B)]], axis=1)
        ss[h][...] = dotnt(lhs, rhs)
    def soft(b, h):
        r0 = pl.multiple_of(b*B, B)
        tops=[]
        for a in range(0, B, 8):
            s = ss[h][a:a+8] + skew(gs[h], a, 8, L)
            ss[h][a:a+8] = s
            tops.append(functools.reduce(jnp.maximum,[s[:,t*128:t*128+128] for t in range(nb)]))
        m = jnp.max(jnp.concatenate(tops,axis=0), axis=1, keepdims=True) * c2
        for a in range(0, B, SR):
            p_ref[h, pl.ds(r0+a,SR), :] = jnp.exp2(ss[h][a:a+SR]*c2 - m[a:a+SR]).astype(jnp.bfloat16)
    def out(b, h):
        r0 = pl.multiple_of(b*B, B)
        return dotnn(p_ref[h, pl.ds(r0,B), :], vx_ref[h])
    def finish(b, o0, o1):
        r0 = pl.multiple_of(b*B, B)
        num = jnp.where(mine[0], o0, o1)
        den = jnp.where(mine[0], pltpu.roll(o0,64,1), pltpu.roll(o1,64,1))
        inv = 1.0/den
        ctx_ref[pl.ds(r0,B),:] = (num*inv).astype(jnp.bfloat16)
        l_ref[pl.ds(r0,B),:] = inv
    scores(0,0)
    def sblock(b, o0):
        scores(b,1)
        soft(b,0)
        o0 = out(b,0)
        scores(jnp.minimum(b+1,nb-1),0)
        soft(b,1)
        o1 = out(b,1)
        finish(b,o0,o1)
        return 0
    lax.fori_loop(0, nb, sblock, 0, unroll=8)


def attn_fwd(length, qkv, far, *, scale):
    _, L, C = qkv.shape
    part = lambda j, r: pl.BlockSpec((None, r, 128), lambda h, *_: (j, 0, h))
    return pl.pallas_call(
        functools.partial(fwd_kernel, L=L, scale=scale),
        grid_spec=pltpu.PrefetchScalarGridSpec(
            num_scalar_prefetch=1,
            grid=(C // 128,),
            in_specs=[part(0, L), part(1, L), part(2, L), part(1, 2 * L), part(0, 2 * L)],
            out_specs=[
                pl.BlockSpec((L, 128), lambda h, *_: (0, h)),
                pl.BlockSpec((2, L, L), lambda h, *_: (h, 0, 0)),
                pl.BlockSpec((L, 128), lambda h, *_: (0, h)),
            ],
            scratch_shapes=[pltpu.VMEM((2, L, L), jnp.bfloat16)]
            + [pltpu.VMEM((2, L, 128), jnp.bfloat16)] * 2
            + [pltpu.VMEM((B, L + B), jnp.float32)] * 2
            + [pltpu.VMEM((B, L), jnp.float32)] * 2,
        ),
        out_shape=[
            jax.ShapeDtypeStruct((L, C), jnp.bfloat16),
            jax.ShapeDtypeStruct((C // HEAD, L, L), jnp.bfloat16),
            jax.ShapeDtypeStruct((L, C), jnp.float32),
        ],
        compiler_params=pltpu.CompilerParams(vmem_limit_bytes=50 << 20),
        cost_estimate=pl.CostEstimate(flops=80 * 10**9, bytes_accessed=60 * 10**6, transcendentals=0),
    )(length, qkv, qkv, qkv, far, far)


def unskew(x, a8):
    nb = x.shape[1]//B
    sub = lax.broadcasted_iota(jnp.int32,(8,128),0)
    lane = lax.broadcasted_iota(jnp.int32,(8,128),1)
    keep = lane >= (127-a8) - sub
    idx=(lane-(127-a8)+sub)&127
    rot=[jnp.take_along_axis(x[:,t*128:t*128+128], idx, axis=1) for t in range(nb)]
    zero = jnp.zeros((8,128), x.dtype)
    return jnp.concatenate([jnp.where(keep, rot[t] if t<nb else zero, rot[t-1] if t>0 else zero) for t in range(nb+1)], axis=1)

def bwd_kernel(p_ref, q_ref, k_ref, v_ref, do_ref, ctx_ref, li_ref, kf_ref, qf_ref,
               dq_ref, dk_ref, dv_ref, dkf_ref, dqf_ref, sums_ref,
               dox_ref, dot_ref, qt_ref, kt_ref, vx_ref, ds_ref, d0, d1, akf, aqf, *, L, scale):
    W = L + B
    nb = L // B
    dd=(d0,d1)
    lane = lax.broadcasted_iota(jnp.int32, (1, 128), 1)
    mine = [lane < 64, lane >= 64]
    base_lane = [64, 0]
    dos = (do_ref[...].astype(jnp.float32) * li_ref[...]).astype(jnp.bfloat16)
    prod = dos.astype(jnp.float32) * ctx_ref[...].astype(jnp.float32)
    for h in range(2):
        delta = -jnp.sum(jnp.where(mine[h], prod, 0.0), axis=1, keepdims=True)
        hi = delta.astype(jnp.bfloat16).astype(jnp.float32)
        lo = delta - hi
        extra = jnp.where(lane == base_lane[h], hi, jnp.where(lane == base_lane[h]+1, lo, 0.0)).astype(jnp.bfloat16)
        dox_ref[h] = jnp.where(mine[h], dos, extra)
        vx_ref[h] = jnp.where(mine[h], v_ref[...], jnp.ones((), jnp.bfloat16))
    dot_ref[...] = dos.T
    qt_ref[...] = q_ref[...].T
    kt_ref[...] = k_ref[...].T
    akf[...] = jnp.zeros_like(akf)
    aqf[...] = jnp.zeros_like(aqf)
    def iblock(b, sq):
        r0 = pl.multiple_of(b*B, B)
        base = pl.multiple_of(L - B - b*B, B)
        outs=[]
        for h in range(2):
            dp = dotnt(dox_ref[h, pl.ds(r0,B), :], vx_ref[h])
            for a in range(0, B, SR):
                ds = p_ref[h, pl.ds(r0+a,SR), :].astype(jnp.float32) * dp[a:a+SR]
                ds_ref[h, pl.ds(r0+a,SR), :] = ds.astype(jnp.bfloat16)
                dd[h][a:a+SR, :] = jnp.concatenate([unskew(ds[s:s+8], a+s) for s in range(0,SR,8)],axis=0).astype(jnp.bfloat16)
            outs.append(dotnn(ds_ref[h, pl.ds(r0,B), :], k_ref[...]) + dotnn(dd[h][...], kf_ref[pl.ds(base, W), :]))
            akf[h*64:h*64+64, pl.ds(base, W)] += dotnn(qt_ref[h*64:h*64+64, pl.ds(r0,B)], dd[h][...])
        dq = jnp.where(mine[0], outs[0], outs[1]) * scale
        dq_ref[pl.ds(r0,B),:] = dq.astype(jnp.bfloat16)
        return sq + jnp.sum(dq.reshape(B//8,8,128), axis=0)
    sq = lax.fori_loop(0, nb, iblock, jnp.zeros((8,128),jnp.float32), unroll=UN)
    def jblock(b, sk):
        r0 = pl.multiple_of(b*B, B)
        base = pl.multiple_of(L - B - b*B, B)
        outs=[]
        for h in range(2):
            dst = ds_ref[h, :, pl.ds(r0,B)].T
            for a in range(0, B, SR):
                x = dst[a:a+SR].astype(jnp.float32)
                dd[h][a:a+SR, :] = jnp.concatenate([unskew(x[s:s+8], a+s) for s in range(0,SR,8)],axis=0).astype(jnp.bfloat16)
            outs.append(dotnn(dst, q_ref[...]) + dotnn(dd[h][...], qf_ref[pl.ds(base, W), :]))
            aqf[h*64:h*64+64, pl.ds(base, W)] += dotnn(kt_ref[h*64:h*64+64, pl.ds(r0,B)], dd[h][...])
        dk = jnp.where(mine[0], outs[0], outs[1]) * scale
        dk_ref[pl.ds(r0,B),:] = dk.astype(jnp.bfloat16)
        return sk + jnp.sum(dk.reshape(B//8,8,128), axis=0)
    sk = lax.fori_loop(0, nb, jblock, jnp.zeros((8,128),jnp.float32), unroll=UN)
    dvt = jnp.concatenate([dotnn(dot_ref[h*64:h*64+64,:], p_ref[h]) for h in range(2)], axis=0)
    dv = dvt.T
    dv_ref[...] = dv.astype(jnp.bfloat16)
    sv = jnp.sum(dv.reshape(L//8,8,128), axis=0)
    sums_ref[0:8] = sq
    sums_ref[8:16] = sk
    sums_ref[16:24] = sv
    dkf_ref[...] = (akf[...]*scale).astype(jnp.bfloat16)
    dqf_ref[...] = (aqf[...]*scale).astype(jnp.bfloat16)


def attn_bwd(p, qkv, do, ctx, linv, far, *, scale):
    _, L, C = qkv.shape
    bf = jnp.bfloat16
    part = lambda j, r: pl.BlockSpec((None, r, 128), lambda h: (j, 0, h))
    col = lambda r: pl.BlockSpec((r, 128), lambda h: (0, h))
    rowb = pl.BlockSpec((128, 2 * L), lambda h: (h, 0))
    return pl.pallas_call(
        functools.partial(bwd_kernel, L=L, scale=scale),
        grid=(C // 128,),
        in_specs=[pl.BlockSpec((2, L, L), lambda h: (h, 0, 0)), part(0, L), part(1, L), part(2, L)]
        + [col(L)] * 3
        + [part(1, 2 * L), part(0, 2 * L)],
        out_specs=[col(L)] * 3 + [rowb] * 2 + [col(24)],
        scratch_shapes=[pltpu.VMEM((2, L, 128), bf)]
        + [pltpu.VMEM((128, L), bf)] * 3
        + [pltpu.VMEM((2, L, 128), bf), pltpu.VMEM((2, L, L), bf)]
        + [pltpu.VMEM((B, L + B), bf)] * 2
        + [pltpu.VMEM((128, 2 * L), jnp.float32)] * 2,
        out_shape=[jax.ShapeDtypeStruct((L, C), bf)] * 3
        + [jax.ShapeDtypeStruct((C, 2 * L), bf)] * 2
        + [jax.ShapeDtypeStruct((24, C), jnp.float32)],
        compiler_params=pltpu.CompilerParams(vmem_limit_bytes=56 << 20),
        cost_estimate=pl.CostEstimate(flops=120 * 10**9, bytes_accessed=80 * 10**6, transcendentals=0),
    )(p, qkv, qkv, qkv, do, ctx, linv, far, far)


def spec(block, index, once=False):
    if once:
        return pl.BlockSpec(block, index, pipeline_mode=pl.Buffered(1))
    return pl.BlockSpec(block, index)


def norm_rows(z):
    center = z - jnp.mean(z, axis=-1, keepdims=True)
    r = lax.rsqrt(jnp.mean(center * center, axis=-1, keepdims=True) + EPSILON)
    return center * r, r


def norm_back(g, n, r):
    return r * (g - jnp.mean(g, axis=-1, keepdims=True) - n * jnp.mean(g * n, axis=-1, keepdims=True))


def fold8(v):
    return jnp.sum(v.reshape(v.shape[0] // 8, 8, v.shape[1]), axis=0)


def project_kernel(xd_ref, rel4_ref, wa_ref, wb_ref, sh_ref, pl_ref, qkv_ref, far_ref, x_ref, rel_ref, hot_ref):
    t, j = pl.program_id(0), pl.program_id(1)
    gn, tn, lg, dt = xd_ref.shape
    spans = rel_ref.shape[0]
    rg = spans // gn

    @pl.when((t == 0) & (j == 0))
    def _():
        for g in range(gn):
            for s in range(tn):
                x_ref[g * lg : (g + 1) * lg, s * dt : (s + 1) * dt] = xd_ref[g, s]
                rel_ref[g * rg : (g + 1) * rg, s * dt : (s + 1) * dt] = rel4_ref[g, s]
        rows = hot_ref.shape[0]
        lanes = lax.broadcasted_iota(jnp.int32, (rows, spans), 1)
        hot_ref[...] = (pl_ref[...] == lanes).astype(jnp.float32).astype(jnp.bfloat16)

    w = jnp.where(j < 2, wa_ref[:, 0], wb_ref[:, 0]).reshape(x_ref.shape[1], dt)
    shift = sh_ref[0, pl.ds(j, 1), :]
    qkv_ref[0] = (dotnn(x_ref[...], w) + shift).astype(jnp.bfloat16)

    @pl.when(j < 2)
    def _():
        place = (dotnn(rel_ref[...], w) + shift).astype(jnp.bfloat16)
        far_ref[0] = dotnn(hot_ref[...], place).astype(jnp.bfloat16)


def project(xd, first, later, shifts, places, per):
    gn, tn, lg, dt = xd.shape
    L, D = gn * lg, tn * dt
    rg = later.shape[2] - per - 8
    spans = rg * gn
    bf = jnp.bfloat16
    return pl.pallas_call(
        project_kernel,
        grid=(tn, 3),
        in_specs=[
            spec((gn, tn, lg, dt), lambda t, j: (0, 0, 0, 0), True),
            spec((gn, tn, rg, dt), lambda t, j: (0, 0, per // rg, 0), True),
            spec((gn, 1, per, dt), lambda t, j: (0, t, jnp.minimum(j, 1), 0)),
            spec((gn, 1, per, dt), lambda t, j: (0, t, 0, 0)),
            spec((1, 3, dt), lambda t, j: (t, 0, 0)),
            spec((2 * L, 1), lambda t, j: (0, 0), True),
        ],
        out_specs=[
            spec((1, L, dt), lambda t, j: (j, 0, t)),
            spec((1, 2 * L, dt), lambda t, j: (jnp.minimum(j, 1), 0, t)),
            spec((L, D), lambda t, j: (0, 0)),
            spec((spans, D), lambda t, j: (0, 0)),
            spec((2 * L, spans), lambda t, j: (0, 0)),
        ],
        out_shape=[
            jax.ShapeDtypeStruct((3, L, D), bf),
            jax.ShapeDtypeStruct((2, 2 * L, D), bf),
            jax.ShapeDtypeStruct((L, D), bf),
            jax.ShapeDtypeStruct((spans, D), bf),
            jax.ShapeDtypeStruct((2 * L, spans), bf),
        ],
        compiler_params=pltpu.CompilerParams(vmem_limit_bytes=50 << 20),
        cost_estimate=pl.CostEstimate(flops=14 * 10**9, bytes_accessed=30 * 10**6, transcendentals=0),
    )(xd, later, first, later, shifts, places)


RB = 256


MB = 256


def middle_kernel(ctx_ref, x_ref, wm_ref, wi_ref, wo_ref, hb_ref, vec_ref, cot_ref,
                  y_ref, pay_ref, hid_ref, da_ref, sums_ref,
                  act_ref, slope_ref, hl_ref, hlt_ref, r1_ref, df_ref, acc_ref, sem):
    step = pl.program_id(0)
    L, D = x_ref.shape
    gn, tn, lg, dt = cot_ref.shape
    _, _, per, ff = wi_ref.shape[0], 0, wi_ref.shape[2], wi_ref.shape[3]
    f32, bf = jnp.float32, jnp.bfloat16

    slots = D // ff

    @pl.when(step == 0)
    def _():
        copies = []
        for n, src in enumerate((ctx_ref, x_ref)):
            for u in range(slots):
                at = n * slots + u
                c = pltpu.make_async_copy(src.at[:, pl.ds(u * ff, ff)], slope_ref.at[1 + at], sem.at[at])
                c.start()
                copies.append(c)
        for c in copies:
            c.wait()
        for r in range(0, L, MB):
            rows = slice(r, r + MB)
            z1 = jnp.concatenate([slope_ref[1 + slots + u, rows] for u in range(slots)], axis=1)
            z1 = vec_ref[0:1] + z1.astype(f32)
            for s in range(tn):
                at = s * dt % ff
                part = slope_ref[1 + s * dt // ff, rows, at : at + dt]
                z1 = z1 + dotnt(part, wm_ref[s].reshape(D, dt))
            n1, r1 = norm_rows(z1)
            h1 = n1 * vec_ref[1:2] + vec_ref[2:3]
            low = h1.astype(bf)
            acc_ref[rows] = h1 + vec_ref[3:4]
            hl_ref[rows] = low
            hlt_ref[:, rows] = low.T
            da_ref[rows] = n1.astype(bf)
            high = r1.astype(bf).astype(f32)
            first_lane = lax.broadcasted_iota(jnp.int32, (MB, 128), 1) == 0
            r1_ref[rows] = jnp.where(first_lane, high, r1 - high).astype(bf)

    @pl.when(step < tn)
    def _():
        for r in range(0, L, MB):
            rows = slice(r, r + MB)
            pre = dotnn(hl_ref[rows], wi_ref[0].reshape(D, ff)) + hb_ref[0]
            phi = 0.5 + 0.5 * lax.erf(pre * math.sqrt(0.5))
            act = (pre * phi).astype(bf)
            act_ref[step, rows] = act
            bell = jnp.exp(-0.5 * pre * pre) * (1.0 / math.sqrt(2.0 * math.pi))
            slope_ref[step, rows] = (phi + pre * bell).astype(bf)
            acc_ref[rows] += dotnt(act, wo_ref[0].reshape(D, ff))

    @pl.when(step == tn - 1)
    def _():
        s0 = jnp.zeros((8, D), f32)
        s1 = jnp.zeros((8, D), f32)
        s2 = jnp.zeros((8, D), f32)
        for g in range(gn):
            rows = slice(g * lg, (g + 1) * lg)
            n2, r2 = norm_rows(acc_ref[rows])
            y = (n2 * vec_ref[4:5] + vec_ref[5:6]).astype(bf)
            for s in range(tn):
                y_ref[g, s] = y[:, s * dt : (s + 1) * dt]
            dy = jnp.concatenate([cot_ref[g, s] for s in range(tn)], axis=1).astype(f32)
            dz2 = norm_back(dy * vec_ref[4:5], n2, r2)
            df_ref[rows] = dz2.astype(bf)
            acc_ref[rows] = dz2
            s0, s1, s2 = s0 + fold8(dz2), s1 + fold8(dy * n2), s2 + fold8(dy)
        sums_ref[24:32], sums_ref[32:40], sums_ref[40:48] = s0, s1, s2
        for r in range(0, L, RB):
            hl_ref[:, r : r + RB] = df_ref[r : r + RB].T

    @pl.when(step >= tn)
    def _():
        t = 2 * tn - 1 - step
        hid = jnp.zeros((8, ff), f32)
        for r in range(0, L, MB):
            rows = slice(r, r + MB)
            dpre = dotnn(df_ref[rows], wo_ref[0].reshape(D, ff)) * slope_ref[t, rows].astype(f32)
            hid = hid + fold8(dpre)
            low = dpre.astype(bf)
            slope_ref[t, rows] = low
            acc_ref[rows] += dotnt(low, wi_ref[0].reshape(D, ff))
        hid_ref[0] = hid
        for r in range(0, D, RB):
            og = dotnn(hl_ref[r : r + RB], act_ref[t]).astype(bf)
            ig = dotnn(hlt_ref[r : r + RB], slope_ref[t]).astype(bf)
            for c in range(0, RB, per):
                pay_ref[(r + c) // per, 0, :, 0:ff] = ig[c : c + per]
                pay_ref[(r + c) // per, 0, :, ff : 2 * ff] = og[c : c + per]

    @pl.when(step == 2 * tn - 1)
    def _():
        s0 = jnp.zeros((8, D), f32)
        s1 = jnp.zeros((8, D), f32)
        s2 = jnp.zeros((8, D), f32)
        for r in range(0, L, 128):
            rows = slice(r, r + 128)
            dh1 = acc_ref[rows]
            n1 = da_ref[rows].astype(f32)
            r1 = r1_ref[rows, 0:1].astype(f32) + r1_ref[rows, 1:2].astype(f32)
            dz1 = norm_back(dh1 * vec_ref[1:2], n1, r1)
            da_ref[rows] = dz1.astype(bf)
            s0, s1, s2 = s0 + fold8(dz1), s1 + fold8(dh1 * n1), s2 + fold8(dh1)
        sums_ref[0:8], sums_ref[8:16], sums_ref[16:24] = s0, s1, s2


def middle(ctx, x, second, hidden_bias, vectors, cot):
    gn, tn, lg, dt = cot.shape
    per, wide = second.shape[2:]
    L, D = x.shape
    assert L == D
    ff = hidden_bias.shape[2]
    bf, f32 = jnp.bfloat16, jnp.float32
    full = lambda shape: spec(shape, lambda i: (0,) * len(shape), True)
    place = lambda i: jnp.minimum(i, 2 * tn - 1 - i)
    back = lambda i: jnp.minimum(2 * tn - 1 - i, tn - 1)
    return pl.pallas_call(
        middle_kernel,
        grid=(2 * tn,),
        in_specs=[
            pl.BlockSpec(memory_space=pl.ANY),
            pl.BlockSpec(memory_space=pl.ANY),
            spec((tn, gn, per, dt), lambda i: (0, 0, 0, 2 * ff // dt), True),
            spec((1, gn, per, ff), lambda i: (place(i), 0, 0, 0)),
            spec((1, gn, per, ff), lambda i: (place(i), 0, 0, 1)),
            spec((1, 1, ff), lambda i: (place(i), 0, 0)),
            full((6, D)),
            full((gn, tn, lg, dt)),
        ],
        out_specs=[
            full((gn, tn, lg, dt)),
            spec((gn, 1, per, 2 * ff), lambda i: (0, back(i), 0, 0)),
            spec((1, 8, ff), lambda i: (back(i), 0, 0)),
            full((L, D)),
            full((48, D)),
        ],
        out_shape=[
            jax.ShapeDtypeStruct((gn, tn, lg, dt), bf),
            jax.ShapeDtypeStruct((gn, tn, per, wide), bf),
            jax.ShapeDtypeStruct((tn, 8, ff), f32),
            jax.ShapeDtypeStruct((L, D), bf),
            jax.ShapeDtypeStruct((48, D), f32),
        ],
        scratch_shapes=[
            pltpu.VMEM((tn, L, ff), bf), pltpu.VMEM((tn, L, ff), bf),
            pltpu.VMEM((L, D), bf), pltpu.VMEM((D, L), bf), pltpu.VMEM((L, 128), bf),
            pltpu.VMEM((L, D), bf), pltpu.VMEM((L, D), f32),
            pltpu.SemaphoreType.DMA((2 * (D // ff),)),
        ],
        compiler_params=pltpu.CompilerParams(vmem_limit_bytes=61 << 20),
        cost_estimate=pl.CostEstimate(flops=75 * 10**9, bytes_accessed=100 * 10**6, transcendentals=0),
    )(ctx, x, second, second, second, hidden_bias, vectors, cot)


def merge_back_kernel(da_ref, ctx_ref, wm_ref, pay_in, pay_ref, dctx_ref, dat_ref):
    t = pl.program_id(0)
    L, D = da_ref.shape
    gn, _, per, dt = pay_ref.shape

    @pl.when(t == 0)
    def _():
        for r in range(0, L, RB):
            dat_ref[:, r : r + RB] = da_ref[r : r + RB].T

    dctx_ref[...] = dotnn(da_ref[...], wm_ref[0].reshape(D, dt)).astype(jnp.bfloat16)
    pay_ref[:, 0] = dotnn(dat_ref[...], ctx_ref[...]).astype(jnp.bfloat16).reshape(gn, per, dt)


def merge_back(dattn, ctx, second, payload):
    tn, gn, per, wide = second.shape
    L, D = dattn.shape
    dt = D // tn
    last = wide // dt - 1
    bf = jnp.bfloat16
    return pl.pallas_call(
        merge_back_kernel,
        grid=(tn,),
        in_specs=[
            spec((L, D), lambda t: (0, 0), True),
            spec((L, dt), lambda t: (0, t)),
            spec((1, gn, per, dt), lambda t: (t, 0, 0, last)),
            pl.BlockSpec(memory_space=pl.ANY),
        ],
        out_specs=[
            spec((gn, 1, per, dt), lambda t: (0, t, 0, last)),
            spec((L, dt), lambda t: (0, t)),
        ],
        out_shape=[
            jax.ShapeDtypeStruct((gn, tn, per, wide), bf),
            jax.ShapeDtypeStruct((L, D), bf),
        ],
        scratch_shapes=[pltpu.VMEM((D, L), bf)],
        input_output_aliases={3: 0},
        compiler_params=pltpu.CompilerParams(vmem_limit_bytes=50 << 20),
        cost_estimate=pl.CostEstimate(flops=4 * 10**9, bytes_accessed=10 * 10**6, transcendentals=0),
    )(dattn, ctx, second, payload)


def input_back_kernel(da_ref, dq_ref, dk_ref, dv_ref, wa_ref, wb_ref, dx_ref, acc_ref):
    t = pl.program_id(0)
    L, D = da_ref.shape
    gn, tn, lg, dt = dx_ref.shape
    per = D // gn

    @pl.when(t == 0)
    def _():
        acc_ref[...] = da_ref[...].astype(jnp.float32)

    w = [wa_ref[:, 0, j * per : (j + 1) * per, :].reshape(D, dt) for j in range(2)]
    w.append(wb_ref[:, 0].reshape(D, dt))
    tops = [dq_ref, dk_ref, dv_ref]
    for r in range(0, L, RB):
        acc_ref[r : r + RB] += sum(dotnt(tops[j][r : r + RB], w[j]) for j in range(3))

    @pl.when(t == pl.num_programs(0) - 1)
    def _():
        for g in range(gn):
            for s in range(tn):
                cols = slice(s * dt, (s + 1) * dt)
                dx_ref[g, s] = acc_ref[g * lg : (g + 1) * lg, cols].astype(jnp.bfloat16)


def input_back(dattn, dq, dk, dv, first, later):
    gn, tn, wide, dt = first.shape
    L, D = dattn.shape
    col = lambda: spec((L, dt), lambda t: (0, t))
    return pl.pallas_call(
        input_back_kernel,
        grid=(tn,),
        in_specs=[
            spec((L, D), lambda t: (0, 0), True),
            col(), col(), col(),
            spec((gn, 1, wide, dt), lambda t: (0, t, 0, 0)),
            spec((gn, 1, D // gn, dt), lambda t: (0, t, 0, 0)),
        ],
        out_specs=spec((gn, tn, L // gn, dt), lambda t: (0, 0, 0, 0), True),
        out_shape=jax.ShapeDtypeStruct((gn, tn, L // gn, dt), jnp.bfloat16),
        scratch_shapes=[pltpu.VMEM((L, D), jnp.float32)],
        compiler_params=pltpu.CompilerParams(vmem_limit_bytes=50 << 20),
        cost_estimate=pl.CostEstimate(flops=7 * 10**9, bytes_accessed=20 * 10**6, transcendentals=0),
    )(dattn, dq, dk, dv, first, later)


def tail_kernel(x_ref, rel_ref, hot_ref, dq_ref, dk_ref, dv_ref, dqf_ref, dkf_ref, sm_ref, w_ref, small_ref,
                pay_ref, xt_ref, ra_ref, *, first_shift):
    t = pl.program_id(0)
    L, D = x_ref.shape
    spans = rel_ref.shape[0]
    gn, tn, _, dt = pay_ref.shape
    per = D // gn
    rg = spans // gn
    sr = small_ref.shape[2]
    f32, bf = jnp.float32, jnp.bfloat16

    @pl.when(t == 0)
    def _():
        for r in range(0, L, RB):
            xt_ref[:, r : r + RB] = x_ref[r : r + RB].T
        for r in range(0, spans, RB):
            xt_ref[:, L + r : L + r + RB] = rel_ref[r : r + RB].T
        ra_ref[...] = jnp.zeros_like(ra_ref)

    w = [w_ref[:, 0, j * per : (j + 1) * per, :].reshape(D, dt) for j in range(2)]
    qp = dotnn(dqf_ref[...], hot_ref[...]).T
    kp = dotnn(dkf_ref[...], hot_ref[...]).T
    pos = [qp.astype(bf), kp.astype(bf)]
    tops = [dq_ref, dk_ref, dv_ref]
    rows = 3 * per + rg
    pay_ref[:, t, rows : rows + sr, :] = small_ref[0].astype(bf)
    for j in range(3):
        total = jnp.sum(sm_ref[8 * j : 8 * j + 8], axis=0, keepdims=True)
        if j < 2:
            total = total + jnp.sum((qp, kp)[j], axis=0, keepdims=True)
            both = jnp.concatenate([tops[j][...], pos[j]], axis=0)
            grad = dotnn(xt_ref[...], both)
            ra_ref[...] += dotnt(pos[j], w[j])
        else:
            grad = dotnn(xt_ref[:, 0:L], tops[j][...])
        pay_ref[:, t, j * per : (j + 1) * per, :] = grad.astype(bf).reshape(gn, per, dt)
        at = first_shift + j
        pay_ref[at // sr, t, rows + at % sr : rows + at % sr + 1, :] = total.astype(bf)
    @pl.when(t == pl.num_programs(0) - 1)
    def _():
        for g in range(gn):
            for s in range(tn):
                cols = slice(s * dt, (s + 1) * dt)
                pay_ref[g, s, 3 * per : rows, :] = ra_ref[g * rg : (g + 1) * rg, cols].astype(bf)


def tail(x, rel, hot, dq, dk, dv, dqf, dkf, sums, first, small, first_shift):
    gn, tn, wide, dt = first.shape
    L, D = x.shape
    spans = rel.shape[0]
    rows = 3 * D // gn + spans // gn + small.shape[2]
    bf, f32 = jnp.bfloat16, jnp.float32
    full = lambda shape: spec(shape, lambda t: (0,) * len(shape), True)
    col = lambda: spec((L, dt), lambda t: (0, t))
    return pl.pallas_call(
        functools.partial(tail_kernel, first_shift=first_shift),
        grid=(tn,),
        in_specs=[
            full((L, D)), full((spans, D)), full((2 * L, spans)),
            col(), col(), col(),
            spec((dt, 2 * L), lambda t: (t, 0)), spec((dt, 2 * L), lambda t: (t, 0)),
            spec((24, dt), lambda t: (0, t)),
            spec((gn, 1, wide, dt), lambda t: (0, t, 0, 0)),
            spec((1,) + small.shape[1:], lambda t: (t, 0, 0, 0)),
        ],
        out_specs=full((gn, tn, rows, dt)),
        out_shape=jax.ShapeDtypeStruct((gn, tn, rows, dt), bf),
        scratch_shapes=[pltpu.VMEM((D, L + spans), bf), pltpu.VMEM((spans, D), f32)],
        compiler_params=pltpu.CompilerParams(vmem_limit_bytes=56 << 20),
        cost_estimate=pl.CostEstimate(flops=13 * 10**9, bytes_accessed=40 * 10**6, transcendentals=0),
    )(x, rel, hot, dq, dk, dv, dqf, dkf, sums, first, small)


MESH = pl.DeviceIdType.MESH


def bit_of(place, i):
    return (place // (1 << i)) % 2


def flipped(place, flips):
    for i in flips:
        place = place + (1 << i) * (1 - 2 * bit_of(place, i))
    return place


def subsets(bits):
    out = [()]
    for i in bits:
        out += [s + (i,) for s in out]
    return out


def greet(tn, gn):
    t, g = lax.axis_index("tensor"), lax.axis_index("dp")
    barrier = pltpu.get_barrier_semaphore()
    bits = list(range(gn.bit_length() - 1))
    for d in range(1, tn):
        pl.semaphore_signal(barrier, inc=1, device_id={"tensor": lax.rem(t + d, tn)}, device_id_type=MESH)
    for i in bits:
        pl.semaphore_signal(barrier, inc=1, device_id={"dp": flipped(g, (i,))}, device_id_type=MESH)
    pl.semaphore_wait(barrier, tn - 1 + len(bits))


class Wire:
    def __init__(self, send, recv):
        self.send, self.recv, self.at = send, recv, 0

    def push(self, src, dst, **device):
        c = pltpu.make_async_remote_copy(
            src, dst, self.send.at[self.at], self.recv.at[self.at], device_id=device, device_id_type=MESH
        )
        self.at += 1
        c.start()
        return c


def run_waves(chunks):
    waves = max(len(stages) + c for c, stages in enumerate(chunks)) + 1
    flight = {}
    for w in range(waves):
        for c, stages in enumerate(chunks):
            s = w - c
            if 0 < s <= len(stages):
                stages[s - 1][1](flight.pop((c, s - 1)))
            if 0 <= s < len(stages):
                flight[c, s] = stages[s][0]()


def wait_all(copies):
    for c in copies:
        c.wait()


def spread_stages(src, out, local, wire, tn, gn):
    t, g = lax.axis_index("tensor"), lax.axis_index("dp")
    bits = list(range(gn.bit_length() - 1))
    half = tn // 2
    plans = [(0, bits[1:] + bits[:1]), (half, bits[:0:-1] + bits[:1])]

    def first():
        own = pltpu.make_async_copy(src(), out(g, pl.ds(t, 1)), local)
        own.start()
        copies = [
            wire.push(src(), out(g, pl.ds(t, 1)), tensor=lax.rem(t + d, tn)) for d in range(1, tn)
        ]
        return [own] + copies

    def later(step):
        def start():
            copies = []
            for lo, plan in plans:
                for s in subsets(plan[:step]):
                    part = out(flipped(g, s), pl.ds(lo, half))
                    copies.append(wire.push(part, part, dp=flipped(g, (plan[step],))))
            return copies

        return start

    return [(first, wait_all)] + [(later(step), wait_all) for step in range(len(bits))]


def spread_count(tn, gn):
    return tn - 1 + 2 * (gn - 1)


def gather_kernel(src_ref, out_ref, local, send, recv, *, tn, gn, cuts):
    greet(tn, gn)
    wire = Wire(send, recv)
    chunks = []
    for n, (lo, hi) in enumerate(cuts):
        rows = pl.ds(lo, hi - lo)
        chunks.append(
            spread_stages(
                lambda rows=rows: src_ref.at[:, rows],
                lambda g, s, rows=rows: out_ref.at[g, s, rows],
                local.at[n], wire, tn, gn,
            )
        )
    run_waves(chunks)


def gather_all(w, tn, gn, number):
    rows = w.shape[0]
    mid = rows // 32 * 16
    cuts = [(0, mid), (mid, rows)]
    n = spread_count(tn, gn) * len(cuts)
    dma = lambda k: pltpu.SemaphoreType.DMA((k,))
    return pl.pallas_call(
        functools.partial(gather_kernel, tn=tn, gn=gn, cuts=cuts),
        in_specs=[pl.BlockSpec(memory_space=pl.ANY)],
        out_specs=pl.BlockSpec(memory_space=pl.ANY),
        out_shape=jax.ShapeDtypeStruct((gn, tn) + w.shape, w.dtype),
        scratch_shapes=[dma(len(cuts)), dma(n), dma(n)],
        compiler_params=pltpu.CompilerParams(collective_id=number, has_side_effects=True),
        cost_estimate=pl.CostEstimate(flops=0, bytes_accessed=w.size * tn * gn * 16, transcendentals=0),
    )(w[None])


def reduce_kernel(pay_ref, q_ref, k_ref, v_ref, rel_ref, small_ref, all_ref, acc_ref, rx_ref, ry_ref, rz_ref, rest_ref,
                  local, send, recv, *, tn, gn, keep):
    t, g = lax.axis_index("tensor"), lax.axis_index("dp")
    bits = list(range(gn.bit_length() - 1))
    f32, bf = jnp.float32, jnp.bfloat16
    rows = acc_ref.shape[2]
    per = keep // 3
    greet(tn, gn)
    wire = Wire(send, recv)
    outer = bits[1:]
    masks = subsets(outer)
    index = {s: n for n, s in enumerate(masks)}
    half = tn // 2
    plans = [(0, outer), (half, outer[::-1])]
    grads = (q_ref, k_ref, v_ref)

    def reduce_stages(n, lo, hi):
        span = pl.ds(lo, hi - lo)

        def add(dst, first, size, src_ref, slot):
            for i in range(size):
                acc_ref[dst, first + i, lo:hi] = (
                    acc_ref[dst, first + i, lo:hi].astype(f32) + src_ref[slot, i, lo:hi].astype(f32)
                ).astype(bf)

        def first():
            copies = []
            for i, s in enumerate(masks):
                copies.append(wire.push(pay_ref.at[flipped(g, (0,) + s), :, span], rx_ref.at[i, :, span], dp=flipped(g, (0,))))
            for i, s in enumerate(masks):
                c = pltpu.make_async_copy(pay_ref.at[flipped(g, s), :, span], acc_ref.at[i, :, span], local.at[n, i])
                c.start()
                copies.append(c)
            return copies

        def first_done(copies):
            for i in range(len(masks)):
                copies[len(masks) + i].wait()
                copies[i].wait()
                add(i, 0, tn, rx_ref, i)

        def outer_stage(step, base):
            def start():
                flight = []
                slot = base
                for place, plan in plans:
                    bit = plan[step]
                    for s in masks:
                        if any(i in plan[: step + 1] for i in s):
                            continue
                        src = tuple(i for i in outer if i in s or i == bit)
                        c = wire.push(
                            acc_ref.at[index[src], pl.ds(place, half), span], ry_ref.at[slot, :, span],
                            dp=flipped(g, (bit,)),
                        )
                        flight.append((c, index[s], place, slot))
                        slot += 1
                return flight

            def done(flight):
                for c, dst, place, slot in flight:
                    c.wait()
                    add(dst, place, half, ry_ref, slot)

            return start, done

        def last():
            return [
                wire.push(acc_ref.at[0, lax.rem(t + d, tn), span], rz_ref.at[d - 1, span], tensor=lax.rem(t + d, tn))
                for d in range(1, tn)
            ]

        def last_done(copies):
            total = acc_ref[0, t, lo:hi].astype(f32)
            for d, c in enumerate(copies):
                c.wait()
                total = total + rz_ref[d, lo:hi].astype(f32)
            if lo >= keep:
                rest_ref[0] = total.astype(bf)
            else:
                for j in range(3):
                    a, b = max(lo, j * per), min(hi, (j + 1) * per)
                    if a < b:
                        grads[j][a - j * per : b - j * per] = total[a - lo : b - lo]

        stages = [(first, first_done)]
        base = 0
        for step in range(len(outer)):
            stages.append(outer_stage(step, base))
            base += 2 * (gn // 4 >> step)
        return stages + [(last, last_done)]

    cut = keep // 32 * 16
    chunks = [
        reduce_stages(0, keep, rows)
        + spread_stages(
            lambda: rest_ref, lambda i, s: all_ref.at[i, s], local.at[3, 0], wire, tn, gn
        ),
        reduce_stages(1, 0, cut),
        reduce_stages(2, cut, keep),
    ]
    run_waves(chunks)
    dt = q_ref.shape[1]
    rg = rel_ref.shape[0] // gn
    for s in range(tn):
        cols = slice(s * dt, (s + 1) * dt)
        for i in range(gn):
            rel_ref[i * rg : (i + 1) * rg, cols] = all_ref[i, s, :rg].astype(f32)
        small_ref[:, cols] = all_ref[0, s, rg:].astype(f32)


def reduce_all(pay, keep, spans, number):
    gn, tn, rows, dt = pay.shape
    bf, f32 = jnp.bfloat16, jnp.float32
    m = gn // 2
    pieces = 2 * (m - 1)
    count = 3 * (m + pieces + tn - 1) + spread_count(tn, gn)
    dma = lambda *k: pltpu.SemaphoreType.DMA(k)
    return pl.pallas_call(
        functools.partial(reduce_kernel, tn=tn, gn=gn, keep=keep),
        in_specs=[pl.BlockSpec(memory_space=pl.ANY)],
        out_specs=[pl.BlockSpec(memory_space=pltpu.VMEM)] * 5,
        out_shape=[jax.ShapeDtypeStruct((keep // 3, dt), f32)] * 3
        + [
            jax.ShapeDtypeStruct((spans, tn * dt), f32),
            jax.ShapeDtypeStruct((rows - keep - spans // gn, tn * dt), f32),
        ],
        scratch_shapes=[
            pltpu.VMEM((gn, tn, rows - keep, dt), bf),
            pltpu.VMEM((m, tn, rows, dt), bf),
            pltpu.VMEM((m, tn, rows, dt), bf),
            pltpu.VMEM((pieces, tn // 2, rows, dt), bf),
            pltpu.VMEM((tn - 1, rows, dt), bf),
            pltpu.VMEM((1, rows - keep, dt), bf),
            dma(4, m), dma(count), dma(count),
        ],
        compiler_params=pltpu.CompilerParams(collective_id=number, has_side_effects=True, vmem_limit_bytes=40 << 20),
        cost_estimate=pl.CostEstimate(flops=0, bytes_accessed=200 * 10**6, transcendentals=0),
    )(pay)


def shards(
    inputs,
    cotangent,
    lengths,
    dealing,
    buckets,
    rel_embed,
    query_weight,
    key_weight,
    value_weight,
    proj_shifts,
    merge_weight,
    inner_weight,
    hidden_shift,
    outer_weight,
    layer_vectors,
):
    tn = lax.axis_size("tensor")
    gn = lax.axis_size("dp")
    me = lax.axis_index("dp") * tn + lax.axis_index("tensor")
    count, lg, dt = inputs.shape
    L, D = lg * gn, dt * tn
    per = query_weight.shape[0]
    rg = rel_embed.shape[0]
    spans = rg * gn
    assert count == tn * gn
    bf = jnp.bfloat16
    f32 = jnp.float32
    scale = 1.0 / math.sqrt(3.0 * HEAD)
    seq_axes = ("dp", "tensor")
    w_axes = ("tensor", "dp")

    def swap(a):
        return lax.all_to_all(a, seq_axes, split_axis=0, concat_axis=0, tiled=True)

    def gather(w):
        return lax.all_gather(w, w_axes, axis=0, tiled=False).reshape((tn, gn) + w.shape)

    rel_cols = lax.dynamic_slice_in_dim(rel_embed, lax.axis_index("tensor") * dt, dt, 1)
    early = jnp.concatenate([query_weight, key_weight], axis=0)
    late = jnp.concatenate(
        [value_weight, rel_cols, proj_shifts, hidden_shift.reshape(-1, dt), jnp.zeros((1, dt), bf)], axis=0
    )
    first = gather_all(early, tn, gn, 0)
    xd = swap(inputs).reshape(gn, tn, lg, dt)
    wide = jnp.concatenate([inner_weight, outer_weight, merge_weight], axis=1)
    first, xd, late, wide, cotangent = lax.optimization_barrier((first, xd, late, wide, cotangent))
    second = gather(wide)
    later = gather_all(late, tn, gn, 2)
    cot = swap(cotangent).reshape(gn, tn, lg, dt)
    biases = later[0, :, per + rg :].astype(f32)
    shifts = biases[:, :3]
    hidden_bias = biases[:, 3:7].reshape(tn, 1, -1)
    vectors = layer_vectors.astype(f32)
    length = jnp.sum(jnp.where(dealing == me, lengths, 0)).reshape(1)
    places = jnp.concatenate([buckets[::-1], jnp.full((1,), -1, jnp.int32)])[:, None]

    qkv, far, x, rel, hot = project(xd, first, later, shifts, places, per)
    ctx, probs, inv = attn_fwd(length, qkv, far, scale=scale)
    y, payload, hidden, dattn, sums12 = middle(ctx, x, second, hidden_bias, vectors, cot)
    out = swap(y.reshape(count, lg, dt))
    payload, dctx = merge_back(dattn, ctx, second, payload)
    wide_grads = lax.psum_scatter(payload, "dp", scatter_dimension=0, tiled=False)
    dq, dk, dv, dkf, dqf, sums = attn_bwd(probs, qkv, dctx, ctx, inv, far, scale=scale)
    dq, out, wide_grads = lax.optimization_barrier((dq, out, wide_grads))
    wide_grads = lax.psum_scatter(wide_grads, "tensor", scatter_dimension=0, tiled=False)
    ff = hidden.shape[2]
    small = jnp.concatenate(
        [
            jnp.sum(sums12.reshape(6, 8, D), axis=1),
            jnp.sum(hidden, axis=1).reshape(-1, D),
        ],
        axis=0,
    )
    first_shift = small.shape[0]
    sr = 16
    small = jnp.pad(small, ((0, sr - first_shift), (0, 0)))
    small = small.reshape(sr, tn, dt).transpose(1, 0, 2)[:, None]
    small = jnp.pad(small, ((0, 0), (0, gn - 1), (0, 0), (0, 0)))
    dx = input_back(dattn, dq, dk, dv, first, later)
    dx, dq = lax.optimization_barrier((dx, dq))
    pay = tail(x, rel, hot, dq, dk, dv, dqf, dkf, sums, first, small, first_shift)
    grad_in = swap(dx.reshape(count, lg, dt))
    wide_grads = wide_grads.astype(f32)
    query_grad, key_grad, value_grad, rel_grad, rest = reduce_all(pay, 3 * per, spans, 1)
    return (
        out,
        grad_in,
        rel_grad,
        query_grad,
        key_grad,
        value_grad,
        rest[first_shift : first_shift + 3],
        wide_grads[:, 2 * ff :],
        wide_grads[:, :ff],
        rest[6:first_shift].reshape(-1),
        wide_grads[:, ff : 2 * ff],
        rest[:6],
    )


def solution(mesh):
    split = P("dp", "tensor")
    whole = P(None, "dp", "tensor")
    in_specs = (
        whole, whole, P(), P(), P(), P("dp", None), split, split, split, P(None, "tensor"),
        split, split, P("tensor"), split, P(),
    )
    out_specs = (whole, whole, P(), split, split, split, P(), split, split, P(), split, P())
    return jax.shard_map(shards, mesh=mesh, in_specs=in_specs, out_specs=out_specs, check_vma=False)
```

```python
import functools
import math

import jax
import jax.numpy as jnp
from jax import lax
from jax.experimental import pallas as pl
from jax.experimental.pallas import tpu as pltpu
from jax.sharding import PartitionSpec as P

EPSILON = 1e-07
HEAD = 64
B = 128
SR = 16
NT = (((1,), (1,)), ((), ()))


def dotnt(a, b):
    return lax.dot_general(a, b, NT, preferred_element_type=jnp.float32)


def dotnn(a, b):
    return lax.dot_general(a, b, (((1,), (0,)), ((), ())), preferred_element_type=jnp.float32)


def skew(g_ref, a, n, L):
    parts=[]
    nb=L//B
    for a8 in range(a,a+n,8):
        rot=[pltpu.roll(g_ref[a8:a8+8,t*128:t*128+128], 1+a8, 1, stride=1, stride_axis=0) for t in range(nb+1)]
        msk=lax.broadcasted_iota(jnp.int32,(8,128),1) < (1+a8+lax.broadcasted_iota(jnp.int32,(8,128),0))
        parts.append(jnp.concatenate([jnp.where(msk,rot[t],rot[t+1]) for t in range(nb)],axis=1))
    return jnp.concatenate(parts,axis=0)

def fwd_kernel(len_ref, q_ref, k_ref, v_ref, kf_ref, qf_ref, ctx_ref, p_ref, l_ref, t_ref, kx_ref, vx_ref, g0, g1, s0, s1, *, L, scale):
    W = L + B
    nb = L // B
    gs=(g0,g1); ss=(s0,s1)
    lane = lax.broadcasted_iota(jnp.int32, (1, 128), 1)
    length = len_ref[0]
    row = lax.broadcasted_iota(jnp.int32, (L, 128), 0)
    c2 = scale * math.log2(math.e)
    eye = (lax.broadcasted_iota(jnp.int32,(B,B),0)==lax.broadcasted_iota(jnp.int32,(B,B),1)).astype(jnp.bfloat16)
    zero = jnp.zeros((), jnp.bfloat16)
    mine = [lane < 64, lane >= 64]
    first_other = [lane==64, lane==0]
    for h in range(2):
        bias = jnp.where((row >= length) & first_other[h], -1e30, 0.0).astype(jnp.bfloat16)
        kx_ref[h] = jnp.where(mine[h], k_ref[...], bias)
        vx_ref[h] = jnp.where(mine[h], v_ref[...], jnp.ones((), jnp.bfloat16))
    def tblock(b, _):
        r0 = pl.multiple_of(b*B, B)
        base = pl.multiple_of(L - B - b*B, B)
        for h in range(2):
            kb = jnp.where(mine[h], k_ref[pl.ds(r0,B),:], zero)
            gs[h][...] = dotnt(kb, qf_ref[pl.ds(base, W), :])
        for h in range(2):
            for a in range(0, B, SR):
                t_ref[h, pl.ds(r0+a,SR), :] = skew(gs[h], a, SR, L).astype(jnp.bfloat16)
        return 0
    lax.fori_loop(0, nb, tblock, 0, unroll=2)
    def scores(b, h):
        r0 = pl.multiple_of(b*B, B)
        base = pl.multiple_of(L - B - b*B, B)
        qb = q_ref[pl.ds(r0,B),:]
        qm = jnp.where(mine[h], qb, zero)
        qx = jnp.where(mine[h], qb, first_other[h].astype(jnp.bfloat16))
        gs[h][...] = dotnt(qm, kf_ref[pl.ds(base, W), :])
        lhs = jnp.concatenate([qx, eye], axis=1)
        rhs = jnp.concatenate([kx_ref[h], t_ref[h, :, pl.ds(r0,B)]], axis=1)
        ss[h][...] = dotnt(lhs, rhs)
    def soft(b, h):
        r0 = pl.multiple_of(b*B, B)
        tops=[]
        for a in range(0, B, 8):
            s = ss[h][a:a+8] + skew(gs[h], a, 8, L)
            ss[h][a:a+8] = s
            tops.append(functools.reduce(jnp.maximum,[s[:,t*128:t*128+128] for t in range(nb)]))
        m = jnp.max(jnp.concatenate(tops,axis=0), axis=1, keepdims=True) * c2
        for a in range(0, B, SR):
            p_ref[h, pl.ds(r0+a,SR), :] = jnp.exp2(ss[h][a:a+SR]*c2 - m[a:a+SR]).astype(jnp.bfloat16)
    def out(b, h):
        r0 = pl.multiple_of(b*B, B)
        return dotnn(p_ref[h, pl.ds(r0,B), :], vx_ref[h])
    def finish(b, o0, o1):
        r0 = pl.multiple_of(b*B, B)
        num = jnp.where(mine[0], o0, o1)
        den = jnp.where(mine[0], pltpu.roll(o0,64,1), pltpu.roll(o1,64,1))
        inv = 1.0/den
        ctx_ref[pl.ds(r0,B),:] = (num*inv).astype(jnp.bfloat16)
        l_ref[pl.ds(r0,B),:] = inv
    scores(0,0)
    def sblock(b, o0):
        scores(b,1)
        soft(b,0)
        o0 = out(b,0)
        scores(jnp.minimum(b+1,nb-1),0)
        soft(b,1)
        o1 = out(b,1)
        finish(b,o0,o1)
        return 0
    lax.fori_loop(0, nb, sblock, 0, unroll=8)


def attn_fwd(length, qkv, far, *, scale):
    _, L, C = qkv.shape
    part = lambda j, r: pl.BlockSpec((None, r, 128), lambda h, *_: (j, 0, h))
    return pl.pallas_call(
        functools.partial(fwd_kernel, L=L, scale=scale),
        grid_spec=pltpu.PrefetchScalarGridSpec(
            num_scalar_prefetch=1,
            grid=(C // 128,),
            in_specs=[part(0, L), part(1, L), part(2, L), part(1, 2 * L), part(0, 2 * L)],
            out_specs=[
                pl.BlockSpec((L, 128), lambda h, *_: (0, h)),
                pl.BlockSpec((2, L, L), lambda h, *_: (h, 0, 0)),
                pl.BlockSpec((L, 128), lambda h, *_: (0, h)),
            ],
            scratch_shapes=[pltpu.VMEM((2, L, L), jnp.bfloat16)]
            + [pltpu.VMEM((2, L, 128), jnp.bfloat16)] * 2
            + [pltpu.VMEM((B, L + B), jnp.float32)] * 2
            + [pltpu.VMEM((B, L), jnp.float32)] * 2,
        ),
        out_shape=[
            jax.ShapeDtypeStruct((L, C), jnp.bfloat16),
            jax.ShapeDtypeStruct((C // HEAD, L, L), jnp.bfloat16),
            jax.ShapeDtypeStruct((L, C), jnp.float32),
        ],
        compiler_params=pltpu.CompilerParams(vmem_limit_bytes=50 << 20),
        cost_estimate=pl.CostEstimate(flops=80 * 10**9, bytes_accessed=60 * 10**6, transcendentals=0),
    )(length, qkv, qkv, qkv, far, far)


FAR = 3


def unskew(x, a8):
    nb = x.shape[1] // B
    sub = lax.broadcasted_iota(jnp.int32, (8, 128), 0)
    lane = lax.broadcasted_iota(jnp.int32, (8, 128), 1)
    keep = lane >= (127 - a8) - sub
    idx = (lane - (127 - a8) + sub) & 127
    rot = [jnp.take_along_axis(x[:, t * 128 : t * 128 + 128], idx, axis=1) for t in range(nb)]
    zero = jnp.zeros((8, 128), x.dtype)
    return jnp.concatenate(
        [jnp.where(keep, rot[t] if t < nb else zero, rot[t - 1] if t > 0 else zero) for t in range(nb + 1)], axis=1
    )


def fold_tiles(x, lo, hi):
    return sum(x[:, t * 128 : t * 128 + 128] for t in range(lo, hi))


def place_back(rows8, d_ref, a, b, nb):
    lo, hi = max(0, b - FAR), min(nb, b + FAR + 1)
    near = jnp.concatenate([unskew(x[:, lo * 128 : hi * 128], a + 8 * n) for n, x in enumerate(rows8)], axis=0)
    d_ref[a : a + SR, 256 : 256 + near.shape[1]] = near.astype(jnp.bfloat16)
    if lo > 0:
        far = jnp.concatenate([fold_tiles(x, 0, lo) for x in rows8], axis=0)
        d_ref[a : a + SR, 0:128] = far.astype(jnp.bfloat16)
    if hi < nb:
        far = jnp.concatenate([fold_tiles(x, hi, nb) for x in rows8], axis=0)
        d_ref[a : a + SR, 128:256] = far.astype(jnp.bfloat16)


def window_products(d_ref, table_ref, ends_ref, e, lhs, acc_ref, sums_ref, rows, b, nb):
    lo, hi = max(0, b - FAR), min(nb, b + FAR + 1)
    base, size = (nb - 1 - b + lo) * B, (hi - lo + 1) * B
    near = d_ref[:, 256 : 256 + size]
    out = dotnn(near, table_ref[base : base + size, :])
    acc_ref[rows, base : base + size] += dotnn(lhs, near)
    for there, k in ((lo > 0, 0), (hi < nb, 1)):
        if there:
            far = d_ref[:, k * 128 : k * 128 + 128]
            out = out + dotnn(far, ends_ref[e + k])
            sums_ref[e + k, rows, :] += dotnn(lhs, far)
    return out


def bwd_kernel(p_ref, q_ref, k_ref, v_ref, do_ref, ctx_ref, li_ref, kf_ref, qf_ref,
               dq_ref, dk_ref, dv_ref, dkf_ref, dqf_ref, sums_ref,
               dox_ref, dot_ref, qt_ref, kt_ref, vx_ref, ds_ref, d0, d1, akf, aqf, ends, far, *, L, scale):
    W = L + B
    nb = L // B
    dd=(d0,d1)
    lane = lax.broadcasted_iota(jnp.int32, (1, 128), 1)
    mine = [lane < 64, lane >= 64]
    base_lane = [64, 0]
    dos = (do_ref[...].astype(jnp.float32) * li_ref[...]).astype(jnp.bfloat16)
    prod = dos.astype(jnp.float32) * ctx_ref[...].astype(jnp.float32)
    for h in range(2):
        delta = -jnp.sum(jnp.where(mine[h], prod, 0.0), axis=1, keepdims=True)
        hi = delta.astype(jnp.bfloat16).astype(jnp.float32)
        lo = delta - hi
        extra = jnp.where(lane == base_lane[h], hi, jnp.where(lane == base_lane[h]+1, lo, 0.0)).astype(jnp.bfloat16)
        dox_ref[h] = jnp.where(mine[h], dos, extra)
        vx_ref[h] = jnp.where(mine[h], v_ref[...], jnp.ones((), jnp.bfloat16))
    dot_ref[...] = dos.T
    qt_ref[...] = q_ref[...].T
    kt_ref[...] = k_ref[...].T
    akf[...] = jnp.zeros_like(akf)
    aqf[...] = jnp.zeros_like(aqf)
    far[...] = jnp.zeros_like(far)
    last = 2 * L - 2
    for e, table in ((0, kf_ref), (2, qf_ref)):
        ends[e] = jnp.broadcast_to(table[0:1, :], (128, 128))
        ends[e + 1] = jnp.broadcast_to(table[last : last + 1, :], (128, 128))
    sq = jnp.zeros((8, 128), jnp.float32)
    for b in range(nb):
        r0 = b * B
        outs = []
        for h in range(2):
            rows = slice(h * 64, h * 64 + 64)
            dp = dotnt(dox_ref[h, r0 : r0 + B, :], vx_ref[h])
            for a in range(0, B, SR):
                ds = p_ref[h, r0 + a : r0 + a + SR, :].astype(jnp.float32) * dp[a : a + SR]
                ds_ref[h, r0 + a : r0 + a + SR, :] = ds.astype(jnp.bfloat16)
                place_back([ds[s : s + 8] for s in range(0, SR, 8)], dd[h], a, b, nb)
            outs.append(
                dotnn(ds_ref[h, r0 : r0 + B, :], k_ref[...])
                + window_products(dd[h], kf_ref, ends, 0, qt_ref[rows, r0 : r0 + B], akf, far, rows, b, nb)
            )
        dq = jnp.where(mine[0], outs[0], outs[1]) * scale
        dq_ref[r0 : r0 + B, :] = dq.astype(jnp.bfloat16)
        sq = sq + jnp.sum(dq.reshape(B // 8, 8, 128), axis=0)
    sk = jnp.zeros((8, 128), jnp.float32)
    for b in range(nb):
        r0 = b * B
        outs = []
        for h in range(2):
            rows = slice(h * 64, h * 64 + 64)
            dst = ds_ref[h, :, r0 : r0 + B].T
            for a in range(0, B, SR):
                x = dst[a : a + SR].astype(jnp.float32)
                place_back([x[s : s + 8] for s in range(0, SR, 8)], dd[h], a, b, nb)
            outs.append(
                dotnn(dst, q_ref[...])
                + window_products(dd[h], qf_ref, ends, 2, kt_ref[rows, r0 : r0 + B], aqf, far, rows, b, nb)
            )
        dk = jnp.where(mine[0], outs[0], outs[1]) * scale
        dk_ref[r0 : r0 + B, :] = dk.astype(jnp.bfloat16)
        sk = sk + jnp.sum(dk.reshape(B // 8, 8, 128), axis=0)
    for e, acc in ((0, akf), (2, aqf)):
        for k, at in ((0, 0), (1, last)):
            tile = at // 128 * 128
            total = jnp.sum(far[e + k], axis=1, keepdims=True)
            acc[:, tile : tile + 128] += jnp.where(lane == at - tile, total, 0.0)
    dvt = jnp.concatenate([dotnn(dot_ref[h*64:h*64+64,:], p_ref[h]) for h in range(2)], axis=0)
    dv = dvt.T
    dv_ref[...] = dv.astype(jnp.bfloat16)
    sv = jnp.sum(dv.reshape(L//8,8,128), axis=0)
    sums_ref[0:8] = sq
    sums_ref[8:16] = sk
    sums_ref[16:24] = sv
    dkf_ref[...] = (akf[...]*scale).astype(jnp.bfloat16)
    dqf_ref[...] = (aqf[...]*scale).astype(jnp.bfloat16)


def attn_bwd(p, qkv, do, ctx, linv, far, *, scale):
    _, L, C = qkv.shape
    bf = jnp.bfloat16
    part = lambda j, r: pl.BlockSpec((None, r, 128), lambda h: (j, 0, h))
    col = lambda r: pl.BlockSpec((r, 128), lambda h: (0, h))
    rowb = pl.BlockSpec((128, 2 * L), lambda h: (h, 0))
    return pl.pallas_call(
        functools.partial(bwd_kernel, L=L, scale=scale),
        grid=(C // 128,),
        in_specs=[pl.BlockSpec((2, L, L), lambda h: (h, 0, 0)), part(0, L), part(1, L), part(2, L)]
        + [col(L)] * 3
        + [part(1, 2 * L), part(0, 2 * L)],
        out_specs=[col(L)] * 3 + [rowb] * 2 + [col(24)],
        scratch_shapes=[pltpu.VMEM((2, L, 128), bf)]
        + [pltpu.VMEM((128, L), bf)] * 3
        + [pltpu.VMEM((2, L, 128), bf), pltpu.VMEM((2, L, L), bf)]
        + [pltpu.VMEM((B, L + 3 * B), bf)] * 2
        + [pltpu.VMEM((128, 2 * L), jnp.float32)] * 2
        + [pltpu.VMEM((4, 128, 128), bf), pltpu.VMEM((4, 128, 128), jnp.float32)],
        out_shape=[jax.ShapeDtypeStruct((L, C), bf)] * 3
        + [jax.ShapeDtypeStruct((C, 2 * L), bf)] * 2
        + [jax.ShapeDtypeStruct((24, C), jnp.float32)],
        compiler_params=pltpu.CompilerParams(vmem_limit_bytes=56 << 20),
        cost_estimate=pl.CostEstimate(flops=120 * 10**9, bytes_accessed=80 * 10**6, transcendentals=0),
    )(p, qkv, qkv, qkv, do, ctx, linv, far, far)


def spec(block, index, once=False):
    if once:
        return pl.BlockSpec(block, index, pipeline_mode=pl.Buffered(1))
    return pl.BlockSpec(block, index)


def norm_rows(z):
    center = z - jnp.mean(z, axis=-1, keepdims=True)
    r = lax.rsqrt(jnp.mean(center * center, axis=-1, keepdims=True) + EPSILON)
    return center * r, r


def norm_back(g, n, r):
    return r * (g - jnp.mean(g, axis=-1, keepdims=True) - n * jnp.mean(g * n, axis=-1, keepdims=True))


def fold8(v):
    return jnp.sum(v.reshape(v.shape[0] // 8, 8, v.shape[1]), axis=0)


def project_kernel(xd_ref, rel4_ref, wa_ref, wb_ref, sh_ref, pl_ref, qkv_ref, far_ref, x_ref, rel_ref, hot_ref):
    t, j = pl.program_id(0), pl.program_id(1)
    gn, tn, lg, dt = xd_ref.shape
    spans = rel_ref.shape[0]
    rg = spans // gn

    @pl.when((t == 0) & (j == 0))
    def _():
        for g in range(gn):
            for s in range(tn):
                x_ref[g * lg : (g + 1) * lg, s * dt : (s + 1) * dt] = xd_ref[g, s]
                rel_ref[g * rg : (g + 1) * rg, s * dt : (s + 1) * dt] = rel4_ref[g, s]
        rows = hot_ref.shape[0]
        lanes = lax.broadcasted_iota(jnp.int32, (rows, spans), 1)
        hot_ref[...] = (pl_ref[...] == lanes).astype(jnp.float32).astype(jnp.bfloat16)

    w = jnp.where(j < 2, wa_ref[:, 0], wb_ref[:, 0]).reshape(x_ref.shape[1], dt)
    shift = sh_ref[0, pl.ds(j, 1), :]
    qkv_ref[0] = (dotnn(x_ref[...], w) + shift).astype(jnp.bfloat16)

    @pl.when(j < 2)
    def _():
        place = (dotnn(rel_ref[...], w) + shift).astype(jnp.bfloat16)
        far_ref[0] = dotnn(hot_ref[...], place).astype(jnp.bfloat16)


def project(xd, first, later, shifts, places, per):
    gn, tn, lg, dt = xd.shape
    L, D = gn * lg, tn * dt
    rg = later.shape[2] - per - 8
    spans = rg * gn
    bf = jnp.bfloat16
    return pl.pallas_call(
        project_kernel,
        grid=(tn, 3),
        in_specs=[
            spec((gn, tn, lg, dt), lambda t, j: (0, 0, 0, 0), True),
            spec((gn, tn, rg, dt), lambda t, j: (0, 0, per // rg, 0), True),
            spec((gn, 1, per, dt), lambda t, j: (0, t, jnp.minimum(j, 1), 0)),
            spec((gn, 1, per, dt), lambda t, j: (0, t, 0, 0)),
            spec((1, 3, dt), lambda t, j: (t, 0, 0)),
            spec((2 * L, 1), lambda t, j: (0, 0), True),
        ],
        out_specs=[
            spec((1, L, dt), lambda t, j: (j, 0, t)),
            spec((1, 2 * L, dt), lambda t, j: (jnp.minimum(j, 1), 0, t)),
            spec((L, D), lambda t, j: (0, 0)),
            spec((spans, D), lambda t, j: (0, 0)),
            spec((2 * L, spans), lambda t, j: (0, 0)),
        ],
        out_shape=[
            jax.ShapeDtypeStruct((3, L, D), bf),
            jax.ShapeDtypeStruct((2, 2 * L, D), bf),
            jax.ShapeDtypeStruct((L, D), bf),
            jax.ShapeDtypeStruct((spans, D), bf),
            jax.ShapeDtypeStruct((2 * L, spans), bf),
        ],
        compiler_params=pltpu.CompilerParams(vmem_limit_bytes=50 << 20),
        cost_estimate=pl.CostEstimate(flops=14 * 10**9, bytes_accessed=30 * 10**6, transcendentals=0),
    )(xd, later, first, later, shifts, places)


RB = 256


MB = 256


def middle_kernel(ctx_ref, x_ref, wm_ref, wi_ref, wo_ref, hb_ref, vec_ref, cot_ref,
                  y_ref, pay_ref, hid_ref, da_ref, sums_ref,
                  act_ref, slope_ref, hl_ref, hlt_ref, r1_ref, df_ref, acc_ref, sem):
    step = pl.program_id(0)
    L, D = x_ref.shape
    gn, tn, lg, dt = cot_ref.shape
    _, _, per, ff = wi_ref.shape[0], 0, wi_ref.shape[2], wi_ref.shape[3]
    f32, bf = jnp.float32, jnp.bfloat16

    slots = D // ff

    @pl.when(step == 0)
    def _():
        copies = []
        for n, src in enumerate((ctx_ref, x_ref)):
            for u in range(slots):
                at = n * slots + u
                c = pltpu.make_async_copy(src.at[:, pl.ds(u * ff, ff)], slope_ref.at[1 + at], sem.at[at])
                c.start()
                copies.append(c)
        for c in copies:
            c.wait()
        for r in range(0, L, MB):
            rows = slice(r, r + MB)
            z1 = jnp.concatenate([slope_ref[1 + slots + u, rows] for u in range(slots)], axis=1)
            z1 = vec_ref[0:1] + z1.astype(f32)
            for s in range(tn):
                at = s * dt % ff
                part = slope_ref[1 + s * dt // ff, rows, at : at + dt]
                z1 = z1 + dotnt(part, wm_ref[s].reshape(D, dt))
            n1, r1 = norm_rows(z1)
            h1 = n1 * vec_ref[1:2] + vec_ref[2:3]
            low = h1.astype(bf)
            acc_ref[rows] = h1 + vec_ref[3:4]
            hl_ref[rows] = low
            hlt_ref[:, rows] = low.T
            da_ref[rows] = n1.astype(bf)
            high = r1.astype(bf).astype(f32)
            first_lane = lax.broadcasted_iota(jnp.int32, (MB, 128), 1) == 0
            r1_ref[rows] = jnp.where(first_lane, high, r1 - high).astype(bf)

    @pl.when(step < tn)
    def _():
        for r in range(0, L, MB):
            rows = slice(r, r + MB)
            pre = dotnn(hl_ref[rows], wi_ref[0].reshape(D, ff)) + hb_ref[0]
            phi = 0.5 + 0.5 * lax.erf(pre * math.sqrt(0.5))
            act = (pre * phi).astype(bf)
            act_ref[step, rows] = act
            bell = jnp.exp(-0.5 * pre * pre) * (1.0 / math.sqrt(2.0 * math.pi))
            slope_ref[step, rows] = (phi + pre * bell).astype(bf)
            acc_ref[rows] += dotnt(act, wo_ref[0].reshape(D, ff))

    @pl.when(step == tn - 1)
    def _():
        s0 = jnp.zeros((8, D), f32)
        s1 = jnp.zeros((8, D), f32)
        s2 = jnp.zeros((8, D), f32)
        for g in range(gn):
            rows = slice(g * lg, (g + 1) * lg)
            n2, r2 = norm_rows(acc_ref[rows])
            y = (n2 * vec_ref[4:5] + vec_ref[5:6]).astype(bf)
            for s in range(tn):
                y_ref[g, s] = y[:, s * dt : (s + 1) * dt]
            dy = jnp.concatenate([cot_ref[g, s] for s in range(tn)], axis=1).astype(f32)
            dz2 = norm_back(dy * vec_ref[4:5], n2, r2)
            df_ref[rows] = dz2.astype(bf)
            acc_ref[rows] = dz2
            s0, s1, s2 = s0 + fold8(dz2), s1 + fold8(dy * n2), s2 + fold8(dy)
        sums_ref[24:32], sums_ref[32:40], sums_ref[40:48] = s0, s1, s2
        for r in range(0, L, RB):
            hl_ref[:, r : r + RB] = df_ref[r : r + RB].T

    @pl.when(step >= tn)
    def _():
        t = 2 * tn - 1 - step
        hid = jnp.zeros((8, ff), f32)
        for r in range(0, L, MB):
            rows = slice(r, r + MB)
            dpre = dotnn(df_ref[rows], wo_ref[0].reshape(D, ff)) * slope_ref[t, rows].astype(f32)
            hid = hid + fold8(dpre)
            low = dpre.astype(bf)
            slope_ref[t, rows] = low
            acc_ref[rows] += dotnt(low, wi_ref[0].reshape(D, ff))
        hid_ref[0] = hid
        for r in range(0, D, RB):
            og = dotnn(hl_ref[r : r + RB], act_ref[t]).astype(bf)
            ig = dotnn(hlt_ref[r : r + RB], slope_ref[t]).astype(bf)
            for c in range(0, RB, per):
                pay_ref[(r + c) // per, 0, :, 0:ff] = ig[c : c + per]
                pay_ref[(r + c) // per, 0, :, ff : 2 * ff] = og[c : c + per]

    @pl.when(step == 2 * tn - 1)
    def _():
        s0 = jnp.zeros((8, D), f32)
        s1 = jnp.zeros((8, D), f32)
        s2 = jnp.zeros((8, D), f32)
        for r in range(0, L, 128):
            rows = slice(r, r + 128)
            dh1 = acc_ref[rows]
            n1 = da_ref[rows].astype(f32)
            r1 = r1_ref[rows, 0:1].astype(f32) + r1_ref[rows, 1:2].astype(f32)
            dz1 = norm_back(dh1 * vec_ref[1:2], n1, r1)
            da_ref[rows] = dz1.astype(bf)
            s0, s1, s2 = s0 + fold8(dz1), s1 + fold8(dh1 * n1), s2 + fold8(dh1)
        sums_ref[0:8], sums_ref[8:16], sums_ref[16:24] = s0, s1, s2


def middle(ctx, x, second, hidden_bias, vectors, cot):
    gn, tn, lg, dt = cot.shape
    per, wide = second.shape[2:]
    L, D = x.shape
    assert L == D
    ff = hidden_bias.shape[2]
    bf, f32 = jnp.bfloat16, jnp.float32
    full = lambda shape: spec(shape, lambda i: (0,) * len(shape), True)
    place = lambda i: jnp.minimum(i, 2 * tn - 1 - i)
    back = lambda i: jnp.minimum(2 * tn - 1 - i, tn - 1)
    return pl.pallas_call(
        middle_kernel,
        grid=(2 * tn,),
        in_specs=[
            pl.BlockSpec(memory_space=pl.ANY),
            pl.BlockSpec(memory_space=pl.ANY),
            spec((tn, gn, per, dt), lambda i: (0, 0, 0, 2 * ff // dt), True),
            spec((1, gn, per, ff), lambda i: (place(i), 0, 0, 0)),
            spec((1, gn, per, ff), lambda i: (place(i), 0, 0, 1)),
            spec((1, 1, ff), lambda i: (place(i), 0, 0)),
            full((6, D)),
            full((gn, tn, lg, dt)),
        ],
        out_specs=[
            full((gn, tn, lg, dt)),
            spec((gn, 1, per, 2 * ff), lambda i: (0, back(i), 0, 0)),
            spec((1, 8, ff), lambda i: (back(i), 0, 0)),
            full((L, D)),
            full((48, D)),
        ],
        out_shape=[
            jax.ShapeDtypeStruct((gn, tn, lg, dt), bf),
            jax.ShapeDtypeStruct((gn, tn, per, wide), bf),
            jax.ShapeDtypeStruct((tn, 8, ff), f32),
            jax.ShapeDtypeStruct((L, D), bf),
            jax.ShapeDtypeStruct((48, D), f32),
        ],
        scratch_shapes=[
            pltpu.VMEM((tn, L, ff), bf), pltpu.VMEM((tn, L, ff), bf),
            pltpu.VMEM((L, D), bf), pltpu.VMEM((D, L), bf), pltpu.VMEM((L, 128), bf),
            pltpu.VMEM((L, D), bf), pltpu.VMEM((L, D), f32),
            pltpu.SemaphoreType.DMA((2 * (D // ff),)),
        ],
        compiler_params=pltpu.CompilerParams(vmem_limit_bytes=61 << 20),
        cost_estimate=pl.CostEstimate(flops=75 * 10**9, bytes_accessed=100 * 10**6, transcendentals=0),
    )(ctx, x, second, second, second, hidden_bias, vectors, cot)


def merge_back_kernel(da_ref, ctx_ref, wm_ref, pay_in, pay_ref, dctx_ref, dat_ref):
    t = pl.program_id(0)
    L, D = da_ref.shape
    gn, _, per, dt = pay_ref.shape

    @pl.when(t == 0)
    def _():
        for r in range(0, L, RB):
            dat_ref[:, r : r + RB] = da_ref[r : r + RB].T

    dctx_ref[...] = dotnn(da_ref[...], wm_ref[0].reshape(D, dt)).astype(jnp.bfloat16)
    pay_ref[:, 0] = dotnn(dat_ref[...], ctx_ref[...]).astype(jnp.bfloat16).reshape(gn, per, dt)


def merge_back(dattn, ctx, second, payload):
    tn, gn, per, wide = second.shape
    L, D = dattn.shape
    dt = D // tn
    last = wide // dt - 1
    bf = jnp.bfloat16
    return pl.pallas_call(
        merge_back_kernel,
        grid=(tn,),
        in_specs=[
            spec((L, D), lambda t: (0, 0), True),
            spec((L, dt), lambda t: (0, t)),
            spec((1, gn, per, dt), lambda t: (t, 0, 0, last)),
            pl.BlockSpec(memory_space=pl.ANY),
        ],
        out_specs=[
            spec((gn, 1, per, dt), lambda t: (0, t, 0, last)),
            spec((L, dt), lambda t: (0, t)),
        ],
        out_shape=[
            jax.ShapeDtypeStruct((gn, tn, per, wide), bf),
            jax.ShapeDtypeStruct((L, D), bf),
        ],
        scratch_shapes=[pltpu.VMEM((D, L), bf)],
        input_output_aliases={3: 0},
        compiler_params=pltpu.CompilerParams(vmem_limit_bytes=50 << 20),
        cost_estimate=pl.CostEstimate(flops=4 * 10**9, bytes_accessed=10 * 10**6, transcendentals=0),
    )(dattn, ctx, second, payload)


def input_back_kernel(da_ref, dq_ref, dk_ref, dv_ref, wa_ref, wb_ref, dx_ref, acc_ref):
    t = pl.program_id(0)
    L, D = da_ref.shape
    gn, tn, lg, dt = dx_ref.shape
    per = D // gn

    @pl.when(t == 0)
    def _():
        acc_ref[...] = da_ref[...].astype(jnp.float32)

    w = [wa_ref[:, 0, j * per : (j + 1) * per, :].reshape(D, dt) for j in range(2)]
    w.append(wb_ref[:, 0].reshape(D, dt))
    tops = [dq_ref, dk_ref, dv_ref]
    for r in range(0, L, RB):
        acc_ref[r : r + RB] += sum(dotnt(tops[j][r : r + RB], w[j]) for j in range(3))

    @pl.when(t == pl.num_programs(0) - 1)
    def _():
        for g in range(gn):
            for s in range(tn):
                cols = slice(s * dt, (s + 1) * dt)
                dx_ref[g, s] = acc_ref[g * lg : (g + 1) * lg, cols].astype(jnp.bfloat16)


def input_back(dattn, dq, dk, dv, first, later):
    gn, tn, wide, dt = first.shape
    L, D = dattn.shape
    col = lambda: spec((L, dt), lambda t: (0, t))
    return pl.pallas_call(
        input_back_kernel,
        grid=(tn,),
        in_specs=[
            spec((L, D), lambda t: (0, 0), True),
            col(), col(), col(),
            spec((gn, 1, wide, dt), lambda t: (0, t, 0, 0)),
            spec((gn, 1, D // gn, dt), lambda t: (0, t, 0, 0)),
        ],
        out_specs=spec((gn, tn, L // gn, dt), lambda t: (0, 0, 0, 0), True),
        out_shape=jax.ShapeDtypeStruct((gn, tn, L // gn, dt), jnp.bfloat16),
        scratch_shapes=[pltpu.VMEM((L, D), jnp.float32)],
        compiler_params=pltpu.CompilerParams(vmem_limit_bytes=50 << 20),
        cost_estimate=pl.CostEstimate(flops=7 * 10**9, bytes_accessed=20 * 10**6, transcendentals=0),
    )(dattn, dq, dk, dv, first, later)


def tail_kernel(x_ref, rel_ref, hot_ref, dq_ref, dk_ref, dv_ref, dqf_ref, dkf_ref, sm_ref, w_ref, small_ref,
                pay_ref, xt_ref, ra_ref, *, first_shift):
    t = pl.program_id(0)
    L, D = x_ref.shape
    spans = rel_ref.shape[0]
    gn, tn, _, dt = pay_ref.shape
    per = D // gn
    rg = spans // gn
    sr = small_ref.shape[2]
    f32, bf = jnp.float32, jnp.bfloat16

    @pl.when(t == 0)
    def _():
        for r in range(0, L, RB):
            xt_ref[:, r : r + RB] = x_ref[r : r + RB].T
        for r in range(0, spans, RB):
            xt_ref[:, L + r : L + r + RB] = rel_ref[r : r + RB].T
        ra_ref[...] = jnp.zeros_like(ra_ref)

    w = [w_ref[:, 0, j * per : (j + 1) * per, :].reshape(D, dt) for j in range(2)]
    qp = dotnn(dqf_ref[...], hot_ref[...]).T
    kp = dotnn(dkf_ref[...], hot_ref[...]).T
    pos = [qp.astype(bf), kp.astype(bf)]
    tops = [dq_ref, dk_ref, dv_ref]
    rows = 3 * per + rg
    pay_ref[:, t, rows : rows + sr, :] = small_ref[0].astype(bf)
    for j in range(3):
        total = jnp.sum(sm_ref[8 * j : 8 * j + 8], axis=0, keepdims=True)
        if j < 2:
            total = total + jnp.sum((qp, kp)[j], axis=0, keepdims=True)
            both = jnp.concatenate([tops[j][...], pos[j]], axis=0)
            grad = dotnn(xt_ref[...], both)
            ra_ref[...] += dotnt(pos[j], w[j])
        else:
            grad = dotnn(xt_ref[:, 0:L], tops[j][...])
        pay_ref[:, t, j * per : (j + 1) * per, :] = grad.astype(bf).reshape(gn, per, dt)
        at = first_shift + j
        pay_ref[at // sr, t, rows + at % sr : rows + at % sr + 1, :] = total.astype(bf)
    @pl.when(t == pl.num_programs(0) - 1)
    def _():
        for g in range(gn):
            for s in range(tn):
                cols = slice(s * dt, (s + 1) * dt)
                pay_ref[g, s, 3 * per : rows, :] = ra_ref[g * rg : (g + 1) * rg, cols].astype(bf)


def tail(x, rel, hot, dq, dk, dv, dqf, dkf, sums, first, small, first_shift):
    gn, tn, wide, dt = first.shape
    L, D = x.shape
    spans = rel.shape[0]
    rows = 3 * D // gn + spans // gn + small.shape[2]
    bf, f32 = jnp.bfloat16, jnp.float32
    full = lambda shape: spec(shape, lambda t: (0,) * len(shape), True)
    col = lambda: spec((L, dt), lambda t: (0, t))
    return pl.pallas_call(
        functools.partial(tail_kernel, first_shift=first_shift),
        grid=(tn,),
        in_specs=[
            full((L, D)), full((spans, D)), full((2 * L, spans)),
            col(), col(), col(),
            spec((dt, 2 * L), lambda t: (t, 0)), spec((dt, 2 * L), lambda t: (t, 0)),
            spec((24, dt), lambda t: (0, t)),
            spec((gn, 1, wide, dt), lambda t: (0, t, 0, 0)),
            spec((1,) + small.shape[1:], lambda t: (t, 0, 0, 0)),
        ],
        out_specs=full((gn, tn, rows, dt)),
        out_shape=jax.ShapeDtypeStruct((gn, tn, rows, dt), bf),
        scratch_shapes=[pltpu.VMEM((D, L + spans), bf), pltpu.VMEM((spans, D), f32)],
        compiler_params=pltpu.CompilerParams(vmem_limit_bytes=56 << 20),
        cost_estimate=pl.CostEstimate(flops=13 * 10**9, bytes_accessed=40 * 10**6, transcendentals=0),
    )(x, rel, hot, dq, dk, dv, dqf, dkf, sums, first, small)


MESH = pl.DeviceIdType.MESH


def bit_of(place, i):
    return (place // (1 << i)) % 2


def flipped(place, flips):
    for i in flips:
        place = place + (1 << i) * (1 - 2 * bit_of(place, i))
    return place


def subsets(bits):
    out = [()]
    for i in bits:
        out += [s + (i,) for s in out]
    return out


def greet(tn, gn):
    t, g = lax.axis_index("tensor"), lax.axis_index("dp")
    barrier = pltpu.get_barrier_semaphore()
    bits = list(range(gn.bit_length() - 1))
    for d in range(1, tn):
        pl.semaphore_signal(barrier, inc=1, device_id={"tensor": lax.rem(t + d, tn)}, device_id_type=MESH)
    for i in bits:
        pl.semaphore_signal(barrier, inc=1, device_id={"dp": flipped(g, (i,))}, device_id_type=MESH)
    pl.semaphore_wait(barrier, tn - 1 + len(bits))


class Wire:
    def __init__(self, send, recv):
        self.send, self.recv, self.at = send, recv, 0

    def push(self, src, dst, **device):
        c = pltpu.make_async_remote_copy(
            src, dst, self.send.at[self.at], self.recv.at[self.at], device_id=device, device_id_type=MESH
        )
        self.at += 1
        c.start()
        return c


def run_waves(chunks):
    waves = max(len(stages) + c for c, stages in enumerate(chunks)) + 1
    flight = {}
    for w in range(waves):
        for c, stages in enumerate(chunks):
            s = w - c
            if 0 < s <= len(stages):
                stages[s - 1][1](flight.pop((c, s - 1)))
            if 0 <= s < len(stages):
                flight[c, s] = stages[s][0]()


def wait_all(copies):
    for c in copies:
        c.wait()


def spread_stages(src, out, local, wire, tn, gn):
    t, g = lax.axis_index("tensor"), lax.axis_index("dp")
    bits = list(range(gn.bit_length() - 1))
    half = tn // 2
    plans = [(0, bits[1:] + bits[:1]), (half, bits[:0:-1] + bits[:1])]

    def first():
        own = pltpu.make_async_copy(src(), out(g, pl.ds(t, 1)), local)
        own.start()
        copies = [
            wire.push(src(), out(g, pl.ds(t, 1)), tensor=lax.rem(t + d, tn)) for d in range(1, tn)
        ]
        return [own] + copies

    def later(step):
        def start():
            copies = []
            for lo, plan in plans:
                for s in subsets(plan[:step]):
                    part = out(flipped(g, s), pl.ds(lo, half))
                    copies.append(wire.push(part, part, dp=flipped(g, (plan[step],))))
            return copies

        return start

    return [(first, wait_all)] + [(later(step), wait_all) for step in range(len(bits))]


def spread_count(tn, gn):
    return tn - 1 + 2 * (gn - 1)


def gather_kernel(src_ref, out_ref, local, send, recv, *, tn, gn, cuts):
    greet(tn, gn)
    wire = Wire(send, recv)
    chunks = []
    for n, (lo, hi) in enumerate(cuts):
        rows = pl.ds(lo, hi - lo)
        chunks.append(
            spread_stages(
                lambda rows=rows: src_ref.at[:, rows],
                lambda g, s, rows=rows: out_ref.at[g, s, rows],
                local.at[n], wire, tn, gn,
            )
        )
    run_waves(chunks)


def gather_all(w, tn, gn, number):
    rows = w.shape[0]
    mid = rows // 32 * 16
    cuts = [(0, mid), (mid, rows)]
    n = spread_count(tn, gn) * len(cuts)
    dma = lambda k: pltpu.SemaphoreType.DMA((k,))
    return pl.pallas_call(
        functools.partial(gather_kernel, tn=tn, gn=gn, cuts=cuts),
        in_specs=[pl.BlockSpec(memory_space=pl.ANY)],
        out_specs=pl.BlockSpec(memory_space=pl.ANY),
        out_shape=jax.ShapeDtypeStruct((gn, tn) + w.shape, w.dtype),
        scratch_shapes=[dma(len(cuts)), dma(n), dma(n)],
        compiler_params=pltpu.CompilerParams(collective_id=number, has_side_effects=True),
        cost_estimate=pl.CostEstimate(flops=0, bytes_accessed=w.size * tn * gn * 16, transcendentals=0),
    )(w[None])


def reduce_kernel(pay_ref, q_ref, k_ref, v_ref, rel_ref, small_ref, all_ref, acc_ref, rx_ref, ry_ref, rz_ref, rest_ref,
                  local, send, recv, *, tn, gn, keep):
    t, g = lax.axis_index("tensor"), lax.axis_index("dp")
    bits = list(range(gn.bit_length() - 1))
    f32, bf = jnp.float32, jnp.bfloat16
    rows = acc_ref.shape[2]
    per = keep // 3
    greet(tn, gn)
    wire = Wire(send, recv)
    outer = bits[1:]
    masks = subsets(outer)
    index = {s: n for n, s in enumerate(masks)}
    half = tn // 2
    plans = [(0, outer), (half, outer[::-1])]
    grads = (q_ref, k_ref, v_ref)

    def reduce_stages(n, lo, hi):
        span = pl.ds(lo, hi - lo)

        def add(dst, first, size, src_ref, slot):
            for i in range(size):
                acc_ref[dst, first + i, lo:hi] = (
                    acc_ref[dst, first + i, lo:hi].astype(f32) + src_ref[slot, i, lo:hi].astype(f32)
                ).astype(bf)

        def first():
            copies = []
            for i, s in enumerate(masks):
                copies.append(wire.push(pay_ref.at[flipped(g, (0,) + s), :, span], rx_ref.at[i, :, span], dp=flipped(g, (0,))))
            for i, s in enumerate(masks):
                c = pltpu.make_async_copy(pay_ref.at[flipped(g, s), :, span], acc_ref.at[i, :, span], local.at[n, i])
                c.start()
                copies.append(c)
            return copies

        def first_done(copies):
            for i in range(len(masks)):
                copies[len(masks) + i].wait()
                copies[i].wait()
                add(i, 0, tn, rx_ref, i)

        def outer_stage(step, base):
            def start():
                flight = []
                slot = base
                for place, plan in plans:
                    bit = plan[step]
                    for s in masks:
                        if any(i in plan[: step + 1] for i in s):
                            continue
                        src = tuple(i for i in outer if i in s or i == bit)
                        c = wire.push(
                            acc_ref.at[index[src], pl.ds(place, half), span], ry_ref.at[slot, :, span],
                            dp=flipped(g, (bit,)),
                        )
                        flight.append((c, index[s], place, slot))
                        slot += 1
                return flight

            def done(flight):
                for c, dst, place, slot in flight:
                    c.wait()
                    add(dst, place, half, ry_ref, slot)

            return start, done

        def last():
            return [
                wire.push(acc_ref.at[0, lax.rem(t + d, tn), span], rz_ref.at[d - 1, span], tensor=lax.rem(t + d, tn))
                for d in range(1, tn)
            ]

        def last_done(copies):
            total = acc_ref[0, t, lo:hi].astype(f32)
            for d, c in enumerate(copies):
                c.wait()
                total = total + rz_ref[d, lo:hi].astype(f32)
            if lo >= keep:
                rest_ref[0] = total.astype(bf)
            else:
                for j in range(3):
                    a, b = max(lo, j * per), min(hi, (j + 1) * per)
                    if a < b:
                        grads[j][a - j * per : b - j * per] = total[a - lo : b - lo]

        stages = [(first, first_done)]
        base = 0
        for step in range(len(outer)):
            stages.append(outer_stage(step, base))
            base += 2 * (gn // 4 >> step)
        return stages + [(last, last_done)]

    cut = keep // 32 * 16
    chunks = [
        reduce_stages(0, keep, rows)
        + spread_stages(
            lambda: rest_ref, lambda i, s: all_ref.at[i, s], local.at[3, 0], wire, tn, gn
        ),
        reduce_stages(1, 0, cut),
        reduce_stages(2, cut, keep),
    ]
    run_waves(chunks)
    dt = q_ref.shape[1]
    rg = rel_ref.shape[0] // gn
    for s in range(tn):
        cols = slice(s * dt, (s + 1) * dt)
        for i in range(gn):
            rel_ref[i * rg : (i + 1) * rg, cols] = all_ref[i, s, :rg].astype(f32)
        small_ref[:, cols] = all_ref[0, s, rg:].astype(f32)


def reduce_all(pay, keep, spans, number):
    gn, tn, rows, dt = pay.shape
    bf, f32 = jnp.bfloat16, jnp.float32
    m = gn // 2
    pieces = 2 * (m - 1)
    count = 3 * (m + pieces + tn - 1) + spread_count(tn, gn)
    dma = lambda *k: pltpu.SemaphoreType.DMA(k)
    return pl.pallas_call(
        functools.partial(reduce_kernel, tn=tn, gn=gn, keep=keep),
        in_specs=[pl.BlockSpec(memory_space=pltpu.VMEM)],
        out_specs=[pl.BlockSpec(memory_space=pltpu.VMEM)] * 5,
        out_shape=[jax.ShapeDtypeStruct((keep // 3, dt), f32)] * 3
        + [
            jax.ShapeDtypeStruct((spans, tn * dt), f32),
            jax.ShapeDtypeStruct((rows - keep - spans // gn, tn * dt), f32),
        ],
        scratch_shapes=[
            pltpu.VMEM((gn, tn, rows - keep, dt), bf),
            pltpu.VMEM((m, tn, rows, dt), bf),
            pltpu.VMEM((m, tn, rows, dt), bf),
            pltpu.VMEM((pieces, tn // 2, rows, dt), bf),
            pltpu.VMEM((tn - 1, rows, dt), bf),
            pltpu.VMEM((1, rows - keep, dt), bf),
            dma(4, m), dma(count), dma(count),
        ],
        compiler_params=pltpu.CompilerParams(collective_id=number, has_side_effects=True, vmem_limit_bytes=40 << 20),
        cost_estimate=pl.CostEstimate(flops=0, bytes_accessed=200 * 10**6, transcendentals=0),
    )(pay)


def shards(
    inputs,
    cotangent,
    lengths,
    dealing,
    buckets,
    rel_embed,
    query_weight,
    key_weight,
    value_weight,
    proj_shifts,
    merge_weight,
    inner_weight,
    hidden_shift,
    outer_weight,
    layer_vectors,
):
    tn = lax.axis_size("tensor")
    gn = lax.axis_size("dp")
    me = lax.axis_index("dp") * tn + lax.axis_index("tensor")
    count, lg, dt = inputs.shape
    L, D = lg * gn, dt * tn
    per = query_weight.shape[0]
    rg = rel_embed.shape[0]
    spans = rg * gn
    assert count == tn * gn
    bf = jnp.bfloat16
    f32 = jnp.float32
    scale = 1.0 / math.sqrt(3.0 * HEAD)
    seq_axes = ("dp", "tensor")
    w_axes = ("tensor", "dp")

    def swap(a):
        return lax.all_to_all(a, seq_axes, split_axis=0, concat_axis=0, tiled=True)

    def gather(w):
        return lax.all_gather(w, w_axes, axis=0, tiled=False).reshape((tn, gn) + w.shape)

    rel_cols = lax.dynamic_slice_in_dim(rel_embed, lax.axis_index("tensor") * dt, dt, 1)
    early = jnp.concatenate([query_weight, key_weight], axis=0)
    late = jnp.concatenate(
        [value_weight, rel_cols, proj_shifts, hidden_shift.reshape(-1, dt), jnp.zeros((1, dt), bf)], axis=0
    )
    first = gather_all(early, tn, gn, 0)
    xd = swap(inputs).reshape(gn, tn, lg, dt)
    wide = jnp.concatenate([inner_weight, outer_weight, merge_weight], axis=1)
    first, xd, late, wide, cotangent = lax.optimization_barrier((first, xd, late, wide, cotangent))
    second = gather(wide)
    later = gather_all(late, tn, gn, 2)
    cot = swap(cotangent).reshape(gn, tn, lg, dt)
    biases = later[0, :, per + rg :].astype(f32)
    shifts = biases[:, :3]
    hidden_bias = biases[:, 3:7].reshape(tn, 1, -1)
    vectors = layer_vectors.astype(f32)
    length = jnp.sum(jnp.where(dealing == me, lengths, 0)).reshape(1)
    places = jnp.concatenate([buckets[::-1], jnp.full((1,), -1, jnp.int32)])[:, None]

    qkv, far, x, rel, hot = project(xd, first, later, shifts, places, per)
    ctx, probs, inv = attn_fwd(length, qkv, far, scale=scale)
    y, payload, hidden, dattn, sums12 = middle(ctx, x, second, hidden_bias, vectors, cot)
    out = swap(y.reshape(count, lg, dt))
    payload, dctx = merge_back(dattn, ctx, second, payload)
    wide_grads = lax.psum_scatter(payload, "dp", scatter_dimension=0, tiled=False)
    dq, dk, dv, dkf, dqf, sums = attn_bwd(probs, qkv, dctx, ctx, inv, far, scale=scale)
    dq, out = lax.optimization_barrier((dq, out))
    ff = hidden.shape[2]
    small = jnp.concatenate(
        [
            jnp.sum(sums12.reshape(6, 8, D), axis=1),
            jnp.sum(hidden, axis=1).reshape(-1, D),
        ],
        axis=0,
    )
    first_shift = small.shape[0]
    sr = 16
    small = jnp.pad(small, ((0, sr - first_shift), (0, 0)))
    small = small.reshape(sr, tn, dt).transpose(1, 0, 2)[:, None]
    small = jnp.pad(small, ((0, 0), (0, gn - 1), (0, 0), (0, 0)))
    dx = input_back(dattn, dq, dk, dv, first, later)
    dx, dq, wide_grads = lax.optimization_barrier((dx, dq, wide_grads))
    wide_grads = lax.psum_scatter(wide_grads, "tensor", scatter_dimension=0, tiled=False)
    pay = tail(x, rel, hot, dq, dk, dv, dqf, dkf, sums, first, small, first_shift)
    grad_in = swap(dx.reshape(count, lg, dt))
    wide_grads = wide_grads.astype(f32)
    query_grad, key_grad, value_grad, rel_grad, rest = reduce_all(pay, 3 * per, spans, 1)
    return (
        out,
        grad_in,
        rel_grad,
        query_grad,
        key_grad,
        value_grad,
        rest[first_shift : first_shift + 3],
        wide_grads[:, 2 * ff :],
        wide_grads[:, :ff],
        rest[6:first_shift].reshape(-1),
        wide_grads[:, ff : 2 * ff],
        rest[:6],
    )


def solution(mesh):
    split = P("dp", "tensor")
    whole = P(None, "dp", "tensor")
    in_specs = (
        whole, whole, P(), P(), P(), P("dp", None), split, split, split, P(None, "tensor"),
        split, split, P("tensor"), split, P(),
    )
    out_specs = (whole, whole, P(), split, split, split, P(), split, split, P(), split, P())
    return jax.shard_map(shards, mesh=mesh, in_specs=in_specs, out_specs=out_specs, check_vma=False)
```

```python
import functools
import math

import jax
import jax.numpy as jnp
from jax import lax
from jax.experimental import pallas as pl
from jax.experimental.pallas import tpu as pltpu
from jax.sharding import PartitionSpec as P

EPSILON = 1e-07
HEAD = 64
B = 128
SR = 16
NT = (((1,), (1,)), ((), ()))


def dotnt(a, b):
    return lax.dot_general(a, b, NT, preferred_element_type=jnp.float32)


def dotnn(a, b):
    return lax.dot_general(a, b, (((1,), (0,)), ((), ())), preferred_element_type=jnp.float32)


def skew(g_ref, a, n, L):
    parts=[]
    nb=L//B
    for a8 in range(a,a+n,8):
        rot=[pltpu.roll(g_ref[a8:a8+8,t*128:t*128+128], 1+a8, 1, stride=1, stride_axis=0) for t in range(nb+1)]
        msk=lax.broadcasted_iota(jnp.int32,(8,128),1) < (1+a8+lax.broadcasted_iota(jnp.int32,(8,128),0))
        parts.append(jnp.concatenate([jnp.where(msk,rot[t],rot[t+1]) for t in range(nb)],axis=1))
    return jnp.concatenate(parts,axis=0)

def fwd_kernel(len_ref, q_ref, k_ref, v_ref, kf_ref, qf_ref, ctx_ref, p_ref, l_ref, t_ref, kx_ref, vx_ref, g0, g1, s0, s1, *, L, scale):
    W = L + B
    nb = L // B
    gs=(g0,g1); ss=(s0,s1)
    lane = lax.broadcasted_iota(jnp.int32, (1, 128), 1)
    length = len_ref[0]
    row = lax.broadcasted_iota(jnp.int32, (L, 128), 0)
    c2 = scale * math.log2(math.e)
    eye = (lax.broadcasted_iota(jnp.int32,(B,B),0)==lax.broadcasted_iota(jnp.int32,(B,B),1)).astype(jnp.bfloat16)
    zero = jnp.zeros((), jnp.bfloat16)
    mine = [lane < 64, lane >= 64]
    first_other = [lane==64, lane==0]
    for h in range(2):
        bias = jnp.where((row >= length) & first_other[h], -1e30, 0.0).astype(jnp.bfloat16)
        kx_ref[h] = jnp.where(mine[h], k_ref[...], bias)
        vx_ref[h] = jnp.where(mine[h], v_ref[...], jnp.ones((), jnp.bfloat16))
    def tblock(b, _):
        r0 = pl.multiple_of(b*B, B)
        base = pl.multiple_of(L - B - b*B, B)
        for h in range(2):
            kb = jnp.where(mine[h], k_ref[pl.ds(r0,B),:], zero)
            gs[h][...] = dotnt(kb, qf_ref[pl.ds(base, W), :])
        for h in range(2):
            for a in range(0, B, SR):
                t_ref[h, pl.ds(r0+a,SR), :] = skew(gs[h], a, SR, L).astype(jnp.bfloat16)
        return 0
    lax.fori_loop(0, nb, tblock, 0, unroll=2)
    def scores(b, h):
        r0 = pl.multiple_of(b*B, B)
        base = pl.multiple_of(L - B - b*B, B)
        qb = q_ref[pl.ds(r0,B),:]
        qm = jnp.where(mine[h], qb, zero)
        qx = jnp.where(mine[h], qb, first_other[h].astype(jnp.bfloat16))
        gs[h][...] = dotnt(qm, kf_ref[pl.ds(base, W), :])
        lhs = jnp.concatenate([qx, eye], axis=1)
        rhs = jnp.concatenate([kx_ref[h], t_ref[h, :, pl.ds(r0,B)]], axis=1)
        ss[h][...] = dotnt(lhs, rhs)
    def soft(b, h):
        r0 = pl.multiple_of(b*B, B)
        tops=[]
        for a in range(0, B, 8):
            s = ss[h][a:a+8] + skew(gs[h], a, 8, L)
            ss[h][a:a+8] = s
            tops.append(functools.reduce(jnp.maximum,[s[:,t*128:t*128+128] for t in range(nb)]))
        m = jnp.max(jnp.concatenate(tops,axis=0), axis=1, keepdims=True) * c2
        for a in range(0, B, SR):
            p_ref[h, pl.ds(r0+a,SR), :] = jnp.exp2(ss[h][a:a+SR]*c2 - m[a:a+SR]).astype(jnp.bfloat16)
    def out(b, h):
        r0 = pl.multiple_of(b*B, B)
        return dotnn(p_ref[h, pl.ds(r0,B), :], vx_ref[h])
    def finish(b, o0, o1):
        r0 = pl.multiple_of(b*B, B)
        num = jnp.where(mine[0], o0, o1)
        den = jnp.where(mine[0], pltpu.roll(o0,64,1), pltpu.roll(o1,64,1))
        inv = 1.0/den
        ctx_ref[pl.ds(r0,B),:] = (num*inv).astype(jnp.bfloat16)
        l_ref[pl.ds(r0,B),:] = inv
    scores(0,0)
    def sblock(b, o0):
        scores(b,1)
        soft(b,0)
        o0 = out(b,0)
        scores(jnp.minimum(b+1,nb-1),0)
        soft(b,1)
        o1 = out(b,1)
        finish(b,o0,o1)
        return 0
    lax.fori_loop(0, nb, sblock, 0, unroll=8)


def attn_fwd(length, qkv, far, *, scale):
    _, L, C = qkv.shape
    part = lambda j, r: pl.BlockSpec((None, r, 128), lambda h, *_: (j, 0, h))
    return pl.pallas_call(
        functools.partial(fwd_kernel, L=L, scale=scale),
        grid_spec=pltpu.PrefetchScalarGridSpec(
            num_scalar_prefetch=1,
            grid=(C // 128,),
            in_specs=[part(0, L), part(1, L), part(2, L), part(1, 2 * L), part(0, 2 * L)],
            out_specs=[
                pl.BlockSpec((L, 128), lambda h, *_: (0, h)),
                pl.BlockSpec((2, L, L), lambda h, *_: (h, 0, 0)),
                pl.BlockSpec((L, 128), lambda h, *_: (0, h)),
            ],
            scratch_shapes=[pltpu.VMEM((2, L, L), jnp.bfloat16)]
            + [pltpu.VMEM((2, L, 128), jnp.bfloat16)] * 2
            + [pltpu.VMEM((B, L + B), jnp.float32)] * 2
            + [pltpu.VMEM((B, L), jnp.float32)] * 2,
        ),
        out_shape=[
            jax.ShapeDtypeStruct((L, C), jnp.bfloat16),
            jax.ShapeDtypeStruct((C // HEAD, L, L), jnp.bfloat16),
            jax.ShapeDtypeStruct((L, C), jnp.float32),
        ],
        compiler_params=pltpu.CompilerParams(vmem_limit_bytes=50 << 20),
        cost_estimate=pl.CostEstimate(flops=80 * 10**9, bytes_accessed=60 * 10**6, transcendentals=0),
    )(length, qkv, qkv, qkv, far, far)


FAR = 3


def unskew(x, a8):
    nb = x.shape[1] // B
    sub = lax.broadcasted_iota(jnp.int32, (8, 128), 0)
    lane = lax.broadcasted_iota(jnp.int32, (8, 128), 1)
    keep = lane >= (127 - a8) - sub
    idx = (lane - (127 - a8) + sub) & 127
    rot = [jnp.take_along_axis(x[:, t * 128 : t * 128 + 128], idx, axis=1) for t in range(nb)]
    zero = jnp.zeros((8, 128), x.dtype)
    return jnp.concatenate(
        [jnp.where(keep, rot[t] if t < nb else zero, rot[t - 1] if t > 0 else zero) for t in range(nb + 1)], axis=1
    )


def fold_tiles(x, lo, hi):
    return sum(x[:, t * 128 : t * 128 + 128] for t in range(lo, hi))


def place_back(rows8, d_ref, a, b, nb):
    lo, hi = max(0, b - FAR), min(nb, b + FAR + 1)
    near = jnp.concatenate([unskew(x[:, lo * 128 : hi * 128], a + 8 * n) for n, x in enumerate(rows8)], axis=0)
    d_ref[a : a + SR, 256 : 256 + near.shape[1]] = near.astype(jnp.bfloat16)
    if lo > 0:
        far = jnp.concatenate([fold_tiles(x, 0, lo) for x in rows8], axis=0)
        d_ref[a : a + SR, 0:128] = far.astype(jnp.bfloat16)
    if hi < nb:
        far = jnp.concatenate([fold_tiles(x, hi, nb) for x in rows8], axis=0)
        d_ref[a : a + SR, 128:256] = far.astype(jnp.bfloat16)


def window_products(d_ref, table_ref, ends_ref, e, lhs, acc_ref, sums_ref, rows, b, nb):
    lo, hi = max(0, b - FAR), min(nb, b + FAR + 1)
    base, size = (nb - 1 - b + lo) * B, (hi - lo + 1) * B
    near = d_ref[:, 256 : 256 + size]
    out = dotnn(near, table_ref[base : base + size, :])
    acc_ref[rows, base : base + size] += dotnn(lhs, near)
    for there, k in ((lo > 0, 0), (hi < nb, 1)):
        if there:
            far = d_ref[:, k * 128 : k * 128 + 128]
            out = out + dotnn(far, ends_ref[e + k])
            sums_ref[e + k, rows, :] += dotnn(lhs, far)
    return out


def bwd_kernel(p_ref, q_ref, k_ref, v_ref, do_ref, ctx_ref, li_ref, kf_ref, qf_ref,
               dq_ref, dk_ref, dv_ref, dkf_ref, dqf_ref, sums_ref,
               dox_ref, dot_ref, qt_ref, kt_ref, vx_ref, ds_ref, d0, d1, akf, aqf, ends, far, *, L, scale):
    W = L + B
    nb = L // B
    dd=(d0,d1)
    lane = lax.broadcasted_iota(jnp.int32, (1, 128), 1)
    mine = [lane < 64, lane >= 64]
    base_lane = [64, 0]
    dos = (do_ref[...].astype(jnp.float32) * li_ref[...]).astype(jnp.bfloat16)
    prod = dos.astype(jnp.float32) * ctx_ref[...].astype(jnp.float32)
    for h in range(2):
        delta = -jnp.sum(jnp.where(mine[h], prod, 0.0), axis=1, keepdims=True)
        hi = delta.astype(jnp.bfloat16).astype(jnp.float32)
        lo = delta - hi
        extra = jnp.where(lane == base_lane[h], hi, jnp.where(lane == base_lane[h]+1, lo, 0.0)).astype(jnp.bfloat16)
        dox_ref[h] = jnp.where(mine[h], dos, extra)
        vx_ref[h] = jnp.where(mine[h], v_ref[...], jnp.ones((), jnp.bfloat16))
    dot_ref[...] = dos.T
    qt_ref[...] = q_ref[...].T
    kt_ref[...] = k_ref[...].T
    akf[...] = jnp.zeros_like(akf)
    aqf[...] = jnp.zeros_like(aqf)
    far[...] = jnp.zeros_like(far)
    last = 2 * L - 2
    for e, table in ((0, kf_ref), (2, qf_ref)):
        ends[e] = jnp.broadcast_to(table[0:1, :], (128, 128))
        ends[e + 1] = jnp.broadcast_to(table[last : last + 1, :], (128, 128))
    sq = jnp.zeros((8, 128), jnp.float32)
    for b in range(nb):
        r0 = b * B
        outs = []
        for h in range(2):
            rows = slice(h * 64, h * 64 + 64)
            dp = dotnt(dox_ref[h, r0 : r0 + B, :], vx_ref[h])
            for a in range(0, B, SR):
                ds = p_ref[h, r0 + a : r0 + a + SR, :].astype(jnp.float32) * dp[a : a + SR]
                ds_ref[h, r0 + a : r0 + a + SR, :] = ds.astype(jnp.bfloat16)
                place_back([ds[s : s + 8] for s in range(0, SR, 8)], dd[h], a, b, nb)
            outs.append(
                dotnn(ds_ref[h, r0 : r0 + B, :], k_ref[...])
                + window_products(dd[h], kf_ref, ends, 0, qt_ref[rows, r0 : r0 + B], akf, far, rows, b, nb)
            )
        dq = jnp.where(mine[0], outs[0], outs[1]) * scale
        dq_ref[r0 : r0 + B, :] = dq.astype(jnp.bfloat16)
        sq = sq + jnp.sum(dq.reshape(B // 8, 8, 128), axis=0)
    sk = jnp.zeros((8, 128), jnp.float32)
    for b in range(nb):
        r0 = b * B
        outs = []
        for h in range(2):
            rows = slice(h * 64, h * 64 + 64)
            dst = ds_ref[h, :, r0 : r0 + B].T
            for a in range(0, B, SR):
                x = dst[a : a + SR].astype(jnp.float32)
                place_back([x[s : s + 8] for s in range(0, SR, 8)], dd[h], a, b, nb)
            outs.append(
                dotnn(dst, q_ref[...])
                + window_products(dd[h], qf_ref, ends, 2, kt_ref[rows, r0 : r0 + B], aqf, far, rows, b, nb)
            )
        dk = jnp.where(mine[0], outs[0], outs[1]) * scale
        dk_ref[r0 : r0 + B, :] = dk.astype(jnp.bfloat16)
        sk = sk + jnp.sum(dk.reshape(B // 8, 8, 128), axis=0)
    for e, acc in ((0, akf), (2, aqf)):
        for k, at in ((0, 0), (1, last)):
            tile = at // 128 * 128
            total = jnp.sum(far[e + k], axis=1, keepdims=True)
            acc[:, tile : tile + 128] += jnp.where(lane == at - tile, total, 0.0)
    dvt = jnp.concatenate([dotnn(dot_ref[h*64:h*64+64,:], p_ref[h]) for h in range(2)], axis=0)
    dv = dvt.T
    dv_ref[...] = dv.astype(jnp.bfloat16)
    sv = jnp.sum(dv.reshape(L//8,8,128), axis=0)
    sums_ref[0:8] = sq
    sums_ref[8:16] = sk
    sums_ref[16:24] = sv
    dkf_ref[...] = (akf[...]*scale).astype(jnp.bfloat16)
    dqf_ref[...] = (aqf[...]*scale).astype(jnp.bfloat16)


def attn_bwd(p, qkv, do, ctx, linv, far, *, scale):
    _, L, C = qkv.shape
    bf = jnp.bfloat16
    part = lambda j, r: pl.BlockSpec((None, r, 128), lambda h: (j, 0, h))
    col = lambda r: pl.BlockSpec((r, 128), lambda h: (0, h))
    rowb = pl.BlockSpec((128, 2 * L), lambda h: (h, 0))
    return pl.pallas_call(
        functools.partial(bwd_kernel, L=L, scale=scale),
        grid=(C // 128,),
        in_specs=[pl.BlockSpec((2, L, L), lambda h: (h, 0, 0)), part(0, L), part(1, L), part(2, L)]
        + [col(L)] * 3
        + [part(1, 2 * L), part(0, 2 * L)],
        out_specs=[col(L)] * 3 + [rowb] * 2 + [col(24)],
        scratch_shapes=[pltpu.VMEM((2, L, 128), bf)]
        + [pltpu.VMEM((128, L), bf)] * 3
        + [pltpu.VMEM((2, L, 128), bf), pltpu.VMEM((2, L, L), bf)]
        + [pltpu.VMEM((B, L + 3 * B), bf)] * 2
        + [pltpu.VMEM((128, 2 * L), jnp.float32)] * 2
        + [pltpu.VMEM((4, 128, 128), bf), pltpu.VMEM((4, 128, 128), jnp.float32)],
        out_shape=[jax.ShapeDtypeStruct((L, C), bf)] * 3
        + [jax.ShapeDtypeStruct((C, 2 * L), bf)] * 2
        + [jax.ShapeDtypeStruct((24, C), jnp.float32)],
        compiler_params=pltpu.CompilerParams(vmem_limit_bytes=56 << 20),
        cost_estimate=pl.CostEstimate(flops=120 * 10**9, bytes_accessed=80 * 10**6, transcendentals=0),
    )(p, qkv, qkv, qkv, do, ctx, linv, far, far)


def spec(block, index, once=False):
    if once:
        return pl.BlockSpec(block, index, pipeline_mode=pl.Buffered(1))
    return pl.BlockSpec(block, index)


def norm_rows(z):
    center = z - jnp.mean(z, axis=-1, keepdims=True)
    r = lax.rsqrt(jnp.mean(center * center, axis=-1, keepdims=True) + EPSILON)
    return center * r, r


def norm_back(g, n, r):
    return r * (g - jnp.mean(g, axis=-1, keepdims=True) - n * jnp.mean(g * n, axis=-1, keepdims=True))


def fold8(v):
    return jnp.sum(v.reshape(v.shape[0] // 8, 8, v.shape[1]), axis=0)


def project_kernel(xd_ref, rel4_ref, wa_ref, wb_ref, sh_ref, pl_ref, qkv_ref, far_ref, x_ref, rel_ref, hot_ref):
    t, j = pl.program_id(0), pl.program_id(1)
    gn, tn, lg, dt = xd_ref.shape
    spans = rel_ref.shape[0]
    rg = spans // gn

    @pl.when((t == 0) & (j == 0))
    def _():
        for g in range(gn):
            for s in range(tn):
                x_ref[g * lg : (g + 1) * lg, s * dt : (s + 1) * dt] = xd_ref[g, s]
                rel_ref[g * rg : (g + 1) * rg, s * dt : (s + 1) * dt] = rel4_ref[g, s]
        rows = hot_ref.shape[0]
        lanes = lax.broadcasted_iota(jnp.int32, (rows, spans), 1)
        hot_ref[...] = (pl_ref[...] == lanes).astype(jnp.float32).astype(jnp.bfloat16)

    w = jnp.where(j < 2, wa_ref[:, 0], wb_ref[:, 0]).reshape(x_ref.shape[1], dt)
    shift = sh_ref[0, pl.ds(j, 1), :]
    qkv_ref[0] = (dotnn(x_ref[...], w) + shift).astype(jnp.bfloat16)

    @pl.when(j < 2)
    def _():
        place = (dotnn(rel_ref[...], w) + shift).astype(jnp.bfloat16)
        far_ref[0] = dotnn(hot_ref[...], place).astype(jnp.bfloat16)


def project(xd, first, later, shifts, places, per):
    gn, tn, lg, dt = xd.shape
    L, D = gn * lg, tn * dt
    rg = later.shape[2] - per - 8
    spans = rg * gn
    bf = jnp.bfloat16
    return pl.pallas_call(
        project_kernel,
        grid=(tn, 3),
        in_specs=[
            spec((gn, tn, lg, dt), lambda t, j: (0, 0, 0, 0), True),
            spec((gn, tn, rg, dt), lambda t, j: (0, 0, per // rg, 0), True),
            spec((gn, 1, per, dt), lambda t, j: (0, t, jnp.minimum(j, 1), 0)),
            spec((gn, 1, per, dt), lambda t, j: (0, t, 0, 0)),
            spec((1, 3, dt), lambda t, j: (t, 0, 0)),
            spec((2 * L, 1), lambda t, j: (0, 0), True),
        ],
        out_specs=[
            spec((1, L, dt), lambda t, j: (j, 0, t)),
            spec((1, 2 * L, dt), lambda t, j: (jnp.minimum(j, 1), 0, t)),
            spec((L, D), lambda t, j: (0, 0)),
            spec((spans, D), lambda t, j: (0, 0)),
            spec((2 * L, spans), lambda t, j: (0, 0)),
        ],
        out_shape=[
            jax.ShapeDtypeStruct((3, L, D), bf),
            jax.ShapeDtypeStruct((2, 2 * L, D), bf),
            jax.ShapeDtypeStruct((L, D), bf),
            jax.ShapeDtypeStruct((spans, D), bf),
            jax.ShapeDtypeStruct((2 * L, spans), bf),
        ],
        compiler_params=pltpu.CompilerParams(vmem_limit_bytes=50 << 20),
        cost_estimate=pl.CostEstimate(flops=14 * 10**9, bytes_accessed=30 * 10**6, transcendentals=0),
    )(xd, later, first, later, shifts, places)


RB = 256


MB = 256


def middle_kernel(ctx_ref, x_ref, wm_ref, wi_ref, wo_ref, hb_ref, vec_ref, cot_ref,
                  y_ref, pay_ref, hid_ref, da_ref, sums_ref,
                  act_ref, slope_ref, hl_ref, hlt_ref, r1_ref, df_ref, acc_ref, sem):
    step = pl.program_id(0)
    L, D = x_ref.shape
    gn, tn, lg, dt = cot_ref.shape
    _, _, per, ff = wi_ref.shape[0], 0, wi_ref.shape[2], wi_ref.shape[3]
    f32, bf = jnp.float32, jnp.bfloat16

    slots = D // ff

    @pl.when(step == 0)
    def _():
        copies = []
        for n, src in enumerate((ctx_ref, x_ref)):
            for u in range(slots):
                at = n * slots + u
                c = pltpu.make_async_copy(src.at[:, pl.ds(u * ff, ff)], slope_ref.at[1 + at], sem.at[at])
                c.start()
                copies.append(c)
        for c in copies:
            c.wait()
        for r in range(0, L, MB):
            rows = slice(r, r + MB)
            z1 = jnp.concatenate([slope_ref[1 + slots + u, rows] for u in range(slots)], axis=1)
            z1 = vec_ref[0:1] + z1.astype(f32)
            for s in range(tn):
                at = s * dt % ff
                part = slope_ref[1 + s * dt // ff, rows, at : at + dt]
                z1 = z1 + dotnt(part, wm_ref[s].reshape(D, dt))
            n1, r1 = norm_rows(z1)
            h1 = n1 * vec_ref[1:2] + vec_ref[2:3]
            low = h1.astype(bf)
            acc_ref[rows] = h1 + vec_ref[3:4]
            hl_ref[rows] = low
            hlt_ref[:, rows] = low.T
            da_ref[rows] = n1.astype(bf)
            high = r1.astype(bf).astype(f32)
            first_lane = lax.broadcasted_iota(jnp.int32, (MB, 128), 1) == 0
            r1_ref[rows] = jnp.where(first_lane, high, r1 - high).astype(bf)

    @pl.when(step < tn)
    def _():
        for r in range(0, L, MB):
            rows = slice(r, r + MB)
            pre = dotnn(hl_ref[rows], wi_ref[0].reshape(D, ff)) + hb_ref[0]
            phi = 0.5 + 0.5 * lax.erf(pre * math.sqrt(0.5))
            act = (pre * phi).astype(bf)
            act_ref[step, rows] = act
            bell = jnp.exp(-0.5 * pre * pre) * (1.0 / math.sqrt(2.0 * math.pi))
            slope_ref[step, rows] = (phi + pre * bell).astype(bf)
            acc_ref[rows] += dotnt(act, wo_ref[0].reshape(D, ff))

    @pl.when(step == tn - 1)
    def _():
        s0 = jnp.zeros((8, D), f32)
        s1 = jnp.zeros((8, D), f32)
        s2 = jnp.zeros((8, D), f32)
        for g in range(gn):
            rows = slice(g * lg, (g + 1) * lg)
            n2, r2 = norm_rows(acc_ref[rows])
            y = (n2 * vec_ref[4:5] + vec_ref[5:6]).astype(bf)
            for s in range(tn):
                y_ref[g, s] = y[:, s * dt : (s + 1) * dt]
            dy = jnp.concatenate([cot_ref[g, s] for s in range(tn)], axis=1).astype(f32)
            dz2 = norm_back(dy * vec_ref[4:5], n2, r2)
            df_ref[rows] = dz2.astype(bf)
            acc_ref[rows] = dz2
            s0, s1, s2 = s0 + fold8(dz2), s1 + fold8(dy * n2), s2 + fold8(dy)
        sums_ref[24:32], sums_ref[32:40], sums_ref[40:48] = s0, s1, s2
        for r in range(0, L, RB):
            hl_ref[:, r : r + RB] = df_ref[r : r + RB].T

    @pl.when(step >= tn)
    def _():
        t = 2 * tn - 1 - step
        hid = jnp.zeros((8, ff), f32)
        for r in range(0, L, MB):
            rows = slice(r, r + MB)
            dpre = dotnn(df_ref[rows], wo_ref[0].reshape(D, ff)) * slope_ref[t, rows].astype(f32)
            hid = hid + fold8(dpre)
            low = dpre.astype(bf)
            slope_ref[t, rows] = low
            acc_ref[rows] += dotnt(low, wi_ref[0].reshape(D, ff))
        hid_ref[0] = hid
        for r in range(0, D, RB):
            og = dotnn(hl_ref[r : r + RB], act_ref[t]).astype(bf)
            ig = dotnn(hlt_ref[r : r + RB], slope_ref[t]).astype(bf)
            for c in range(0, RB, per):
                pay_ref[(r + c) // per, 0, :, 0:ff] = ig[c : c + per]
                pay_ref[(r + c) // per, 0, :, ff : 2 * ff] = og[c : c + per]

    @pl.when(step == 2 * tn - 1)
    def _():
        s0 = jnp.zeros((8, D), f32)
        s1 = jnp.zeros((8, D), f32)
        s2 = jnp.zeros((8, D), f32)
        for r in range(0, L, 128):
            rows = slice(r, r + 128)
            dh1 = acc_ref[rows]
            n1 = da_ref[rows].astype(f32)
            r1 = r1_ref[rows, 0:1].astype(f32) + r1_ref[rows, 1:2].astype(f32)
            dz1 = norm_back(dh1 * vec_ref[1:2], n1, r1)
            da_ref[rows] = dz1.astype(bf)
            s0, s1, s2 = s0 + fold8(dz1), s1 + fold8(dh1 * n1), s2 + fold8(dh1)
        sums_ref[0:8], sums_ref[8:16], sums_ref[16:24] = s0, s1, s2


def middle(ctx, x, second, hidden_bias, vectors, cot):
    gn, tn, lg, dt = cot.shape
    per = second.shape[2]
    L, D = x.shape
    assert L == D
    ff = hidden_bias.shape[2]
    bf, f32 = jnp.bfloat16, jnp.float32
    full = lambda shape: spec(shape, lambda i: (0,) * len(shape), True)
    place = lambda i: jnp.minimum(i, 2 * tn - 1 - i)
    back = lambda i: jnp.minimum(2 * tn - 1 - i, tn - 1)
    return pl.pallas_call(
        middle_kernel,
        grid=(2 * tn,),
        in_specs=[
            pl.BlockSpec(memory_space=pl.ANY),
            pl.BlockSpec(memory_space=pl.ANY),
            spec((tn, gn, per, dt), lambda i: (0, 0, 0, 2 * ff // dt), True),
            spec((1, gn, per, ff), lambda i: (place(i), 0, 0, 0)),
            spec((1, gn, per, ff), lambda i: (place(i), 0, 0, 1)),
            spec((1, 1, ff), lambda i: (place(i), 0, 0)),
            full((6, D)),
            full((gn, tn, lg, dt)),
        ],
        out_specs=[
            full((gn, tn, lg, dt)),
            spec((gn, 1, per, 2 * ff), lambda i: (0, back(i), 0, 0)),
            spec((1, 8, ff), lambda i: (back(i), 0, 0)),
            full((L, D)),
            full((48, D)),
        ],
        out_shape=[
            jax.ShapeDtypeStruct((gn, tn, lg, dt), bf),
            jax.ShapeDtypeStruct((gn, tn, per, 2 * ff), bf),
            jax.ShapeDtypeStruct((tn, 8, ff), f32),
            jax.ShapeDtypeStruct((L, D), bf),
            jax.ShapeDtypeStruct((48, D), f32),
        ],
        scratch_shapes=[
            pltpu.VMEM((tn, L, ff), bf), pltpu.VMEM((tn, L, ff), bf),
            pltpu.VMEM((L, D), bf), pltpu.VMEM((D, L), bf), pltpu.VMEM((L, 128), bf),
            pltpu.VMEM((L, D), bf), pltpu.VMEM((L, D), f32),
            pltpu.SemaphoreType.DMA((2 * (D // ff),)),
        ],
        compiler_params=pltpu.CompilerParams(vmem_limit_bytes=61 << 20),
        cost_estimate=pl.CostEstimate(flops=75 * 10**9, bytes_accessed=100 * 10**6, transcendentals=0),
    )(ctx, x, second, second, second, hidden_bias, vectors, cot)


def merge_back_kernel(da_ref, ctx_ref, wm_ref, pay_ref, dctx_ref, dat_ref):
    t = pl.program_id(0)
    L, D = da_ref.shape
    gn, _, per, dt = pay_ref.shape

    @pl.when(t == 0)
    def _():
        for r in range(0, L, RB):
            dat_ref[:, r : r + RB] = da_ref[r : r + RB].T

    dctx_ref[...] = dotnn(da_ref[...], wm_ref[0].reshape(D, dt)).astype(jnp.bfloat16)
    pay_ref[:, 0] = dotnn(dat_ref[...], ctx_ref[...]).astype(jnp.bfloat16).reshape(gn, per, dt)


def merge_back(dattn, ctx, second):
    tn, gn, per, wide = second.shape
    L, D = dattn.shape
    dt = D // tn
    last = wide // dt - 1
    bf = jnp.bfloat16
    return pl.pallas_call(
        merge_back_kernel,
        grid=(tn,),
        in_specs=[
            spec((L, D), lambda t: (0, 0), True),
            spec((L, dt), lambda t: (0, t)),
            spec((1, gn, per, dt), lambda t: (t, 0, 0, last)),
        ],
        out_specs=[
            spec((gn, 1, per, dt), lambda t: (0, t, 0, 0)),
            spec((L, dt), lambda t: (0, t)),
        ],
        out_shape=[
            jax.ShapeDtypeStruct((gn, tn, per, dt), bf),
            jax.ShapeDtypeStruct((L, D), bf),
        ],
        scratch_shapes=[pltpu.VMEM((D, L), bf)],
        compiler_params=pltpu.CompilerParams(vmem_limit_bytes=50 << 20),
        cost_estimate=pl.CostEstimate(flops=4 * 10**9, bytes_accessed=10 * 10**6, transcendentals=0),
    )(dattn, ctx, second)


def input_back_kernel(da_ref, dq_ref, dk_ref, dv_ref, wa_ref, wb_ref, dx_ref, acc_ref):
    t = pl.program_id(0)
    L, D = da_ref.shape
    gn, tn, lg, dt = dx_ref.shape
    per = D // gn

    @pl.when(t == 0)
    def _():
        acc_ref[...] = da_ref[...].astype(jnp.float32)

    w = [wa_ref[:, 0, j * per : (j + 1) * per, :].reshape(D, dt) for j in range(2)]
    w.append(wb_ref[:, 0].reshape(D, dt))
    tops = [dq_ref, dk_ref, dv_ref]
    for r in range(0, L, RB):
        acc_ref[r : r + RB] += sum(dotnt(tops[j][r : r + RB], w[j]) for j in range(3))

    @pl.when(t == pl.num_programs(0) - 1)
    def _():
        for g in range(gn):
            for s in range(tn):
                cols = slice(s * dt, (s + 1) * dt)
                dx_ref[g, s] = acc_ref[g * lg : (g + 1) * lg, cols].astype(jnp.bfloat16)


def input_back(dattn, dq, dk, dv, first, later):
    gn, tn, wide, dt = first.shape
    L, D = dattn.shape
    col = lambda: spec((L, dt), lambda t: (0, t))
    return pl.pallas_call(
        input_back_kernel,
        grid=(tn,),
        in_specs=[
            spec((L, D), lambda t: (0, 0), True),
            col(), col(), col(),
            spec((gn, 1, wide, dt), lambda t: (0, t, 0, 0)),
            spec((gn, 1, D // gn, dt), lambda t: (0, t, 0, 0)),
        ],
        out_specs=spec((gn, tn, L // gn, dt), lambda t: (0, 0, 0, 0), True),
        out_shape=jax.ShapeDtypeStruct((gn, tn, L // gn, dt), jnp.bfloat16),
        scratch_shapes=[pltpu.VMEM((L, D), jnp.float32)],
        compiler_params=pltpu.CompilerParams(vmem_limit_bytes=50 << 20),
        cost_estimate=pl.CostEstimate(flops=7 * 10**9, bytes_accessed=20 * 10**6, transcendentals=0),
    )(dattn, dq, dk, dv, first, later)


def tail_kernel(x_ref, rel_ref, hot_ref, dq_ref, dk_ref, dv_ref, dqf_ref, dkf_ref, sm_ref, w_ref, small_ref, mg_ref,
                pay_ref, xt_ref, ra_ref, *, first_shift):
    t = pl.program_id(0)
    L, D = x_ref.shape
    spans = rel_ref.shape[0]
    gn, tn, _, dt = pay_ref.shape
    per = D // gn
    rg = spans // gn
    sr = small_ref.shape[2]
    f32, bf = jnp.float32, jnp.bfloat16

    @pl.when(t == 0)
    def _():
        for r in range(0, L, RB):
            xt_ref[:, r : r + RB] = x_ref[r : r + RB].T
        for r in range(0, spans, RB):
            xt_ref[:, L + r : L + r + RB] = rel_ref[r : r + RB].T
        ra_ref[...] = jnp.zeros_like(ra_ref)

    w = [w_ref[:, 0, j * per : (j + 1) * per, :].reshape(D, dt) for j in range(2)]
    qp = dotnn(dqf_ref[...], hot_ref[...]).T
    kp = dotnn(dkf_ref[...], hot_ref[...]).T
    pos = [qp.astype(bf), kp.astype(bf)]
    tops = [dq_ref, dk_ref, dv_ref]
    rows = 4 * per + rg
    pay_ref[:, t, 3 * per : 4 * per, :] = mg_ref[:, 0]
    pay_ref[:, t, rows : rows + sr, :] = small_ref[0].astype(bf)
    for j in range(3):
        total = jnp.sum(sm_ref[8 * j : 8 * j + 8], axis=0, keepdims=True)
        if j < 2:
            total = total + jnp.sum((qp, kp)[j], axis=0, keepdims=True)
            both = jnp.concatenate([tops[j][...], pos[j]], axis=0)
            grad = dotnn(xt_ref[...], both)
            ra_ref[...] += dotnt(pos[j], w[j])
        else:
            grad = dotnn(xt_ref[:, 0:L], tops[j][...])
        pay_ref[:, t, j * per : (j + 1) * per, :] = grad.astype(bf).reshape(gn, per, dt)
        at = first_shift + j
        pay_ref[at // sr, t, rows + at % sr : rows + at % sr + 1, :] = total.astype(bf)
    @pl.when(t == pl.num_programs(0) - 1)
    def _():
        for g in range(gn):
            for s in range(tn):
                cols = slice(s * dt, (s + 1) * dt)
                pay_ref[g, s, 4 * per : rows, :] = ra_ref[g * rg : (g + 1) * rg, cols].astype(bf)


def tail(x, rel, hot, dq, dk, dv, dqf, dkf, sums, first, small, merged, first_shift):
    gn, tn, wide, dt = first.shape
    L, D = x.shape
    spans = rel.shape[0]
    rows = 4 * D // gn + spans // gn + small.shape[2]
    bf, f32 = jnp.bfloat16, jnp.float32
    full = lambda shape: spec(shape, lambda t: (0,) * len(shape), True)
    col = lambda: spec((L, dt), lambda t: (0, t))
    return pl.pallas_call(
        functools.partial(tail_kernel, first_shift=first_shift),
        grid=(tn,),
        in_specs=[
            full((L, D)), full((spans, D)), full((2 * L, spans)),
            col(), col(), col(),
            spec((dt, 2 * L), lambda t: (t, 0)), spec((dt, 2 * L), lambda t: (t, 0)),
            spec((24, dt), lambda t: (0, t)),
            spec((gn, 1, wide, dt), lambda t: (0, t, 0, 0)),
            spec((1,) + small.shape[1:], lambda t: (t, 0, 0, 0)),
            spec((gn, 1, D // gn, dt), lambda t: (0, t, 0, 0)),
        ],
        out_specs=full((gn, tn, rows, dt)),
        out_shape=jax.ShapeDtypeStruct((gn, tn, rows, dt), bf),
        scratch_shapes=[pltpu.VMEM((D, L + spans), bf), pltpu.VMEM((spans, D), f32)],
        compiler_params=pltpu.CompilerParams(vmem_limit_bytes=56 << 20),
        cost_estimate=pl.CostEstimate(flops=13 * 10**9, bytes_accessed=40 * 10**6, transcendentals=0),
    )(x, rel, hot, dq, dk, dv, dqf, dkf, sums, first, small, merged)


MESH = pl.DeviceIdType.MESH


def bit_of(place, i):
    return (place // (1 << i)) % 2


def flipped(place, flips):
    for i in flips:
        place = place + (1 << i) * (1 - 2 * bit_of(place, i))
    return place


def subsets(bits):
    out = [()]
    for i in bits:
        out += [s + (i,) for s in out]
    return out


def greet(tn, gn):
    t, g = lax.axis_index("tensor"), lax.axis_index("dp")
    barrier = pltpu.get_barrier_semaphore()
    bits = list(range(gn.bit_length() - 1))
    for d in range(1, tn):
        pl.semaphore_signal(barrier, inc=1, device_id={"tensor": lax.rem(t + d, tn)}, device_id_type=MESH)
    for i in bits:
        pl.semaphore_signal(barrier, inc=1, device_id={"dp": flipped(g, (i,))}, device_id_type=MESH)
    pl.semaphore_wait(barrier, tn - 1 + len(bits))


class Wire:
    def __init__(self, send, recv):
        self.send, self.recv, self.at = send, recv, 0

    def push(self, src, dst, **device):
        c = pltpu.make_async_remote_copy(
            src, dst, self.send.at[self.at], self.recv.at[self.at], device_id=device, device_id_type=MESH
        )
        self.at += 1
        c.start()
        return c


def run_waves(chunks):
    waves = max(len(stages) + c for c, stages in enumerate(chunks)) + 1
    flight = {}
    for w in range(waves):
        for c, stages in enumerate(chunks):
            s = w - c
            if 0 < s <= len(stages):
                stages[s - 1][1](flight.pop((c, s - 1)))
            if 0 <= s < len(stages):
                flight[c, s] = stages[s][0]()


def wait_all(copies):
    for c in copies:
        c.wait()


def spread_stages(src, out, local, wire, tn, gn):
    t, g = lax.axis_index("tensor"), lax.axis_index("dp")
    bits = list(range(gn.bit_length() - 1))
    half = tn // 2
    plans = [(0, bits[1:] + bits[:1]), (half, bits[:0:-1] + bits[:1])]

    def first():
        own = pltpu.make_async_copy(src(), out(g, pl.ds(t, 1)), local)
        own.start()
        copies = [
            wire.push(src(), out(g, pl.ds(t, 1)), tensor=lax.rem(t + d, tn)) for d in range(1, tn)
        ]
        return [own] + copies

    def later(step):
        def start():
            copies = []
            for lo, plan in plans:
                for s in subsets(plan[:step]):
                    part = out(flipped(g, s), pl.ds(lo, half))
                    copies.append(wire.push(part, part, dp=flipped(g, (plan[step],))))
            return copies

        return start

    return [(first, wait_all)] + [(later(step), wait_all) for step in range(len(bits))]


def spread_count(tn, gn):
    return tn - 1 + 2 * (gn - 1)


def gather_kernel(src_ref, out_ref, local, send, recv, *, tn, gn, cuts):
    greet(tn, gn)
    wire = Wire(send, recv)
    chunks = []
    for n, (lo, hi) in enumerate(cuts):
        rows = pl.ds(lo, hi - lo)
        chunks.append(
            spread_stages(
                lambda rows=rows: src_ref.at[:, rows],
                lambda g, s, rows=rows: out_ref.at[g, s, rows],
                local.at[n], wire, tn, gn,
            )
        )
    run_waves(chunks)


def gather_all(w, tn, gn, number):
    rows = w.shape[0]
    mid = rows // 32 * 16
    cuts = [(0, mid), (mid, rows)]
    n = spread_count(tn, gn) * len(cuts)
    dma = lambda k: pltpu.SemaphoreType.DMA((k,))
    return pl.pallas_call(
        functools.partial(gather_kernel, tn=tn, gn=gn, cuts=cuts),
        in_specs=[pl.BlockSpec(memory_space=pl.ANY)],
        out_specs=pl.BlockSpec(memory_space=pl.ANY),
        out_shape=jax.ShapeDtypeStruct((gn, tn) + w.shape, w.dtype),
        scratch_shapes=[dma(len(cuts)), dma(n), dma(n)],
        compiler_params=pltpu.CompilerParams(collective_id=number, has_side_effects=True),
        cost_estimate=pl.CostEstimate(flops=0, bytes_accessed=w.size * tn * gn * 16, transcendentals=0),
    )(w[None])


def reduce_kernel(pay_ref, q_ref, k_ref, v_ref, m_ref, rel_ref, small_ref, all_ref, acc_ref, rx_ref, ry_ref, rz_ref, rest_ref,
                  local, send, recv, *, tn, gn, keep):
    t, g = lax.axis_index("tensor"), lax.axis_index("dp")
    bits = list(range(gn.bit_length() - 1))
    f32, bf = jnp.float32, jnp.bfloat16
    rows = acc_ref.shape[2]
    per = keep // 4
    greet(tn, gn)
    wire = Wire(send, recv)
    outer = bits[1:]
    masks = subsets(outer)
    index = {s: n for n, s in enumerate(masks)}
    half = tn // 2
    plans = [(0, outer), (half, outer[::-1])]
    grads = (q_ref, k_ref, v_ref, m_ref)

    def reduce_stages(n, lo, hi):
        span = pl.ds(lo, hi - lo)

        def add(dst, first, size, src_ref, slot):
            for i in range(size):
                acc_ref[dst, first + i, lo:hi] = (
                    acc_ref[dst, first + i, lo:hi].astype(f32) + src_ref[slot, i, lo:hi].astype(f32)
                ).astype(bf)

        def first():
            copies = []
            for i, s in enumerate(masks):
                copies.append(wire.push(pay_ref.at[flipped(g, (0,) + s), :, span], rx_ref.at[i, :, span], dp=flipped(g, (0,))))
            for i, s in enumerate(masks):
                c = pltpu.make_async_copy(pay_ref.at[flipped(g, s), :, span], acc_ref.at[i, :, span], local.at[n, i])
                c.start()
                copies.append(c)
            return copies

        def first_done(copies):
            for i in range(len(masks)):
                copies[len(masks) + i].wait()
                copies[i].wait()
                add(i, 0, tn, rx_ref, i)

        def outer_stage(step, base):
            def start():
                flight = []
                slot = base
                for place, plan in plans:
                    bit = plan[step]
                    for s in masks:
                        if any(i in plan[: step + 1] for i in s):
                            continue
                        src = tuple(i for i in outer if i in s or i == bit)
                        c = wire.push(
                            acc_ref.at[index[src], pl.ds(place, half), span], ry_ref.at[slot, :, span],
                            dp=flipped(g, (bit,)),
                        )
                        flight.append((c, index[s], place, slot))
                        slot += 1
                return flight

            def done(flight):
                for c, dst, place, slot in flight:
                    c.wait()
                    add(dst, place, half, ry_ref, slot)

            return start, done

        def last():
            return [
                wire.push(acc_ref.at[0, lax.rem(t + d, tn), span], rz_ref.at[d - 1, span], tensor=lax.rem(t + d, tn))
                for d in range(1, tn)
            ]

        def last_done(copies):
            total = acc_ref[0, t, lo:hi].astype(f32)
            for d, c in enumerate(copies):
                c.wait()
                total = total + rz_ref[d, lo:hi].astype(f32)
            if lo >= keep:
                rest_ref[0] = total.astype(bf)
            else:
                for j in range(4):
                    a, b = max(lo, j * per), min(hi, (j + 1) * per)
                    if a < b:
                        grads[j][a - j * per : b - j * per] = total[a - lo : b - lo]

        stages = [(first, first_done)]
        base = 0
        for step in range(len(outer)):
            stages.append(outer_stage(step, base))
            base += 2 * (gn // 4 >> step)
        return stages + [(last, last_done)]

    cut = keep // 32 * 16
    chunks = [
        reduce_stages(0, keep, rows)
        + spread_stages(
            lambda: rest_ref, lambda i, s: all_ref.at[i, s], local.at[3, 0], wire, tn, gn
        ),
        reduce_stages(1, 0, cut),
        reduce_stages(2, cut, keep),
    ]
    run_waves(chunks)
    dt = q_ref.shape[1]
    rg = rel_ref.shape[0] // gn
    for s in range(tn):
        cols = slice(s * dt, (s + 1) * dt)
        for i in range(gn):
            rel_ref[i * rg : (i + 1) * rg, cols] = all_ref[i, s, :rg].astype(f32)
        small_ref[:, cols] = all_ref[0, s, rg:].astype(f32)


def reduce_all(pay, keep, spans, number):
    gn, tn, rows, dt = pay.shape
    bf, f32 = jnp.bfloat16, jnp.float32
    m = gn // 2
    pieces = 2 * (m - 1)
    count = 3 * (m + pieces + tn - 1) + spread_count(tn, gn)
    dma = lambda *k: pltpu.SemaphoreType.DMA(k)
    return pl.pallas_call(
        functools.partial(reduce_kernel, tn=tn, gn=gn, keep=keep),
        in_specs=[pl.BlockSpec(memory_space=pl.ANY)],
        out_specs=[pl.BlockSpec(memory_space=pltpu.VMEM)] * 6,
        out_shape=[jax.ShapeDtypeStruct((keep // 4, dt), f32)] * 4
        + [
            jax.ShapeDtypeStruct((spans, tn * dt), f32),
            jax.ShapeDtypeStruct((rows - keep - spans // gn, tn * dt), f32),
        ],
        scratch_shapes=[
            pltpu.VMEM((gn, tn, rows - keep, dt), bf),
            pltpu.VMEM((m, tn, rows, dt), bf),
            pltpu.VMEM((m, tn, rows, dt), bf),
            pltpu.VMEM((pieces, tn // 2, rows, dt), bf),
            pltpu.VMEM((tn - 1, rows, dt), bf),
            pltpu.VMEM((1, rows - keep, dt), bf),
            dma(4, m), dma(count), dma(count),
        ],
        compiler_params=pltpu.CompilerParams(collective_id=number, has_side_effects=True, vmem_limit_bytes=58 << 20),
        cost_estimate=pl.CostEstimate(flops=0, bytes_accessed=200 * 10**6, transcendentals=0),
    )(pay)


def shards(
    inputs,
    cotangent,
    lengths,
    dealing,
    buckets,
    rel_embed,
    query_weight,
    key_weight,
    value_weight,
    proj_shifts,
    merge_weight,
    inner_weight,
    hidden_shift,
    outer_weight,
    layer_vectors,
):
    tn = lax.axis_size("tensor")
    gn = lax.axis_size("dp")
    me = lax.axis_index("dp") * tn + lax.axis_index("tensor")
    count, lg, dt = inputs.shape
    L, D = lg * gn, dt * tn
    per = query_weight.shape[0]
    rg = rel_embed.shape[0]
    spans = rg * gn
    assert count == tn * gn
    bf = jnp.bfloat16
    f32 = jnp.float32
    scale = 1.0 / math.sqrt(3.0 * HEAD)
    seq_axes = ("dp", "tensor")
    w_axes = ("tensor", "dp")

    def swap(a):
        return lax.all_to_all(a, seq_axes, split_axis=0, concat_axis=0, tiled=True)

    def gather(w):
        return lax.all_gather(w, w_axes, axis=0, tiled=False).reshape((tn, gn) + w.shape)

    rel_cols = lax.dynamic_slice_in_dim(rel_embed, lax.axis_index("tensor") * dt, dt, 1)
    early = jnp.concatenate([query_weight, key_weight], axis=0)
    late = jnp.concatenate(
        [value_weight, rel_cols, proj_shifts, hidden_shift.reshape(-1, dt), jnp.zeros((1, dt), bf)], axis=0
    )
    first = gather_all(early, tn, gn, 0)
    xd = swap(inputs).reshape(gn, tn, lg, dt)
    wide = jnp.concatenate([inner_weight, outer_weight, merge_weight], axis=1)
    first, xd, late, wide, cotangent = lax.optimization_barrier((first, xd, late, wide, cotangent))
    second = gather(wide)
    later = gather_all(late, tn, gn, 2)
    cot = swap(cotangent).reshape(gn, tn, lg, dt)
    biases = later[0, :, per + rg :].astype(f32)
    shifts = biases[:, :3]
    hidden_bias = biases[:, 3:7].reshape(tn, 1, -1)
    vectors = layer_vectors.astype(f32)
    length = jnp.sum(jnp.where(dealing == me, lengths, 0)).reshape(1)
    places = jnp.concatenate([buckets[::-1], jnp.full((1,), -1, jnp.int32)])[:, None]

    qkv, far, x, rel, hot = project(xd, first, later, shifts, places, per)
    ctx, probs, inv = attn_fwd(length, qkv, far, scale=scale)
    y, payload, hidden, dattn, sums12 = middle(ctx, x, second, hidden_bias, vectors, cot)
    out = swap(y.reshape(count, lg, dt))
    wide_grads = lax.psum_scatter(payload, "dp", scatter_dimension=0, tiled=False)
    merged, dctx = merge_back(dattn, ctx, second)
    dq, dk, dv, dkf, dqf, sums = attn_bwd(probs, qkv, dctx, ctx, inv, far, scale=scale)
    dq, out, wide_grads = lax.optimization_barrier((dq, out, wide_grads))
    wide_grads = lax.psum_scatter(wide_grads, "tensor", scatter_dimension=0, tiled=False)
    ff = hidden.shape[2]
    small = jnp.concatenate(
        [
            jnp.sum(sums12.reshape(6, 8, D), axis=1),
            jnp.sum(hidden, axis=1).reshape(-1, D),
        ],
        axis=0,
    )
    first_shift = small.shape[0]
    sr = 16
    small = jnp.pad(small, ((0, sr - first_shift), (0, 0)))
    small = small.reshape(sr, tn, dt).transpose(1, 0, 2)[:, None]
    small = jnp.pad(small, ((0, 0), (0, gn - 1), (0, 0), (0, 0)))
    dx = input_back(dattn, dq, dk, dv, first, later)
    dx, dq = lax.optimization_barrier((dx, dq))
    pay = tail(x, rel, hot, dq, dk, dv, dqf, dkf, sums, first, small, merged, first_shift)
    grad_in = swap(dx.reshape(count, lg, dt))
    wide_grads = wide_grads.astype(f32)
    query_grad, key_grad, value_grad, merge_grad, rel_grad, rest = reduce_all(pay, 4 * per, spans, 1)
    return (
        out,
        grad_in,
        rel_grad,
        query_grad,
        key_grad,
        value_grad,
        rest[first_shift : first_shift + 3],
        merge_grad,
        wide_grads[:, :ff],
        rest[6:first_shift].reshape(-1),
        wide_grads[:, ff:],
        rest[:6],
    )


def solution(mesh):
    split = P("dp", "tensor")
    whole = P(None, "dp", "tensor")
    in_specs = (
        whole, whole, P(), P(), P(), P("dp", None), split, split, split, P(None, "tensor"),
        split, split, P("tensor"), split, P(),
    )
    out_specs = (whole, whole, P(), split, split, split, P(), split, split, P(), split, P())
    return jax.shard_map(shards, mesh=mesh, in_specs=in_specs, out_specs=out_specs, check_vma=False)
```

```python
import functools
import math

import jax
import jax.numpy as jnp
from jax import lax
from jax.experimental import pallas as pl
from jax.experimental.pallas import tpu as pltpu
from jax.sharding import PartitionSpec as P

EPSILON = 1e-07
HEAD = 64
B = 128
SR = 16
NT = (((1,), (1,)), ((), ()))


def dotnt(a, b):
    return lax.dot_general(a, b, NT, preferred_element_type=jnp.float32)


def dotnn(a, b):
    return lax.dot_general(a, b, (((1,), (0,)), ((), ())), preferred_element_type=jnp.float32)


def skew(g_ref, a, n, L):
    parts=[]
    nb=L//B
    for a8 in range(a,a+n,8):
        rot=[pltpu.roll(g_ref[a8:a8+8,t*128:t*128+128], 1+a8, 1, stride=1, stride_axis=0) for t in range(nb+1)]
        msk=lax.broadcasted_iota(jnp.int32,(8,128),1) < (1+a8+lax.broadcasted_iota(jnp.int32,(8,128),0))
        parts.append(jnp.concatenate([jnp.where(msk,rot[t],rot[t+1]) for t in range(nb)],axis=1))
    return jnp.concatenate(parts,axis=0)

def fwd_kernel(len_ref, q_ref, k_ref, v_ref, kf_ref, qf_ref, ctx_ref, p_ref, l_ref, t_ref, kx_ref, vx_ref, g0, g1, s0, s1, *, L, scale):
    W = L + B
    nb = L // B
    gs=(g0,g1); ss=(s0,s1)
    lane = lax.broadcasted_iota(jnp.int32, (1, 128), 1)
    length = len_ref[0]
    row = lax.broadcasted_iota(jnp.int32, (L, 128), 0)
    c2 = scale * math.log2(math.e)
    eye = (lax.broadcasted_iota(jnp.int32,(B,B),0)==lax.broadcasted_iota(jnp.int32,(B,B),1)).astype(jnp.bfloat16)
    zero = jnp.zeros((), jnp.bfloat16)
    mine = [lane < 64, lane >= 64]
    first_other = [lane==64, lane==0]
    for h in range(2):
        bias = jnp.where((row >= length) & first_other[h], -1e30, 0.0).astype(jnp.bfloat16)
        kx_ref[h] = jnp.where(mine[h], k_ref[...], bias)
        vx_ref[h] = jnp.where(mine[h], v_ref[...], jnp.ones((), jnp.bfloat16))
    def tblock(b, _):
        r0 = pl.multiple_of(b*B, B)
        base = pl.multiple_of(L - B - b*B, B)
        for h in range(2):
            kb = jnp.where(mine[h], k_ref[pl.ds(r0,B),:], zero)
            gs[h][...] = dotnt(kb, qf_ref[pl.ds(base, W), :])
        for h in range(2):
            for a in range(0, B, SR):
                t_ref[h, pl.ds(r0+a,SR), :] = skew(gs[h], a, SR, L).astype(jnp.bfloat16)
        return 0
    lax.fori_loop(0, nb, tblock, 0, unroll=2)
    def scores(b, h):
        r0 = pl.multiple_of(b*B, B)
        base = pl.multiple_of(L - B - b*B, B)
        qb = q_ref[pl.ds(r0,B),:]
        qm = jnp.where(mine[h], qb, zero)
        qx = jnp.where(mine[h], qb, first_other[h].astype(jnp.bfloat16))
        gs[h][...] = dotnt(qm, kf_ref[pl.ds(base, W), :])
        lhs = jnp.concatenate([qx, eye], axis=1)
        rhs = jnp.concatenate([kx_ref[h], t_ref[h, :, pl.ds(r0,B)]], axis=1)
        ss[h][...] = dotnt(lhs, rhs)
    def soft(b, h):
        r0 = pl.multiple_of(b*B, B)
        tops=[]
        for a in range(0, B, 8):
            s = ss[h][a:a+8] + skew(gs[h], a, 8, L)
            ss[h][a:a+8] = s
            tops.append(functools.reduce(jnp.maximum,[s[:,t*128:t*128+128] for t in range(nb)]))
        m = jnp.max(jnp.concatenate(tops,axis=0), axis=1, keepdims=True) * c2
        for a in range(0, B, SR):
            p_ref[h, pl.ds(r0+a,SR), :] = jnp.exp2(ss[h][a:a+SR]*c2 - m[a:a+SR]).astype(jnp.bfloat16)
    def out(b, h):
        r0 = pl.multiple_of(b*B, B)
        return dotnn(p_ref[h, pl.ds(r0,B), :], vx_ref[h])
    def finish(b, o0, o1):
        r0 = pl.multiple_of(b*B, B)
        num = jnp.where(mine[0], o0, o1)
        den = jnp.where(mine[0], pltpu.roll(o0,64,1), pltpu.roll(o1,64,1))
        inv = 1.0/den
        ctx_ref[pl.ds(r0,B),:] = (num*inv).astype(jnp.bfloat16)
        l_ref[pl.ds(r0,B),:] = inv
    scores(0,0)
    def sblock(b, o0):
        scores(b,1)
        soft(b,0)
        o0 = out(b,0)
        scores(jnp.minimum(b+1,nb-1),0)
        soft(b,1)
        o1 = out(b,1)
        finish(b,o0,o1)
        return 0
    lax.fori_loop(0, nb, sblock, 0, unroll=8)


def attn_fwd(length, qkv, far, *, scale):
    _, L, C = qkv.shape
    part = lambda j, r: pl.BlockSpec((None, r, 128), lambda h, *_: (j, 0, h))
    return pl.pallas_call(
        functools.partial(fwd_kernel, L=L, scale=scale),
        grid_spec=pltpu.PrefetchScalarGridSpec(
            num_scalar_prefetch=1,
            grid=(C // 128,),
            in_specs=[part(0, L), part(1, L), part(2, L), part(1, 2 * L), part(0, 2 * L)],
            out_specs=[
                pl.BlockSpec((L, 128), lambda h, *_: (0, h)),
                pl.BlockSpec((2, L, L), lambda h, *_: (h, 0, 0)),
                pl.BlockSpec((L, 128), lambda h, *_: (0, h)),
            ],
            scratch_shapes=[pltpu.VMEM((2, L, L), jnp.bfloat16)]
            + [pltpu.VMEM((2, L, 128), jnp.bfloat16)] * 2
            + [pltpu.VMEM((B, L + B), jnp.float32)] * 2
            + [pltpu.VMEM((B, L), jnp.float32)] * 2,
        ),
        out_shape=[
            jax.ShapeDtypeStruct((L, C), jnp.bfloat16),
            jax.ShapeDtypeStruct((C // HEAD, L, L), jnp.bfloat16),
            jax.ShapeDtypeStruct((L, C), jnp.float32),
        ],
        compiler_params=pltpu.CompilerParams(vmem_limit_bytes=50 << 20),
        cost_estimate=pl.CostEstimate(flops=80 * 10**9, bytes_accessed=60 * 10**6, transcendentals=0),
    )(length, qkv, qkv, qkv, far, far)


FAR = 3


def unskew(x, a8):
    nb = x.shape[1] // B
    sub = lax.broadcasted_iota(jnp.int32, (8, 128), 0)
    lane = lax.broadcasted_iota(jnp.int32, (8, 128), 1)
    keep = lane >= (127 - a8) - sub
    idx = (lane - (127 - a8) + sub) & 127
    rot = [jnp.take_along_axis(x[:, t * 128 : t * 128 + 128], idx, axis=1) for t in range(nb)]
    zero = jnp.zeros((8, 128), x.dtype)
    return jnp.concatenate(
        [jnp.where(keep, rot[t] if t < nb else zero, rot[t - 1] if t > 0 else zero) for t in range(nb + 1)], axis=1
    )


def fold_tiles(x, lo, hi):
    return sum(x[:, t * 128 : t * 128 + 128] for t in range(lo, hi))


def place_back(rows8, d_ref, a, b, nb):
    lo, hi = max(0, b - FAR), min(nb, b + FAR + 1)
    near = jnp.concatenate([unskew(x[:, lo * 128 : hi * 128], a + 8 * n) for n, x in enumerate(rows8)], axis=0)
    d_ref[a : a + SR, 256 : 256 + near.shape[1]] = near.astype(jnp.bfloat16)
    if lo > 0:
        far = jnp.concatenate([fold_tiles(x, 0, lo) for x in rows8], axis=0)
        d_ref[a : a + SR, 0:128] = far.astype(jnp.bfloat16)
    if hi < nb:
        far = jnp.concatenate([fold_tiles(x, hi, nb) for x in rows8], axis=0)
        d_ref[a : a + SR, 128:256] = far.astype(jnp.bfloat16)


def window_products(d_ref, table_ref, ends_ref, e, lhs, acc_ref, sums_ref, rows, b, nb):
    lo, hi = max(0, b - FAR), min(nb, b + FAR + 1)
    base, size = (nb - 1 - b + lo) * B, (hi - lo + 1) * B
    near = d_ref[:, 256 : 256 + size]
    out = dotnn(near, table_ref[base : base + size, :])
    acc_ref[rows, base : base + size] += dotnn(lhs, near)
    for there, k in ((lo > 0, 0), (hi < nb, 1)):
        if there:
            far = d_ref[:, k * 128 : k * 128 + 128]
            out = out + dotnn(far, ends_ref[e + k])
            sums_ref[e + k, rows, :] += dotnn(lhs, far)
    return out


def bwd_kernel(p_ref, q_ref, k_ref, v_ref, do_ref, ctx_ref, li_ref, kf_ref, qf_ref,
               dq_ref, dk_ref, dv_ref, dkf_ref, dqf_ref, sums_ref,
               dox_ref, dot_ref, qt_ref, kt_ref, vx_ref, ds_ref, d0, d1, akf, aqf, ends, far, *, L, scale):
    W = L + B
    nb = L // B
    dd=(d0,d1)
    lane = lax.broadcasted_iota(jnp.int32, (1, 128), 1)
    mine = [lane < 64, lane >= 64]
    base_lane = [64, 0]
    dos = (do_ref[...].astype(jnp.float32) * li_ref[...]).astype(jnp.bfloat16)
    prod = dos.astype(jnp.float32) * ctx_ref[...].astype(jnp.float32)
    for h in range(2):
        delta = -jnp.sum(jnp.where(mine[h], prod, 0.0), axis=1, keepdims=True)
        hi = delta.astype(jnp.bfloat16).astype(jnp.float32)
        lo = delta - hi
        extra = jnp.where(lane == base_lane[h], hi, jnp.where(lane == base_lane[h]+1, lo, 0.0)).astype(jnp.bfloat16)
        dox_ref[h] = jnp.where(mine[h], dos, extra)
        vx_ref[h] = jnp.where(mine[h], v_ref[...], jnp.ones((), jnp.bfloat16))
    dot_ref[...] = dos.T
    qt_ref[...] = q_ref[...].T
    kt_ref[...] = k_ref[...].T
    akf[...] = jnp.zeros_like(akf)
    aqf[...] = jnp.zeros_like(aqf)
    far[...] = jnp.zeros_like(far)
    last = 2 * L - 2
    for e, table in ((0, kf_ref), (2, qf_ref)):
        ends[e] = jnp.broadcast_to(table[0:1, :], (128, 128))
        ends[e + 1] = jnp.broadcast_to(table[last : last + 1, :], (128, 128))
    sq = jnp.zeros((8, 128), jnp.float32)
    for b in range(nb):
        r0 = b * B
        outs = []
        for h in range(2):
            rows = slice(h * 64, h * 64 + 64)
            dp = dotnt(dox_ref[h, r0 : r0 + B, :], vx_ref[h])
            for a in range(0, B, SR):
                ds = p_ref[h, r0 + a : r0 + a + SR, :].astype(jnp.float32) * dp[a : a + SR]
                ds_ref[h, r0 + a : r0 + a + SR, :] = ds.astype(jnp.bfloat16)
                place_back([ds[s : s + 8] for s in range(0, SR, 8)], dd[h], a, b, nb)
            outs.append(
                dotnn(ds_ref[h, r0 : r0 + B, :], k_ref[...])
                + window_products(dd[h], kf_ref, ends, 0, qt_ref[rows, r0 : r0 + B], akf, far, rows, b, nb)
            )
        dq = jnp.where(mine[0], outs[0], outs[1]) * scale
        dq_ref[r0 : r0 + B, :] = dq.astype(jnp.bfloat16)
        sq = sq + jnp.sum(dq.reshape(B // 8, 8, 128), axis=0)
    sk = jnp.zeros((8, 128), jnp.float32)
    for b in range(nb):
        r0 = b * B
        outs = []
        for h in range(2):
            rows = slice(h * 64, h * 64 + 64)
            dst = ds_ref[h, :, r0 : r0 + B].T
            for a in range(0, B, SR):
                x = dst[a : a + SR].astype(jnp.float32)
                place_back([x[s : s + 8] for s in range(0, SR, 8)], dd[h], a, b, nb)
            outs.append(
                dotnn(dst, q_ref[...])
                + window_products(dd[h], qf_ref, ends, 2, kt_ref[rows, r0 : r0 + B], aqf, far, rows, b, nb)
            )
        dk = jnp.where(mine[0], outs[0], outs[1]) * scale
        dk_ref[r0 : r0 + B, :] = dk.astype(jnp.bfloat16)
        sk = sk + jnp.sum(dk.reshape(B // 8, 8, 128), axis=0)
    for e, acc in ((0, akf), (2, aqf)):
        for k, at in ((0, 0), (1, last)):
            tile = at // 128 * 128
            total = jnp.sum(far[e + k], axis=1, keepdims=True)
            acc[:, tile : tile + 128] += jnp.where(lane == at - tile, total, 0.0)
    dvt = jnp.concatenate([dotnn(dot_ref[h*64:h*64+64,:], p_ref[h]) for h in range(2)], axis=0)
    dv = dvt.T
    dv_ref[...] = dv.astype(jnp.bfloat16)
    sv = jnp.sum(dv.reshape(L//8,8,128), axis=0)
    sums_ref[0:8] = sq
    sums_ref[8:16] = sk
    sums_ref[16:24] = sv
    dkf_ref[...] = (akf[...]*scale).astype(jnp.bfloat16)
    dqf_ref[...] = (aqf[...]*scale).astype(jnp.bfloat16)


def attn_bwd(p, qkv, do, ctx, linv, far, *, scale):
    _, L, C = qkv.shape
    bf = jnp.bfloat16
    part = lambda j, r: pl.BlockSpec((None, r, 128), lambda h: (j, 0, h))
    col = lambda r: pl.BlockSpec((r, 128), lambda h: (0, h))
    rowb = pl.BlockSpec((128, 2 * L), lambda h: (h, 0))
    return pl.pallas_call(
        functools.partial(bwd_kernel, L=L, scale=scale),
        grid=(C // 128,),
        in_specs=[pl.BlockSpec((2, L, L), lambda h: (h, 0, 0)), part(0, L), part(1, L), part(2, L)]
        + [col(L)] * 3
        + [part(1, 2 * L), part(0, 2 * L)],
        out_specs=[col(L)] * 3 + [rowb] * 2 + [col(24)],
        scratch_shapes=[pltpu.VMEM((2, L, 128), bf)]
        + [pltpu.VMEM((128, L), bf)] * 3
        + [pltpu.VMEM((2, L, 128), bf), pltpu.VMEM((2, L, L), bf)]
        + [pltpu.VMEM((B, L + 3 * B), bf)] * 2
        + [pltpu.VMEM((128, 2 * L), jnp.float32)] * 2
        + [pltpu.VMEM((4, 128, 128), bf), pltpu.VMEM((4, 128, 128), jnp.float32)],
        out_shape=[jax.ShapeDtypeStruct((L, C), bf)] * 3
        + [jax.ShapeDtypeStruct((C, 2 * L), bf)] * 2
        + [jax.ShapeDtypeStruct((24, C), jnp.float32)],
        compiler_params=pltpu.CompilerParams(vmem_limit_bytes=56 << 20),
        cost_estimate=pl.CostEstimate(flops=120 * 10**9, bytes_accessed=80 * 10**6, transcendentals=0),
    )(p, qkv, qkv, qkv, do, ctx, linv, far, far)


def spec(block, index, once=False):
    if once:
        return pl.BlockSpec(block, index, pipeline_mode=pl.Buffered(1))
    return pl.BlockSpec(block, index)


def norm_rows(z):
    center = z - jnp.mean(z, axis=-1, keepdims=True)
    r = lax.rsqrt(jnp.mean(center * center, axis=-1, keepdims=True) + EPSILON)
    return center * r, r


def norm_back(g, n, r):
    return r * (g - jnp.mean(g, axis=-1, keepdims=True) - n * jnp.mean(g * n, axis=-1, keepdims=True))


def fold8(v):
    return jnp.sum(v.reshape(v.shape[0] // 8, 8, v.shape[1]), axis=0)


def project_kernel(xd_ref, rel4_ref, wa_ref, wb_ref, sh_ref, pl_ref, qkv_ref, far_ref, x_ref, rel_ref, hot_ref):
    t, j = pl.program_id(0), pl.program_id(1)
    gn, tn, lg, dt = xd_ref.shape
    spans = rel_ref.shape[0]
    rg = spans // gn

    @pl.when((t == 0) & (j == 0))
    def _():
        for g in range(gn):
            for s in range(tn):
                x_ref[g * lg : (g + 1) * lg, s * dt : (s + 1) * dt] = xd_ref[g, s]
                rel_ref[g * rg : (g + 1) * rg, s * dt : (s + 1) * dt] = rel4_ref[g, s]
        rows = hot_ref.shape[0]
        lanes = lax.broadcasted_iota(jnp.int32, (rows, spans), 1)
        hot_ref[...] = (pl_ref[...] == lanes).astype(jnp.float32).astype(jnp.bfloat16)

    w = jnp.where(j < 2, wa_ref[:, 0], wb_ref[:, 0]).reshape(x_ref.shape[1], dt)
    shift = sh_ref[0, pl.ds(j, 1), :]
    qkv_ref[0] = (dotnn(x_ref[...], w) + shift).astype(jnp.bfloat16)

    @pl.when(j < 2)
    def _():
        place = (dotnn(rel_ref[...], w) + shift).astype(jnp.bfloat16)
        far_ref[0] = dotnn(hot_ref[...], place).astype(jnp.bfloat16)


def project(xd, first, later, shifts, places, per):
    gn, tn, lg, dt = xd.shape
    L, D = gn * lg, tn * dt
    rg = later.shape[2] - per - 8
    spans = rg * gn
    bf = jnp.bfloat16
    return pl.pallas_call(
        project_kernel,
        grid=(tn, 3),
        in_specs=[
            spec((gn, tn, lg, dt), lambda t, j: (0, 0, 0, 0), True),
            spec((gn, tn, rg, dt), lambda t, j: (0, 0, per // rg, 0), True),
            spec((gn, 1, per, dt), lambda t, j: (0, t, jnp.minimum(j, 1), 0)),
            spec((gn, 1, per, dt), lambda t, j: (0, t, 0, 0)),
            spec((1, 3, dt), lambda t, j: (t, 0, 0)),
            spec((2 * L, 1), lambda t, j: (0, 0), True),
        ],
        out_specs=[
            spec((1, L, dt), lambda t, j: (j, 0, t)),
            spec((1, 2 * L, dt), lambda t, j: (jnp.minimum(j, 1), 0, t)),
            spec((L, D), lambda t, j: (0, 0)),
            spec((spans, D), lambda t, j: (0, 0)),
            spec((2 * L, spans), lambda t, j: (0, 0)),
        ],
        out_shape=[
            jax.ShapeDtypeStruct((3, L, D), bf),
            jax.ShapeDtypeStruct((2, 2 * L, D), bf),
            jax.ShapeDtypeStruct((L, D), bf),
            jax.ShapeDtypeStruct((spans, D), bf),
            jax.ShapeDtypeStruct((2 * L, spans), bf),
        ],
        compiler_params=pltpu.CompilerParams(vmem_limit_bytes=50 << 20),
        cost_estimate=pl.CostEstimate(flops=14 * 10**9, bytes_accessed=30 * 10**6, transcendentals=0),
    )(xd, later, first, later, shifts, places)


RB = 256


MB = 256


def middle_kernel(ctx_ref, x_ref, wm_ref, wi_ref, wo_ref, hb_ref, vec_ref, cot_ref,
                  y_ref, pay_ref, hid_ref, da_ref, sums_ref,
                  act_ref, slope_ref, hl_ref, hlt_ref, r1_ref, df_ref, acc_ref, sem):
    step = pl.program_id(0)
    L, D = x_ref.shape
    gn, tn, lg, dt = cot_ref.shape
    _, _, per, ff = wi_ref.shape[0], 0, wi_ref.shape[2], wi_ref.shape[3]
    f32, bf = jnp.float32, jnp.bfloat16

    slots = D // ff

    @pl.when(step == 0)
    def _():
        copies = []
        for n, src in enumerate((ctx_ref, x_ref)):
            for u in range(slots):
                at = n * slots + u
                c = pltpu.make_async_copy(src.at[:, pl.ds(u * ff, ff)], slope_ref.at[1 + at], sem.at[at])
                c.start()
                copies.append(c)
        for c in copies:
            c.wait()
        for r in range(0, L, MB):
            rows = slice(r, r + MB)
            z1 = jnp.concatenate([slope_ref[1 + slots + u, rows] for u in range(slots)], axis=1)
            z1 = vec_ref[0:1] + z1.astype(f32)
            for s in range(tn):
                at = s * dt % ff
                part = slope_ref[1 + s * dt // ff, rows, at : at + dt]
                z1 = z1 + dotnt(part, wm_ref[s].reshape(D, dt))
            n1, r1 = norm_rows(z1)
            h1 = n1 * vec_ref[1:2] + vec_ref[2:3]
            low = h1.astype(bf)
            acc_ref[rows] = h1 + vec_ref[3:4]
            hl_ref[rows] = low
            hlt_ref[:, rows] = low.T
            da_ref[rows] = n1.astype(bf)
            high = r1.astype(bf).astype(f32)
            first_lane = lax.broadcasted_iota(jnp.int32, (MB, 128), 1) == 0
            r1_ref[rows] = jnp.where(first_lane, high, r1 - high).astype(bf)

    @pl.when(step < tn)
    def _():
        for r in range(0, L, MB):
            rows = slice(r, r + MB)
            pre = dotnn(hl_ref[rows], wi_ref[0].reshape(D, ff)) + hb_ref[0]
            phi = 0.5 + 0.5 * lax.erf(pre * math.sqrt(0.5))
            act = (pre * phi).astype(bf)
            act_ref[step, rows] = act
            bell = jnp.exp(-0.5 * pre * pre) * (1.0 / math.sqrt(2.0 * math.pi))
            slope_ref[step, rows] = (phi + pre * bell).astype(bf)
            acc_ref[rows] += dotnt(act, wo_ref[0].reshape(D, ff))

    @pl.when(step == tn - 1)
    def _():
        s0 = jnp.zeros((8, D), f32)
        s1 = jnp.zeros((8, D), f32)
        s2 = jnp.zeros((8, D), f32)
        for g in range(gn):
            rows = slice(g * lg, (g + 1) * lg)
            n2, r2 = norm_rows(acc_ref[rows])
            y = (n2 * vec_ref[4:5] + vec_ref[5:6]).astype(bf)
            for s in range(tn):
                y_ref[g, s] = y[:, s * dt : (s + 1) * dt]
            dy = jnp.concatenate([cot_ref[g, s] for s in range(tn)], axis=1).astype(f32)
            dz2 = norm_back(dy * vec_ref[4:5], n2, r2)
            df_ref[rows] = dz2.astype(bf)
            acc_ref[rows] = dz2
            s0, s1, s2 = s0 + fold8(dz2), s1 + fold8(dy * n2), s2 + fold8(dy)
        sums_ref[24:32], sums_ref[32:40], sums_ref[40:48] = s0, s1, s2
        for r in range(0, L, RB):
            hl_ref[:, r : r + RB] = df_ref[r : r + RB].T

    @pl.when(step >= tn)
    def _():
        t = 2 * tn - 1 - step
        hid = jnp.zeros((8, ff), f32)
        for r in range(0, L, MB):
            rows = slice(r, r + MB)
            dpre = dotnn(df_ref[rows], wo_ref[0].reshape(D, ff)) * slope_ref[t, rows].astype(f32)
            hid = hid + fold8(dpre)
            low = dpre.astype(bf)
            slope_ref[t, rows] = low
            acc_ref[rows] += dotnt(low, wi_ref[0].reshape(D, ff))
        hid_ref[0] = hid
        for r in range(0, D, RB):
            og = dotnn(hl_ref[r : r + RB], act_ref[t]).astype(bf)
            ig = dotnn(hlt_ref[r : r + RB], slope_ref[t]).astype(bf)
            for c in range(0, RB, per):
                pay_ref[(r + c) // per, 0, :, 0:ff] = ig[c : c + per]
                pay_ref[(r + c) // per, 0, :, ff : 2 * ff] = og[c : c + per]

    @pl.when(step == 2 * tn - 1)
    def _():
        s0 = jnp.zeros((8, D), f32)
        s1 = jnp.zeros((8, D), f32)
        s2 = jnp.zeros((8, D), f32)
        for r in range(0, L, 128):
            rows = slice(r, r + 128)
            dh1 = acc_ref[rows]
            n1 = da_ref[rows].astype(f32)
            r1 = r1_ref[rows, 0:1].astype(f32) + r1_ref[rows, 1:2].astype(f32)
            dz1 = norm_back(dh1 * vec_ref[1:2], n1, r1)
            da_ref[rows] = dz1.astype(bf)
            s0, s1, s2 = s0 + fold8(dz1), s1 + fold8(dh1 * n1), s2 + fold8(dh1)
        sums_ref[0:8], sums_ref[8:16], sums_ref[16:24] = s0, s1, s2


def middle(ctx, x, second, hidden_bias, vectors, cot):
    gn, tn, lg, dt = cot.shape
    per = second.shape[2]
    L, D = x.shape
    assert L == D
    ff = hidden_bias.shape[2]
    bf, f32 = jnp.bfloat16, jnp.float32
    full = lambda shape: spec(shape, lambda i: (0,) * len(shape), True)
    place = lambda i: jnp.minimum(i, 2 * tn - 1 - i)
    back = lambda i: jnp.minimum(2 * tn - 1 - i, tn - 1)
    return pl.pallas_call(
        middle_kernel,
        grid=(2 * tn,),
        in_specs=[
            pl.BlockSpec(memory_space=pl.ANY),
            pl.BlockSpec(memory_space=pl.ANY),
            spec((tn, gn, per, dt), lambda i: (0, 0, 0, 2 * ff // dt), True),
            spec((1, gn, per, ff), lambda i: (place(i), 0, 0, 0)),
            spec((1, gn, per, ff), lambda i: (place(i), 0, 0, 1)),
            spec((1, 1, ff), lambda i: (place(i), 0, 0)),
            full((6, D)),
            full((gn, tn, lg, dt)),
        ],
        out_specs=[
            full((gn, tn, lg, dt)),
            spec((gn, 1, per, 2 * ff), lambda i: (0, back(i), 0, 0)),
            spec((1, 8, ff), lambda i: (back(i), 0, 0)),
            full((L, D)),
            full((48, D)),
        ],
        out_shape=[
            jax.ShapeDtypeStruct((gn, tn, lg, dt), bf),
            jax.ShapeDtypeStruct((gn, tn, per, 2 * ff), bf),
            jax.ShapeDtypeStruct((tn, 8, ff), f32),
            jax.ShapeDtypeStruct((L, D), bf),
            jax.ShapeDtypeStruct((48, D), f32),
        ],
        scratch_shapes=[
            pltpu.VMEM((tn, L, ff), bf), pltpu.VMEM((tn, L, ff), bf),
            pltpu.VMEM((L, D), bf), pltpu.VMEM((D, L), bf), pltpu.VMEM((L, 128), bf),
            pltpu.VMEM((L, D), bf), pltpu.VMEM((L, D), f32),
            pltpu.SemaphoreType.DMA((2 * (D // ff),)),
        ],
        compiler_params=pltpu.CompilerParams(vmem_limit_bytes=61 << 20),
        cost_estimate=pl.CostEstimate(flops=75 * 10**9, bytes_accessed=100 * 10**6, transcendentals=0),
    )(ctx, x, second, second, second, hidden_bias, vectors, cot)


def merge_back_kernel(da_ref, ctx_ref, wm_ref, pay_ref, dctx_ref, dat_ref):
    t = pl.program_id(0)
    L, D = da_ref.shape
    gn, _, per, dt = pay_ref.shape

    @pl.when(t == 0)
    def _():
        for r in range(0, L, RB):
            dat_ref[:, r : r + RB] = da_ref[r : r + RB].T

    dctx_ref[...] = dotnn(da_ref[...], wm_ref[0].reshape(D, dt)).astype(jnp.bfloat16)
    pay_ref[:, 0] = dotnn(dat_ref[...], ctx_ref[...]).astype(jnp.bfloat16).reshape(gn, per, dt)


def merge_back(dattn, ctx, second):
    tn, gn, per, wide = second.shape
    L, D = dattn.shape
    dt = D // tn
    last = wide // dt - 1
    bf = jnp.bfloat16
    return pl.pallas_call(
        merge_back_kernel,
        grid=(tn,),
        in_specs=[
            spec((L, D), lambda t: (0, 0), True),
            spec((L, dt), lambda t: (0, t)),
            spec((1, gn, per, dt), lambda t: (t, 0, 0, last)),
        ],
        out_specs=[
            spec((gn, 1, per, dt), lambda t: (0, t, 0, 0)),
            spec((L, dt), lambda t: (0, t)),
        ],
        out_shape=[
            jax.ShapeDtypeStruct((gn, tn, per, dt), bf),
            jax.ShapeDtypeStruct((L, D), bf),
        ],
        scratch_shapes=[pltpu.VMEM((D, L), bf)],
        compiler_params=pltpu.CompilerParams(vmem_limit_bytes=50 << 20),
        cost_estimate=pl.CostEstimate(flops=4 * 10**9, bytes_accessed=10 * 10**6, transcendentals=0),
    )(dattn, ctx, second)


def input_back_kernel(da_ref, dq_ref, dk_ref, dv_ref, wa_ref, wb_ref, dx_ref, acc_ref):
    t = pl.program_id(0)
    L, D = da_ref.shape
    gn, tn, lg, dt = dx_ref.shape
    per = D // gn

    @pl.when(t == 0)
    def _():
        acc_ref[...] = da_ref[...].astype(jnp.float32)

    w = [wa_ref[:, 0, j * per : (j + 1) * per, :].reshape(D, dt) for j in range(2)]
    w.append(wb_ref[:, 0].reshape(D, dt))
    tops = [dq_ref, dk_ref, dv_ref]
    for r in range(0, L, RB):
        acc_ref[r : r + RB] += sum(dotnt(tops[j][r : r + RB], w[j]) for j in range(3))

    @pl.when(t == pl.num_programs(0) - 1)
    def _():
        for g in range(gn):
            for s in range(tn):
                cols = slice(s * dt, (s + 1) * dt)
                dx_ref[g, s] = acc_ref[g * lg : (g + 1) * lg, cols].astype(jnp.bfloat16)


def input_back(dattn, dq, dk, dv, first, later):
    gn, tn, wide, dt = first.shape
    L, D = dattn.shape
    col = lambda: spec((L, dt), lambda t: (0, t))
    return pl.pallas_call(
        input_back_kernel,
        grid=(tn,),
        in_specs=[
            spec((L, D), lambda t: (0, 0), True),
            col(), col(), col(),
            spec((gn, 1, wide, dt), lambda t: (0, t, 0, 0)),
            spec((gn, 1, D // gn, dt), lambda t: (0, t, 0, 0)),
        ],
        out_specs=spec((gn, tn, L // gn, dt), lambda t: (0, 0, 0, 0), True),
        out_shape=jax.ShapeDtypeStruct((gn, tn, L // gn, dt), jnp.bfloat16),
        scratch_shapes=[pltpu.VMEM((L, D), jnp.float32)],
        compiler_params=pltpu.CompilerParams(vmem_limit_bytes=50 << 20),
        cost_estimate=pl.CostEstimate(flops=7 * 10**9, bytes_accessed=20 * 10**6, transcendentals=0),
    )(dattn, dq, dk, dv, first, later)


def tail_kernel(x_ref, rel_ref, hot_ref, dq_ref, dk_ref, dv_ref, dqf_ref, dkf_ref, sm_ref, w_ref, small_ref, mg_ref,
                pay_ref, xt_ref, ra_ref, *, first_shift):
    t = pl.program_id(0)
    L, D = x_ref.shape
    spans = rel_ref.shape[0]
    gn, tn, _, dt = pay_ref.shape
    per = D // gn
    rg = spans // gn
    sr = small_ref.shape[2]
    f32, bf = jnp.float32, jnp.bfloat16

    @pl.when(t == 0)
    def _():
        for r in range(0, L, RB):
            xt_ref[:, r : r + RB] = x_ref[r : r + RB].T
        for r in range(0, spans, RB):
            xt_ref[:, L + r : L + r + RB] = rel_ref[r : r + RB].T
        ra_ref[...] = jnp.zeros_like(ra_ref)

    w = [w_ref[:, 0, j * per : (j + 1) * per, :].reshape(D, dt) for j in range(2)]
    qp = dotnn(dqf_ref[...], hot_ref[...]).T
    kp = dotnn(dkf_ref[...], hot_ref[...]).T
    pos = [qp.astype(bf), kp.astype(bf)]
    tops = [dq_ref, dk_ref, dv_ref]
    rows = 4 * per + rg
    pay_ref[:, t, 3 * per : 4 * per, :] = mg_ref[:, 0]
    pay_ref[:, t, rows : rows + sr, :] = small_ref[0].astype(bf)
    for j in range(3):
        total = jnp.sum(sm_ref[8 * j : 8 * j + 8], axis=0, keepdims=True)
        if j < 2:
            total = total + jnp.sum((qp, kp)[j], axis=0, keepdims=True)
            both = jnp.concatenate([tops[j][...], pos[j]], axis=0)
            grad = dotnn(xt_ref[...], both)
            ra_ref[...] += dotnt(pos[j], w[j])
        else:
            grad = dotnn(xt_ref[:, 0:L], tops[j][...])
        pay_ref[:, t, j * per : (j + 1) * per, :] = grad.astype(bf).reshape(gn, per, dt)
        at = first_shift + j
        pay_ref[at // sr, t, rows + at % sr : rows + at % sr + 1, :] = total.astype(bf)
    @pl.when(t == pl.num_programs(0) - 1)
    def _():
        for g in range(gn):
            for s in range(tn):
                cols = slice(s * dt, (s + 1) * dt)
                pay_ref[g, s, 4 * per : rows, :] = ra_ref[g * rg : (g + 1) * rg, cols].astype(bf)


def tail(x, rel, hot, dq, dk, dv, dqf, dkf, sums, first, small, merged, first_shift):
    gn, tn, wide, dt = first.shape
    L, D = x.shape
    spans = rel.shape[0]
    rows = 4 * D // gn + spans // gn + small.shape[2]
    bf, f32 = jnp.bfloat16, jnp.float32
    full = lambda shape: spec(shape, lambda t: (0,) * len(shape), True)
    col = lambda: spec((L, dt), lambda t: (0, t))
    return pl.pallas_call(
        functools.partial(tail_kernel, first_shift=first_shift),
        grid=(tn,),
        in_specs=[
            full((L, D)), full((spans, D)), full((2 * L, spans)),
            col(), col(), col(),
            spec((dt, 2 * L), lambda t: (t, 0)), spec((dt, 2 * L), lambda t: (t, 0)),
            spec((24, dt), lambda t: (0, t)),
            spec((gn, 1, wide, dt), lambda t: (0, t, 0, 0)),
            spec((1,) + small.shape[1:], lambda t: (t, 0, 0, 0)),
            spec((gn, 1, D // gn, dt), lambda t: (0, t, 0, 0)),
        ],
        out_specs=full((gn, tn, rows, dt)),
        out_shape=jax.ShapeDtypeStruct((gn, tn, rows, dt), bf),
        scratch_shapes=[pltpu.VMEM((D, L + spans), bf), pltpu.VMEM((spans, D), f32)],
        compiler_params=pltpu.CompilerParams(vmem_limit_bytes=56 << 20),
        cost_estimate=pl.CostEstimate(flops=13 * 10**9, bytes_accessed=40 * 10**6, transcendentals=0),
    )(x, rel, hot, dq, dk, dv, dqf, dkf, sums, first, small, merged)


MESH = pl.DeviceIdType.MESH


def bit_of(place, i):
    return (place // (1 << i)) % 2


def flipped(place, flips):
    for i in flips:
        place = place + (1 << i) * (1 - 2 * bit_of(place, i))
    return place


def subsets(bits):
    out = [()]
    for i in bits:
        out += [s + (i,) for s in out]
    return out


def greet(tn, gn):
    t, g = lax.axis_index("tensor"), lax.axis_index("dp")
    barrier = pltpu.get_barrier_semaphore()
    bits = list(range(gn.bit_length() - 1))
    for d in range(1, tn):
        pl.semaphore_signal(barrier, inc=1, device_id={"tensor": lax.rem(t + d, tn)}, device_id_type=MESH)
    for i in bits:
        pl.semaphore_signal(barrier, inc=1, device_id={"dp": flipped(g, (i,))}, device_id_type=MESH)
    pl.semaphore_wait(barrier, tn - 1 + len(bits))


class Wire:
    def __init__(self, send, recv):
        self.send, self.recv, self.at = send, recv, 0

    def push(self, src, dst, **device):
        c = pltpu.make_async_remote_copy(
            src, dst, self.send.at[self.at], self.recv.at[self.at], device_id=device, device_id_type=MESH
        )
        self.at += 1
        c.start()
        return c


def run_waves(chunks):
    waves = max(len(stages) + c for c, stages in enumerate(chunks)) + 1
    flight = {}
    for w in range(waves):
        for c, stages in enumerate(chunks):
            s = w - c
            if 0 < s <= len(stages):
                stages[s - 1][1](flight.pop((c, s - 1)))
            if 0 <= s < len(stages):
                flight[c, s] = stages[s][0]()


def wait_all(copies):
    for c in copies:
        c.wait()


def spread_stages(src, out, local, wire, tn, gn):
    t, g = lax.axis_index("tensor"), lax.axis_index("dp")
    bits = list(range(gn.bit_length() - 1))
    half = tn // 2
    plans = [(0, bits[1:] + bits[:1]), (half, bits[:0:-1] + bits[:1])]

    def first():
        own = pltpu.make_async_copy(src(), out(g, pl.ds(t, 1)), local)
        own.start()
        copies = [
            wire.push(src(), out(g, pl.ds(t, 1)), tensor=lax.rem(t + d, tn)) for d in range(1, tn)
        ]
        return [own] + copies

    def later(step):
        def start():
            copies = []
            for lo, plan in plans:
                for s in subsets(plan[:step]):
                    part = out(flipped(g, s), pl.ds(lo, half))
                    copies.append(wire.push(part, part, dp=flipped(g, (plan[step],))))
            return copies

        return start

    return [(first, wait_all)] + [(later(step), wait_all) for step in range(len(bits))]


def spread_count(tn, gn):
    return tn - 1 + 2 * (gn - 1)


def gather_kernel(src_ref, out_ref, local, send, recv, *, tn, gn, cuts):
    greet(tn, gn)
    wire = Wire(send, recv)
    chunks = []
    for n, (lo, hi) in enumerate(cuts):
        rows = pl.ds(lo, hi - lo)
        chunks.append(
            spread_stages(
                lambda rows=rows: src_ref.at[:, rows],
                lambda g, s, rows=rows: out_ref.at[g, s, rows],
                local.at[n], wire, tn, gn,
            )
        )
    run_waves(chunks)


def gather_all(w, tn, gn, number):
    rows = w.shape[0]
    mid = rows // 32 * 16
    cuts = [(0, mid), (mid, rows)]
    n = spread_count(tn, gn) * len(cuts)
    dma = lambda k: pltpu.SemaphoreType.DMA((k,))
    return pl.pallas_call(
        functools.partial(gather_kernel, tn=tn, gn=gn, cuts=cuts),
        in_specs=[pl.BlockSpec(memory_space=pl.ANY)],
        out_specs=pl.BlockSpec(memory_space=pl.ANY),
        out_shape=jax.ShapeDtypeStruct((gn, tn) + w.shape, w.dtype),
        scratch_shapes=[dma(len(cuts)), dma(n), dma(n)],
        compiler_params=pltpu.CompilerParams(collective_id=number, has_side_effects=True),
        cost_estimate=pl.CostEstimate(flops=0, bytes_accessed=w.size * tn * gn * 16, transcendentals=0),
    )(w[None])


def reduce_kernel(pay_ref, q_ref, k_ref, v_ref, m_ref, rel_ref, small_ref, all_ref, acc_ref, rx_ref, ry_ref, rz_ref, rest_ref,
                  local, send, recv, *, tn, gn, keep):
    t, g = lax.axis_index("tensor"), lax.axis_index("dp")
    bits = list(range(gn.bit_length() - 1))
    f32, bf = jnp.float32, jnp.bfloat16
    rows = acc_ref.shape[2]
    per = keep // 4
    greet(tn, gn)
    wire = Wire(send, recv)
    outer = bits[1:]
    masks = subsets(outer)
    index = {s: n for n, s in enumerate(masks)}
    half = tn // 2
    plans = [(0, outer), (half, outer[::-1])]
    grads = (q_ref, k_ref, v_ref, m_ref)

    def reduce_stages(n, lo, hi):
        span = pl.ds(lo, hi - lo)

        def add(dst, first, size, src_ref, slot):
            for i in range(size):
                acc_ref[dst, first + i, lo:hi] = (
                    acc_ref[dst, first + i, lo:hi].astype(f32) + src_ref[slot, i, lo:hi].astype(f32)
                ).astype(bf)

        def first():
            copies = []
            for i, s in enumerate(masks):
                copies.append(wire.push(pay_ref.at[flipped(g, (0,) + s), :, span], rx_ref.at[i, :, span], dp=flipped(g, (0,))))
            for i, s in enumerate(masks):
                c = pltpu.make_async_copy(pay_ref.at[flipped(g, s), :, span], acc_ref.at[i, :, span], local.at[n, i])
                c.start()
                copies.append(c)
            return copies

        def first_done(copies):
            for i in range(len(masks)):
                copies[len(masks) + i].wait()
                copies[i].wait()
                add(i, 0, tn, rx_ref, i)

        def outer_stage(step, base):
            def start():
                flight = []
                slot = base
                for place, plan in plans:
                    bit = plan[step]
                    for s in masks:
                        if any(i in plan[: step + 1] for i in s):
                            continue
                        src = tuple(i for i in outer if i in s or i == bit)
                        c = wire.push(
                            acc_ref.at[index[src], pl.ds(place, half), span], ry_ref.at[slot, :, span],
                            dp=flipped(g, (bit,)),
                        )
                        flight.append((c, index[s], place, slot))
                        slot += 1
                return flight

            def done(flight):
                for c, dst, place, slot in flight:
                    c.wait()
                    add(dst, place, half, ry_ref, slot)

            return start, done

        def last():
            return [
                wire.push(acc_ref.at[0, lax.rem(t + d, tn), span], rz_ref.at[d - 1, span], tensor=lax.rem(t + d, tn))
                for d in range(1, tn)
            ]

        def last_done(copies):
            total = acc_ref[0, t, lo:hi].astype(f32)
            for d, c in enumerate(copies):
                c.wait()
                total = total + rz_ref[d, lo:hi].astype(f32)
            if lo >= keep:
                rest_ref[0] = total.astype(bf)
            else:
                for j in range(4):
                    a, b = max(lo, j * per), min(hi, (j + 1) * per)
                    if a < b:
                        grads[j][a - j * per : b - j * per] = total[a - lo : b - lo]

        stages = [(first, first_done)]
        base = 0
        for step in range(len(outer)):
            stages.append(outer_stage(step, base))
            base += 2 * (gn // 4 >> step)
        return stages + [(last, last_done)]

    cuts = [0, keep // 48 * 16, keep // 24 * 16, keep]
    chunks = [
        reduce_stages(0, keep, rows)
        + spread_stages(
            lambda: rest_ref, lambda i, s: all_ref.at[i, s], local.at[4, 0], wire, tn, gn
        ),
    ] + [reduce_stages(n + 1, cuts[n], cuts[n + 1]) for n in range(3)]
    run_waves(chunks)
    dt = q_ref.shape[1]
    rg = rel_ref.shape[0] // gn
    for s in range(tn):
        cols = slice(s * dt, (s + 1) * dt)
        for i in range(gn):
            rel_ref[i * rg : (i + 1) * rg, cols] = all_ref[i, s, :rg].astype(f32)
        small_ref[:, cols] = all_ref[0, s, rg:].astype(f32)


def reduce_all(pay, keep, spans, number):
    gn, tn, rows, dt = pay.shape
    bf, f32 = jnp.bfloat16, jnp.float32
    m = gn // 2
    pieces = 2 * (m - 1)
    count = 4 * (m + pieces + tn - 1) + spread_count(tn, gn)
    dma = lambda *k: pltpu.SemaphoreType.DMA(k)
    return pl.pallas_call(
        functools.partial(reduce_kernel, tn=tn, gn=gn, keep=keep),
        in_specs=[pl.BlockSpec(memory_space=pl.ANY)],
        out_specs=[pl.BlockSpec(memory_space=pltpu.VMEM)] * 6,
        out_shape=[jax.ShapeDtypeStruct((keep // 4, dt), f32)] * 4
        + [
            jax.ShapeDtypeStruct((spans, tn * dt), f32),
            jax.ShapeDtypeStruct((rows - keep - spans // gn, tn * dt), f32),
        ],
        scratch_shapes=[
            pltpu.VMEM((gn, tn, rows - keep, dt), bf),
            pltpu.VMEM((m, tn, rows, dt), bf),
            pltpu.VMEM((m, tn, rows, dt), bf),
            pltpu.VMEM((pieces, tn // 2, rows, dt), bf),
            pltpu.VMEM((tn - 1, rows, dt), bf),
            pltpu.VMEM((1, rows - keep, dt), bf),
            dma(5, m), dma(count), dma(count),
        ],
        compiler_params=pltpu.CompilerParams(collective_id=number, has_side_effects=True, vmem_limit_bytes=58 << 20),
        cost_estimate=pl.CostEstimate(flops=0, bytes_accessed=200 * 10**6, transcendentals=0),
    )(pay)


def shards(
    inputs,
    cotangent,
    lengths,
    dealing,
    buckets,
    rel_embed,
    query_weight,
    key_weight,
    value_weight,
    proj_shifts,
    merge_weight,
    inner_weight,
    hidden_shift,
    outer_weight,
    layer_vectors,
):
    tn = lax.axis_size("tensor")
    gn = lax.axis_size("dp")
    me = lax.axis_index("dp") * tn + lax.axis_index("tensor")
    count, lg, dt = inputs.shape
    L, D = lg * gn, dt * tn
    per = query_weight.shape[0]
    rg = rel_embed.shape[0]
    spans = rg * gn
    assert count == tn * gn
    bf = jnp.bfloat16
    f32 = jnp.float32
    scale = 1.0 / math.sqrt(3.0 * HEAD)
    seq_axes = ("dp", "tensor")
    w_axes = ("tensor", "dp")

    def swap(a):
        return lax.all_to_all(a, seq_axes, split_axis=0, concat_axis=0, tiled=True)

    def gather(w):
        return lax.all_gather(w, w_axes, axis=0, tiled=False).reshape((tn, gn) + w.shape)

    rel_cols = lax.dynamic_slice_in_dim(rel_embed, lax.axis_index("tensor") * dt, dt, 1)
    early = jnp.concatenate([query_weight, key_weight], axis=0)
    late = jnp.concatenate(
        [value_weight, rel_cols, proj_shifts, hidden_shift.reshape(-1, dt), jnp.zeros((1, dt), bf)], axis=0
    )
    first = gather_all(early, tn, gn, 0)
    xd = swap(inputs).reshape(gn, tn, lg, dt)
    wide = jnp.concatenate([inner_weight, outer_weight, merge_weight], axis=1)
    first, xd, late, wide, cotangent = lax.optimization_barrier((first, xd, late, wide, cotangent))
    second = gather(wide)
    later = gather_all(late, tn, gn, 2)
    cot = swap(cotangent).reshape(gn, tn, lg, dt)
    biases = later[0, :, per + rg :].astype(f32)
    shifts = biases[:, :3]
    hidden_bias = biases[:, 3:7].reshape(tn, 1, -1)
    vectors = layer_vectors.astype(f32)
    length = jnp.sum(jnp.where(dealing == me, lengths, 0)).reshape(1)
    places = jnp.concatenate([buckets[::-1], jnp.full((1,), -1, jnp.int32)])[:, None]

    qkv, far, x, rel, hot = project(xd, first, later, shifts, places, per)
    ctx, probs, inv = attn_fwd(length, qkv, far, scale=scale)
    y, payload, hidden, dattn, sums12 = middle(ctx, x, second, hidden_bias, vectors, cot)
    out = swap(y.reshape(count, lg, dt))
    wide_grads = lax.psum_scatter(payload, "dp", scatter_dimension=0, tiled=False)
    merged, dctx = merge_back(dattn, ctx, second)
    dq, dk, dv, dkf, dqf, sums = attn_bwd(probs, qkv, dctx, ctx, inv, far, scale=scale)
    dq, out, wide_grads = lax.optimization_barrier((dq, out, wide_grads))
    wide_grads = lax.psum_scatter(wide_grads, "tensor", scatter_dimension=0, tiled=False)
    ff = hidden.shape[2]
    small = jnp.concatenate(
        [
            jnp.sum(sums12.reshape(6, 8, D), axis=1),
            jnp.sum(hidden, axis=1).reshape(-1, D),
        ],
        axis=0,
    )
    first_shift = small.shape[0]
    sr = 16
    small = jnp.pad(small, ((0, sr - first_shift), (0, 0)))
    small = small.reshape(sr, tn, dt).transpose(1, 0, 2)[:, None]
    small = jnp.pad(small, ((0, 0), (0, gn - 1), (0, 0), (0, 0)))
    dx = input_back(dattn, dq, dk, dv, first, later)
    dx, dq = lax.optimization_barrier((dx, dq))
    pay = tail(x, rel, hot, dq, dk, dv, dqf, dkf, sums, first, small, merged, first_shift)
    grad_in = swap(dx.reshape(count, lg, dt))
    wide_grads = wide_grads.astype(f32)
    query_grad, key_grad, value_grad, merge_grad, rel_grad, rest = reduce_all(pay, 4 * per, spans, 1)
    return (
        out,
        grad_in,
        rel_grad,
        query_grad,
        key_grad,
        value_grad,
        rest[first_shift : first_shift + 3],
        merge_grad,
        wide_grads[:, :ff],
        rest[6:first_shift].reshape(-1),
        wide_grads[:, ff:],
        rest[:6],
    )


def solution(mesh):
    split = P("dp", "tensor")
    whole = P(None, "dp", "tensor")
    in_specs = (
        whole, whole, P(), P(), P(), P("dp", None), split, split, split, P(None, "tensor"),
        split, split, P("tensor"), split, P(),
    )
    out_specs = (whole, whole, P(), split, split, split, P(), split, split, P(), split, P())
    return jax.shard_map(shards, mesh=mesh, in_specs=in_specs, out_specs=out_specs, check_vma=False)
```
